128 devices in a mesh: slab: 8 (over y, core), grp: 16 (over z, x).
Axes of the slice: x: 4, y: 4, z: 4, core: 2. Of those that a mesh axis runs over, the one named last changes fastest.
Arguments:
- node_feats: bfloat16 [1048576, 128], P(('slab', 'grp')), may hold values from -6 to 6
- cotangent: bfloat16 [1048576, 128], P(('slab', 'grp')), may hold values from -6 to 6
- fine_adjacency: bfloat16 [16384, 64, 768], P(('slab', 'grp')), may hold values from -0.21875 to 0.21875
- fine_columns: int32 [16384, 12], P(('slab', 'grp')), may hold values from 0 to 143, as said below
- pool_one: bfloat16 [2048, 64, 512], P(('slab', 'grp')), may hold values from -0.25 to 0.25
- pool_one_columns: int32 [2048, 8], P(('slab', 'grp')), may hold values from 0 to 127
- count_one: int32 [128], P(('slab', 'grp')), may hold values from 256 to 1024, as said below
- owner_one: int32 [131072], P(('slab', 'grp')), may hold values from 0 to 8191, as said below
- adjacency_one: bfloat16 [1024, 64, 512], P(('slab', 'grp')), may hold values from -0.25 to 0.25
- columns_one: int32 [1024, 8], P(('slab', 'grp')), may hold values from 0 to 127
- pool_two: bfloat16 [512, 64, 512], P(('slab', 'grp')), may hold values from -0.25 to 0.25
- pool_two_columns: int32 [512, 8], P(('slab', 'grp')), may hold values from 0 to 7
- count_two: int32 [128], P(('slab', 'grp')), may hold values from 64 to 256, as said below
- owner_two: int32 [32768], P(('slab', 'grp')), may hold values from 0 to 2047, as said below
- adjacency_two: bfloat16 [256, 64, 512], P(('slab', 'grp')), may hold values from -0.25 to 0.25
- columns_two: int32 [256, 8], P(('slab', 'grp')), may hold values from 0 to 31
- weight_in: bfloat16 [3, 256, 128], replicated, may hold values from -0.375 to 0.375
- weight_out: bfloat16 [3, 128, 128], replicated, may hold values from -0.5 to 0.5
- biases: float32 [3, 128], replicated, may hold values from -3 to 3
Outputs:
- node_out: bfloat16 [1048576, 128], P(('slab', 'grp'))
- grad_feats: bfloat16 [1048576, 128], P(('slab', 'grp'))
- grad_weight_in: float32 [3, 256, 128], replicated
- grad_weight_out: float32 [3, 128, 128], replicated
- grad_biases: float32 [3, 128], replicated
The draws below stay inside these ranges and needn't reach their ends.
Inputs may be any that keep to these rules, and one draw needn't show every extreme that they name: `fine_columns`: row block r of a device reads blocks r to r + 16 of its extended rows. `count_one`: the 16 counts of one slab sum to 8192, and one of them equals 1024. `owner_one`: the live slots of a device are its first count_one slots. In one slab the live slots' values take each value below 8192 exactly once; value v names row v % 512 of device v // 512 of the slab. At most 64 live slots of one device name rows of one device, and in every slab some device has exactly that many for every device. Values of other slots are unused. `count_two`: the 16 counts of one slab sum to 2048, and one of them equals 256. `owner_two`: the live slots of a device are its first count_two slots. In one slab the live slots' values take each value below 2048 exactly once; value v names row v % 128 of device v // 128 of the slab. At most 16 live slots of one device name rows of one device, and in every slab some device has exactly that many for every device. Values of other slots are unused.
All inputs are finite; a program needn't handle non-finite values.
Results may differ from the reference program's by a relative error of at most 0.012.
Values may be sent and summed in bfloat16 or wider, within the bound.
A program may use at most 320 MiB of HBM per device.

```python
import math
import jax
import jax.numpy as jnp
from jax import lax

H = 128
BLK = 64
F_DEV = 8192
HALO = 512
K0 = 12
K1 = 8
K2 = 8
KR = 8
C1 = 1024
B1 = 512
C2 = 256
B2 = 128
NODES = 1048576
N_SLAB = 8
N_GRP = 16


def level_routes(key, slot_total, balance):

    def one_slab(slab_key):
        key_list = jax.random.split(slab_key, 5)
        shuffled = jax.random.permutation(key_list[0], N_GRP)
        position = jnp.arange(N_GRP, dtype=jnp.int32)
        amounts = jax.random.randint(key_list[1], (N_GRP,), 0, balance // 2 + 1)
        parity = jnp.mod(position - 3, 2)
        first_of = position - parity
        paired = (position >= 3) & (first_of + 1 <= N_GRP - 1)
        signs = 1 - 2 * parity
        shared = amounts[jnp.clip((first_of - 3) // 2, 0, N_GRP - 1)]
        deltas = jnp.where(position == 0, balance, jnp.where(position <= 2, -(balance // 2), jnp.where(paired, signs * shared, 0)))
        counts = jnp.zeros((N_GRP,), jnp.int32).at[shuffled].set((balance + deltas).astype(jnp.int32))
        starts = jnp.cumsum(counts) - counts
        within = jnp.arange(slot_total, dtype=jnp.int32)
        live_mask = within[None, :] < counts[:, None]
        global_rank = starts[:, None] + within[None, :]
        rotation = jax.random.randint(key_list[2], (), 0, N_GRP)
        owners = jnp.mod(global_rank + rotation, N_GRP)
        depth = jnp.clip(global_rank // N_GRP, 0, balance - 1)
        shuffles = jax.vmap(lambda sub_key: jax.random.permutation(sub_key, balance))(jax.random.split(key_list[3], N_GRP))
        owner_rows = owners * balance + shuffles[owners, depth]
        spare_rows = jax.random.randint(key_list[4], (N_GRP, slot_total), 0, N_GRP * balance)
        return (counts, jnp.where(live_mask, owner_rows, spare_rows).astype(jnp.int32).reshape(-1))
    counts, owners = jax.vmap(one_slab)(jax.random.split(key, N_SLAB))
    return (counts.reshape(-1).astype(jnp.int32), owners.reshape(-1).astype(jnp.int32))


def draw_fine_columns(key, part):
    block_total = N_SLAB * N_GRP * (F_DEV // BLK)
    reach = HALO // BLK
    local_rows = jnp.arange(block_total, dtype=jnp.int32) % (F_DEV // BLK)
    offsets = jax.random.randint(jax.random.fold_in(key, 5), (block_total, K0), -reach, reach + 1)
    return (local_rows[:, None] + reach + offsets).astype(jnp.int32)


def draw_count_one(key, part):
    return level_routes(jax.random.fold_in(key, 11), C1, B1)[0]


def draw_owner_one(key, part):
    return level_routes(jax.random.fold_in(key, 11), C1, B1)[1]


def draw_count_two(key, part):
    return level_routes(jax.random.fold_in(key, 22), C2, B2)[0]


def draw_owner_two(key, part):
    return level_routes(jax.random.fold_in(key, 22), C2, B2)[1]


def place_ends(values, rng, low, largest):
    extent = values.shape
    spot = [jax.random.randint(jax.random.fold_in(rng, axis), (), 0, extent[axis]) for axis in range(len(extent))]
    values = values.at[tuple(spot)].set(low)
    longest = extent.index(max(extent))
    spot[longest] = (spot[longest] + 1) % extent[longest]
    return values.at[tuple(spot)].set(largest)


def block_levels(key, extent, cuts, smallest, high):
    factor_of = 1.0
    for axis_at, parts in cuts:
        steps = jax.random.uniform(jax.random.fold_in(jax.random.fold_in(key, 6), axis_at), (parts,), jnp.float32, smallest / len(cuts), high / len(cuts))
        factor_of = factor_of * jnp.repeat(jnp.exp(steps), extent[axis_at] // parts).reshape((-1,) + (1,) * (len(extent) - 1 - axis_at))
    return factor_of


def noise(own_key, shape, scale, most, cuts=(), kind=jnp.bfloat16):
    drawn = scale * jax.random.normal(own_key, shape, jnp.float32)
    if cuts:
        drawn = drawn * block_levels(own_key, shape, cuts, -0.22, 0.18)
    return jnp.clip(drawn, -most, most).astype(kind)


def setup_inputs(seed: int = 0) -> dict:
    seeds = jax.random.split(jax.random.key(seed), 20)
    return {
        "node_feats": noise(seeds[0], (NODES, H), 1.0, 6.0, ((0, 128),)),
        "cotangent": noise(seeds[1], (NODES, H), 1.0, 6.0, ((0, 128),)),
        "fine_adjacency": noise(seeds[2], (N_SLAB * N_GRP * (F_DEV // BLK), BLK, K0 * BLK), (K0 * BLK) ** -0.5, 0.21875, ((0, 128),)),
        "fine_columns": draw_fine_columns(jax.random.fold_in(seeds[19], 71), 0),
        "pool_one": noise(seeds[4], (N_SLAB * N_GRP * (C1 // BLK), BLK, KR * BLK), (KR * BLK) ** -0.5, 0.25, ((0, 128),)),
        "pool_one_columns": place_ends(jax.random.randint(seeds[5], (N_SLAB * N_GRP * (C1 // BLK), KR), 0, F_DEV // BLK), jax.random.fold_in(seeds[5], 1), 0, (F_DEV // BLK) - 1).astype(jnp.int32),
        "count_one": draw_count_one(jax.random.fold_in(seeds[19], 71), 0),
        "owner_one": draw_owner_one(jax.random.fold_in(seeds[19], 71), 0),
        "adjacency_one": noise(seeds[8], (N_SLAB * N_GRP * (B1 // BLK), BLK, K1 * BLK), (K1 * BLK) ** -0.5, 0.25, ((0, 128),)),
        "columns_one": place_ends(jax.random.randint(seeds[9], (N_SLAB * N_GRP * (B1 // BLK), K1), 0, N_GRP * (B1 // BLK)), jax.random.fold_in(seeds[9], 1), 0, (N_GRP * (B1 // BLK)) - 1).astype(jnp.int32),
        "pool_two": noise(seeds[10], (N_SLAB * N_GRP * (C2 // BLK), BLK, KR * BLK), (KR * BLK) ** -0.5, 0.25, ((0, 128),)),
        "pool_two_columns": place_ends(jax.random.randint(seeds[11], (N_SLAB * N_GRP * (C2 // BLK), KR), 0, B1 // BLK), jax.random.fold_in(seeds[11], 1), 0, (B1 // BLK) - 1).astype(jnp.int32),
        "count_two": draw_count_two(jax.random.fold_in(seeds[19], 71), 0),
        "owner_two": draw_owner_two(jax.random.fold_in(seeds[19], 71), 0),
        "adjacency_two": noise(seeds[14], (N_SLAB * N_GRP * (B2 // BLK), BLK, K2 * BLK), (K2 * BLK) ** -0.5, 0.25, ((0, 128),)),
        "columns_two": place_ends(jax.random.randint(seeds[15], (N_SLAB * N_GRP * (B2 // BLK), K2), 0, N_GRP * (B2 // BLK)), jax.random.fold_in(seeds[15], 1), 0, (N_GRP * (B2 // BLK)) - 1).astype(jnp.int32),
        "weight_in": noise(seeds[16], (3, 2 * H, H), (2 * H) ** -0.5, 0.375),
        "weight_out": noise(seeds[17], (3, H, H), H ** -0.5, 0.5),
        "biases": noise(seeds[18], (3, H), 0.5, 3.0, (), jnp.float32),
    }


HIGHEST_PRECISION = lax.Precision.HIGHEST

def device_map(function, *arrays):
    return lax.map(lambda packed: function(*packed), arrays)

def block_apply(blocks, columns, context):
    block_count, block_rows, span = blocks.shape
    feature = context.shape[1]
    tiles = context.reshape(-1, block_rows, feature)
    picked = tiles[columns].reshape(block_count, span, feature)
    product = jnp.einsum('rij,rjh->rih', blocks.astype(jnp.float32), picked.astype(jnp.float32), precision=HIGHEST_PRECISION)
    return product.reshape(block_count * block_rows, feature)

def block_transpose(blocks, columns, row_grads, targets):
    block_count, block_rows, span = blocks.shape
    feature = row_grads.shape[1]
    pieces = row_grads.reshape(block_count, block_rows, feature)
    spread = jnp.einsum('rij,rih->rjh', blocks.astype(jnp.float32), pieces.astype(jnp.float32), precision=HIGHEST_PRECISION)
    spread = spread.reshape(block_count * columns.shape[1], block_rows, feature)
    summed = jax.ops.segment_sum(spread, columns.reshape(-1), num_segments=targets)
    return summed.reshape(targets * block_rows, feature)

def restrict(blocks, columns, source, live_mask):
    pooled = block_apply(blocks, columns, source)
    return jnp.where(live_mask[:, None], pooled, 0.0).astype(jnp.bfloat16)

def layer_forward(node_rows, message, weight_in, weight_out, bias_row):
    joined = jnp.concatenate([node_rows, message], axis=1)
    pre_act = jnp.dot(joined, weight_in, preferred_element_type=jnp.float32) + bias_row
    hidden = jax.nn.silu(pre_act).astype(jnp.bfloat16)
    result = node_rows.astype(jnp.float32) + jnp.dot(hidden, weight_out, preferred_element_type=jnp.float32)
    return (result.astype(jnp.bfloat16), pre_act, hidden)

def layer_backward(cotan_rows, node_rows, message, hidden, pre_act, weight_in, weight_out, blocks, columns, targets):
    grad_low = cotan_rows.astype(jnp.bfloat16)
    delta_out = lax.dot_general(hidden, grad_low, (((0,), (0,)), ((), ())), preferred_element_type=jnp.float32)
    grad_hidden = lax.dot_general(grad_low, weight_out, (((1,), (1,)), ((), ())), preferred_element_type=jnp.float32)
    sigmoid_pre = jax.nn.sigmoid(pre_act)
    grad_pre = grad_hidden * sigmoid_pre * (1.0 + pre_act * (1.0 - sigmoid_pre))
    grad_pre_low = grad_pre.astype(jnp.bfloat16)
    delta_bias = lax.optimization_barrier(jnp.sum(grad_pre, axis=0))
    joined = jnp.concatenate([node_rows, message], axis=1)
    delta_in = lax.dot_general(joined, grad_pre_low, (((0,), (0,)), ((), ())), preferred_element_type=jnp.float32)
    grad_joined = lax.dot_general(grad_pre_low, weight_in, (((1,), (1,)), ((), ())), preferred_element_type=jnp.float32)
    feature = node_rows.shape[1]
    grad_rows = cotan_rows + grad_joined[:, :feature]
    grad_message = grad_joined[:, feature:].astype(jnp.bfloat16)
    grad_context = block_transpose(blocks, columns, grad_message, targets)
    return ((delta_in, delta_out, delta_bias), grad_rows, grad_context)

def pick_slots(table, owners, live_mask):
    taken = jnp.take(table, jnp.clip(owners, 0, table.shape[0] - 1), axis=0)
    return jnp.where(live_mask[..., None], taken, jnp.zeros_like(taken))

def slab_pass(items, weight_in, weight_out, biases):
    node_feats, cotangent, fine_adjacency, fine_columns, pool_one, pool_one_columns, count_one, owner_one, adjacency_one, columns_one, pool_two, pool_two_columns, count_two, owner_two, adjacency_two, columns_two = items
    zero_rim = jnp.zeros((1, HALO, H), jnp.bfloat16)
    before = jnp.concatenate([zero_rim, node_feats[:-1, F_DEV - HALO:]], axis=0)
    after = jnp.concatenate([node_feats[1:, :HALO], zero_rim], axis=0)
    extended = jnp.concatenate([before, node_feats, after], axis=1)

    def fine_message(blocks, columns, context):
        return block_apply(blocks, columns, context).astype(jnp.bfloat16)
    message0 = device_map(fine_message, fine_adjacency, fine_columns, extended)
    result0, pre_act0, hidden0 = device_map(lambda node_rows, message: layer_forward(node_rows, message, weight_in[0], weight_out[0], biases[0]), node_feats, message0)
    live_one = jnp.arange(C1)[None, :] < count_one[:, None]
    coarse_one = device_map(restrict, pool_one, pool_one_columns, result0, live_one)
    target_one = jnp.where(live_one, owner_one, N_GRP * B1).reshape(-1)
    whole_one = jnp.zeros((N_GRP * B1, H), jnp.bfloat16).at[target_one].set(coarse_one.reshape(-1, H), mode='drop')
    message_one = device_map(lambda blocks, columns: fine_message(blocks, columns, whole_one), adjacency_one, columns_one)
    own_one = whole_one.reshape(N_GRP, B1, H)
    result1, pre_act1, hidden1 = device_map(lambda node_rows, message: layer_forward(node_rows, message, weight_in[1], weight_out[1], biases[1]), own_one, message_one)
    live_two = jnp.arange(C2)[None, :] < count_two[:, None]
    coarse_two = device_map(restrict, pool_two, pool_two_columns, result1, live_two)
    target_two = jnp.where(live_two, owner_two, N_GRP * B2).reshape(-1)
    whole_two = jnp.zeros((N_GRP * B2, H), jnp.bfloat16).at[target_two].set(coarse_two.reshape(-1, H), mode='drop')
    message_two = device_map(lambda blocks, columns: fine_message(blocks, columns, whole_two), adjacency_two, columns_two)
    own_two = whole_two.reshape(N_GRP, B2, H)
    result2, pre_act2, hidden2 = device_map(lambda node_rows, message: layer_forward(node_rows, message, weight_in[2], weight_out[2], biases[2]), own_two, message_two)
    back_two = pick_slots(result2.reshape(-1, H), owner_two, live_two)

    def lift_one(blocks, columns, spread, base):
        return (base.astype(jnp.float32) + block_transpose(blocks, columns, spread, B1 // BLK)).astype(jnp.bfloat16)

    def lift_zero(blocks, columns, spread, base):
        return (base.astype(jnp.float32) + block_transpose(blocks, columns, spread, F_DEV // BLK)).astype(jnp.bfloat16)
    up_one = device_map(lift_one, pool_two, pool_two_columns, back_two, result1)
    back_one = pick_slots(up_one.reshape(-1, H), owner_one, live_one)
    node_out = device_map(lift_zero, pool_one, pool_one_columns, back_one, result0)
    grad_slots_one = device_map(restrict, pool_one, pool_one_columns, cotangent, live_one)
    grad_up_one = jnp.zeros((N_GRP * B1, H), jnp.bfloat16).at[target_one].set(grad_slots_one.reshape(-1, H), mode='drop').reshape(N_GRP, B1, H)
    grad_slots_two = device_map(restrict, pool_two, pool_two_columns, grad_up_one, live_two)
    grad_out_two = jnp.zeros((N_GRP * B2, H), jnp.bfloat16).at[target_two].set(grad_slots_two.reshape(-1, H), mode='drop').reshape(N_GRP, B2, H)
    sums_two, grad_rows_two, grad_ctx_two = device_map(lambda cotan_rows, node_rows, message, hidden, pre_act, blocks, columns: layer_backward(cotan_rows.astype(jnp.float32), node_rows, message, hidden, pre_act, weight_in[2], weight_out[2], blocks, columns, N_GRP * B2 // BLK), grad_out_two, own_two, message_two, hidden2, pre_act2, adjacency_two, columns_two)
    grad_own_two = grad_rows_two + lax.optimization_barrier(jnp.sum(grad_ctx_two, axis=0)).reshape(N_GRP, B2, H)
    grad_coarse_two = pick_slots(grad_own_two.reshape(-1, H).astype(jnp.bfloat16), owner_two, live_two)
    grad_out_one = device_map(lambda base, blocks, columns, spread: base.astype(jnp.float32) + block_transpose(blocks, columns, spread, B1 // BLK), grad_up_one, pool_two, pool_two_columns, grad_coarse_two)
    sums_one, grad_rows_one, grad_ctx_one = device_map(lambda cotan_rows, node_rows, message, hidden, pre_act, blocks, columns: layer_backward(cotan_rows, node_rows, message, hidden, pre_act, weight_in[1], weight_out[1], blocks, columns, N_GRP * B1 // BLK), grad_out_one, own_one, message_one, hidden1, pre_act1, adjacency_one, columns_one)
    grad_own_one = grad_rows_one + lax.optimization_barrier(jnp.sum(grad_ctx_one, axis=0)).reshape(N_GRP, B1, H)
    grad_coarse_one = pick_slots(grad_own_one.reshape(-1, H).astype(jnp.bfloat16), owner_one, live_one)
    grad_out_zero = device_map(lambda base, blocks, columns, spread: base.astype(jnp.float32) + block_transpose(blocks, columns, spread, F_DEV // BLK), cotangent, pool_one, pool_one_columns, grad_coarse_one)
    sums_zero, grad_rows_zero, grad_ctx_zero = device_map(lambda cotan_rows, node_rows, message, hidden, pre_act, blocks, columns: layer_backward(cotan_rows, node_rows, message, hidden, pre_act, weight_in[0], weight_out[0], blocks, columns, (F_DEV + 2 * HALO) // BLK), grad_out_zero, node_feats, message0, hidden0, pre_act0, fine_adjacency, fine_columns)
    zero_grads = jnp.zeros((1, HALO, H), jnp.float32)
    from_next = jnp.concatenate([grad_ctx_zero[1:, :HALO], zero_grads], axis=0)
    from_prev = jnp.concatenate([zero_grads, grad_ctx_zero[:-1, HALO + F_DEV:]], axis=0)
    middle = grad_rows_zero + grad_ctx_zero[:, HALO:HALO + F_DEV]
    middle = middle.at[:, :HALO].add(from_prev).at[:, F_DEV - HALO:].add(from_next)
    grad_feats = middle.astype(jnp.bfloat16)
    stack_in = jnp.stack([lax.optimization_barrier(jnp.sum(sums_zero[0], axis=0)), lax.optimization_barrier(jnp.sum(sums_one[0], axis=0)), lax.optimization_barrier(jnp.sum(sums_two[0], axis=0))])
    stack_out = jnp.stack([lax.optimization_barrier(jnp.sum(sums_zero[1], axis=0)), lax.optimization_barrier(jnp.sum(sums_one[1], axis=0)), lax.optimization_barrier(jnp.sum(sums_two[1], axis=0))])
    stack_bias = jnp.stack([lax.optimization_barrier(jnp.sum(sums_zero[2], axis=0)), lax.optimization_barrier(jnp.sum(sums_one[2], axis=0)), lax.optimization_barrier(jnp.sum(sums_two[2], axis=0))])
    return (node_out, grad_feats, stack_in, stack_out, stack_bias)

def reference(node_feats, cotangent, fine_adjacency, fine_columns, pool_one, pool_one_columns, count_one, owner_one, adjacency_one, columns_one, pool_two, pool_two_columns, count_two, owner_two, adjacency_two, columns_two, weight_in, weight_out, biases):

    def split_slab(array):
        return array.reshape((N_SLAB, N_GRP, -1) + array.shape[1:])
    items = (split_slab(node_feats), split_slab(cotangent), split_slab(fine_adjacency), split_slab(fine_columns), split_slab(pool_one), split_slab(pool_one_columns), count_one.reshape(N_SLAB, N_GRP), split_slab(owner_one), split_slab(adjacency_one), split_slab(columns_one), split_slab(pool_two), split_slab(pool_two_columns), count_two.reshape(N_SLAB, N_GRP), split_slab(owner_two), split_slab(adjacency_two), split_slab(columns_two))
    outcome = lax.map(lambda packed: slab_pass(packed, weight_in, weight_out, biases), items)
    inv_root = 1.0 / math.sqrt(NODES)
    return (outcome[0].reshape(-1, H), outcome[1].reshape(-1, H), lax.optimization_barrier(jnp.sum(outcome[2], axis=0)) * inv_root, lax.optimization_barrier(jnp.sum(outcome[3], axis=0)) * inv_root, lax.optimization_barrier(jnp.sum(outcome[4], axis=0)) * inv_root)
```

```python
import functools
import math

import jax
import jax.numpy as jnp
from jax import lax
from jax.experimental import pallas as pl
from jax.experimental.pallas import tpu as pltpu
from jax.sharding import PartitionSpec as P

HALO = 512


def with_halo(cells, sides, width):
    for axis, dim in sides:
        count = lax.axis_size(axis)
        ends = count - 1
        head = lax.slice_in_dim(cells, 0, width, axis=dim)
        tail = lax.slice_in_dim(cells, cells.shape[dim] - width, cells.shape[dim], axis=dim)
        cells = jnp.concatenate(
            [
                lax.ppermute(tail, axis, [(i, (i + 1) % count) for i in range(ends)]),
                cells,
                lax.ppermute(head, axis, [((i + 1) % count, i) for i in range(ends)]),
            ],
            axis=dim,
        )
    return cells


def _per_step(block_count):
    return min(block_count, 8)


def _apply_kernel(cols_ref, m_ref, q_ref, o_ref, *, k, per_step, blk):
    step = pl.program_id(0)
    for j in range(per_step):
        r = step * per_step + j
        pieces = [
            q_ref[pl.ds(pl.multiple_of(cols_ref[r * k + i] * blk, blk), blk), :] for i in range(k)
        ]
        stacked = jnp.concatenate(pieces, axis=0)
        res = jnp.dot(m_ref[j], stacked, preferred_element_type=jnp.float32)
        o_ref[j * blk : (j + 1) * blk, :] = res.astype(o_ref.dtype)


def block_apply(blocks, columns, context, out_dtype=jnp.bfloat16):
    block_count, block_rows, span = blocks.shape
    k = columns.shape[1]
    rows, feature = context.shape
    per_step = _per_step(block_count)
    kernel = functools.partial(_apply_kernel, k=k, per_step=per_step, blk=block_rows)
    return pl.pallas_call(
        kernel,
        out_shape=jax.ShapeDtypeStruct((block_count * block_rows, feature), out_dtype),
        grid_spec=pltpu.PrefetchScalarGridSpec(
            num_scalar_prefetch=1,
            grid=(block_count // per_step,),
            in_specs=[
                pl.BlockSpec((per_step, block_rows, span), lambda s, c: (s, 0, 0)),
                pl.BlockSpec((rows, feature), lambda s, c: (0, 0)),
            ],
            out_specs=pl.BlockSpec((per_step * block_rows, feature), lambda s, c: (s, 0)),
        ),
        cost_estimate=pl.CostEstimate(
            flops=2 * block_count * block_rows * span * feature,
            transcendentals=0,
            bytes_accessed=blocks.size * 2 + context.size * 2 + block_count * block_rows * feature * 4,
        ),
    )(columns.reshape(-1), blocks, context)


def _apply_t_kernel(cols_ref, m_ref, p_ref, o_ref, *, k, per_step, blk):
    step = pl.program_id(0)

    @pl.when(step == 0)
    def _():
        o_ref[...] = jnp.zeros_like(o_ref)

    for j in range(per_step):
        r = step * per_step + j
        spread = lax.dot_general(
            m_ref[j],
            p_ref[j * blk : (j + 1) * blk, :],
            (((0,), (0,)), ((), ())),
            preferred_element_type=jnp.float32,
        )
        for i in range(k):
            at = pl.multiple_of(cols_ref[r * k + i] * blk, blk)
            o_ref[pl.ds(at, blk), :] += spread[i * blk : (i + 1) * blk]


def block_transpose(blocks, columns, row_grads, targets):
    block_count, block_rows, span = blocks.shape
    k = columns.shape[1]
    feature = row_grads.shape[1]
    per_step = _per_step(block_count)
    kernel = functools.partial(_apply_t_kernel, k=k, per_step=per_step, blk=block_rows)
    return pl.pallas_call(
        kernel,
        out_shape=jax.ShapeDtypeStruct((targets * block_rows, feature), jnp.float32),
        grid_spec=pltpu.PrefetchScalarGridSpec(
            num_scalar_prefetch=1,
            grid=(block_count // per_step,),
            in_specs=[
                pl.BlockSpec((per_step, block_rows, span), lambda s, c: (s, 0, 0)),
                pl.BlockSpec((per_step * block_rows, feature), lambda s, c: (s, 0)),
            ],
            out_specs=pl.BlockSpec((targets * block_rows, feature), lambda s, c: (0, 0)),
        ),
        compiler_params=pltpu.CompilerParams(dimension_semantics=("arbitrary",)),
        cost_estimate=pl.CostEstimate(
            flops=2 * block_count * block_rows * span * feature,
            transcendentals=0,
            bytes_accessed=blocks.size * 2 + row_grads.size * 2 + targets * block_rows * feature * 4,
        ),
    )(columns.reshape(-1), blocks, row_grads.astype(jnp.bfloat16))


def grp_gather(rows):
    groups = lax.axis_size("grp")
    spread = jnp.broadcast_to(rows[None], (groups,) + rows.shape)
    return lax.all_to_all(spread, "grp", 0, 0, tiled=True).reshape(-1, rows.shape[1])


def grp_sum_scatter(values):
    groups = lax.axis_size("grp")
    pieces = values.astype(jnp.bfloat16).reshape(groups, -1, values.shape[1])
    got = lax.all_to_all(pieces, "grp", 0, 0, tiled=True)
    return jnp.sum(got.astype(jnp.float32), axis=0)


def all_sum(parts):
    axes = ("slab", "grp")
    devices = lax.axis_size("slab") * lax.axis_size("grp")
    flat = jnp.concatenate([p.reshape(-1) for p in parts])
    total = flat.shape[0]
    chunk = -(-total // devices)
    chunk = -(-chunk // 128) * 128
    flat = jnp.pad(flat, (0, devices * chunk - total)).reshape(devices, chunk)
    got = lax.all_to_all(flat, axes, 0, 0, tiled=True)
    mine = jnp.sum(got, axis=0, keepdims=True)
    back = lax.all_to_all(jnp.broadcast_to(mine, (devices, chunk)), axes, 0, 0, tiled=True)
    back = back.reshape(-1)[:total]
    out, at = [], 0
    for p in parts:
        out.append(back[at : at + p.size].reshape(p.shape))
        at += p.size
    return out


def restrict(blocks, columns, source, live_mask):
    pooled = block_apply(blocks, columns, source)
    return jnp.where(live_mask[:, None], pooled, jnp.zeros_like(pooled))


def layer_forward(node_rows, message, weight_in, weight_out, bias_row):
    joined = jnp.concatenate([node_rows, message], axis=1)
    pre_act = jnp.dot(joined, weight_in, preferred_element_type=jnp.float32) + bias_row
    hidden = jax.nn.silu(pre_act).astype(jnp.bfloat16)
    result = node_rows.astype(jnp.float32) + jnp.dot(
        hidden, weight_out, preferred_element_type=jnp.float32
    )
    return (result.astype(jnp.bfloat16), pre_act, hidden)


def layer_backward(
    cotan_rows, node_rows, message, hidden, pre_act, weight_in, weight_out, blocks, columns, targets
):
    grad_low = cotan_rows.astype(jnp.bfloat16)
    delta_out = lax.dot_general(
        hidden, grad_low, (((0,), (0,)), ((), ())), preferred_element_type=jnp.float32
    )
    grad_hidden = lax.dot_general(
        grad_low, weight_out, (((1,), (1,)), ((), ())), preferred_element_type=jnp.float32
    )
    sigmoid_pre = jax.nn.sigmoid(pre_act)
    grad_pre = grad_hidden * sigmoid_pre * (1.0 + pre_act * (1.0 - sigmoid_pre))
    grad_pre_low = grad_pre.astype(jnp.bfloat16)
    delta_bias = jnp.sum(grad_pre, axis=0)
    joined = jnp.concatenate([node_rows, message], axis=1)
    delta_in = lax.dot_general(
        joined, grad_pre_low, (((0,), (0,)), ((), ())), preferred_element_type=jnp.float32
    )
    grad_joined = lax.dot_general(
        grad_pre_low, weight_in, (((1,), (1,)), ((), ())), preferred_element_type=jnp.float32
    )
    feature = node_rows.shape[1]
    grad_rows = cotan_rows + grad_joined[:, :feature]
    grad_message = grad_joined[:, feature:].astype(jnp.bfloat16)
    grad_context = block_transpose(blocks, columns, grad_message, targets)
    return ((delta_in, delta_out, delta_bias), grad_rows, grad_context)


def pack_layout(owners, live_mask, groups, balance):
    slot_count = owners.shape[0]
    capacity = slot_count // groups
    target = owners // balance
    onehot = (
        (target[:, None] == jnp.arange(groups, dtype=jnp.int32)[None, :]) & live_mask[:, None]
    ).astype(jnp.int32)
    slot_ranks = jnp.sum(onehot * jnp.cumsum(onehot, axis=0), axis=1) - 1
    place_at = jnp.where(live_mask, target * capacity + slot_ranks, groups * capacity)
    row_table = (
        jnp.full((groups * capacity,), balance, jnp.int32)
        .at[place_at]
        .set(owners % balance, mode="drop")
    )
    return (place_at, row_table.reshape(groups, capacity))


def pack_values(values, place_at, groups):
    capacity = values.shape[0] // groups
    buffer = (
        jnp.zeros((groups * capacity, values.shape[1]), values.dtype)
        .at[place_at]
        .set(values, mode="drop")
    )
    return buffer.reshape(groups, capacity, values.shape[1])


def place_rows(received, row_table, balance):
    feature = received.shape[-1]
    flat = received.reshape(-1, feature)
    return (
        jnp.zeros((balance, feature), received.dtype)
        .at[row_table.reshape(-1)]
        .set(flat, mode="drop")
    )


def pick_rows(table, row_table):
    balance = table.shape[0]
    flat = row_table.reshape(-1)
    taken = jnp.take(table, jnp.clip(flat, 0, balance - 1), axis=0)
    taken = jnp.where((flat < balance)[:, None], taken, jnp.zeros_like(taken))
    return taken.reshape(row_table.shape[0], row_table.shape[1], table.shape[1])


def unpack_rows(received, place_at, live_mask):
    feature = received.shape[-1]
    flat = received.reshape(-1, feature)
    taken = jnp.take(flat, jnp.clip(place_at, 0, flat.shape[0] - 1), axis=0)
    return jnp.where(live_mask[:, None], taken, jnp.zeros_like(taken))


def body(
    node_feats,
    cotangent,
    fine_adjacency,
    fine_columns,
    pool_one,
    pool_one_columns,
    count_one,
    owner_one,
    adjacency_one,
    columns_one,
    pool_two,
    pool_two_columns,
    count_two,
    owner_two,
    adjacency_two,
    columns_two,
    weight_in,
    weight_out,
    biases,
):
    groups = lax.axis_size("grp")
    block_rows = fine_adjacency.shape[1]
    fine_rows = node_feats.shape[0]
    slots_one = owner_one.shape[0]
    balance_one = slots_one // 2
    slots_two = owner_two.shape[0]
    balance_two = slots_two // 2
    extended = with_halo(node_feats, (("grp", 0),), HALO)
    message0 = block_apply(fine_adjacency, fine_columns, extended)
    result0, pre_act0, hidden0 = layer_forward(
        node_feats, message0, weight_in[0], weight_out[0], biases[0]
    )
    live_one = jnp.arange(slots_one) < count_one[0]
    coarse_one = restrict(pool_one, pool_one_columns, result0, live_one)
    place_one, sent_one = pack_layout(owner_one, live_one, groups, balance_one)
    got_values, rows_one = (
        lax.all_to_all(
            pack_values(coarse_one, place_one, groups),
            "grp",
            split_axis=0,
            concat_axis=0,
            tiled=True,
        ),
        lax.all_to_all(sent_one, "grp", split_axis=0, concat_axis=0, tiled=True),
    )
    own_one = place_rows(got_values, rows_one, balance_one)
    context_one = grp_gather(own_one)
    message_one = block_apply(adjacency_one, columns_one, context_one)
    result1, pre_act1, hidden1 = layer_forward(
        own_one, message_one, weight_in[1], weight_out[1], biases[1]
    )
    live_two = jnp.arange(slots_two) < count_two[0]
    coarse_two = restrict(pool_two, pool_two_columns, result1, live_two)
    place_two, sent_two = pack_layout(owner_two, live_two, groups, balance_two)
    got_two, rows_two = (
        lax.all_to_all(
            pack_values(coarse_two, place_two, groups),
            "grp",
            split_axis=0,
            concat_axis=0,
            tiled=True,
        ),
        lax.all_to_all(sent_two, "grp", split_axis=0, concat_axis=0, tiled=True),
    )
    own_two = place_rows(got_two, rows_two, balance_two)
    context_two = grp_gather(own_two)
    message_two = block_apply(adjacency_two, columns_two, context_two)
    result2, pre_act2, hidden2 = layer_forward(
        own_two, message_two, weight_in[2], weight_out[2], biases[2]
    )
    returned_two = lax.all_to_all(
        pick_rows(result2, rows_two), "grp", split_axis=0, concat_axis=0, tiled=True
    )
    back_two = unpack_rows(returned_two, place_two, live_two)
    up_one = (
        result1.astype(jnp.float32)
        + block_transpose(pool_two, pool_two_columns, back_two, balance_one // block_rows)
    ).astype(jnp.bfloat16)
    returned_one = lax.all_to_all(
        pick_rows(up_one, rows_one), "grp", split_axis=0, concat_axis=0, tiled=True
    )
    back_one = unpack_rows(returned_one, place_one, live_one)
    node_out = (
        result0.astype(jnp.float32)
        + block_transpose(pool_one, pool_one_columns, back_one, fine_rows // block_rows)
    ).astype(jnp.bfloat16)
    grad_slots_one = restrict(pool_one, pool_one_columns, cotangent, live_one)
    arrived_one = lax.all_to_all(
        pack_values(grad_slots_one, place_one, groups),
        "grp",
        split_axis=0,
        concat_axis=0,
        tiled=True,
    )
    grad_up_one = place_rows(arrived_one, rows_one, balance_one)
    grad_slots_two = restrict(pool_two, pool_two_columns, grad_up_one, live_two)
    arrived_two = lax.all_to_all(
        pack_values(grad_slots_two, place_two, groups),
        "grp",
        split_axis=0,
        concat_axis=0,
        tiled=True,
    )
    grad_out_two = place_rows(arrived_two, rows_two, balance_two)
    sums_two, grad_rows_two, grad_ctx_two = layer_backward(
        grad_out_two.astype(jnp.float32),
        own_two,
        message_two,
        hidden2,
        pre_act2,
        weight_in[2],
        weight_out[2],
        adjacency_two,
        columns_two,
        groups * balance_two // block_rows,
    )
    grad_own_two = grad_rows_two + grp_sum_scatter(grad_ctx_two)
    sent_back_two = lax.all_to_all(
        pick_rows(grad_own_two.astype(jnp.bfloat16), rows_two),
        "grp",
        split_axis=0,
        concat_axis=0,
        tiled=True,
    )
    grad_coarse_two = unpack_rows(sent_back_two, place_two, live_two)
    grad_out_one = grad_up_one.astype(jnp.float32) + block_transpose(
        pool_two, pool_two_columns, grad_coarse_two, balance_one // block_rows
    )
    sums_one, grad_rows_one, grad_ctx_one = layer_backward(
        grad_out_one,
        own_one,
        message_one,
        hidden1,
        pre_act1,
        weight_in[1],
        weight_out[1],
        adjacency_one,
        columns_one,
        groups * balance_one // block_rows,
    )
    grad_own_one = grad_rows_one + grp_sum_scatter(grad_ctx_one)
    sent_back_one = lax.all_to_all(
        pick_rows(grad_own_one.astype(jnp.bfloat16), rows_one),
        "grp",
        split_axis=0,
        concat_axis=0,
        tiled=True,
    )
    grad_coarse_one = unpack_rows(sent_back_one, place_one, live_one)
    grad_out_zero = cotangent.astype(jnp.float32) + block_transpose(
        pool_one, pool_one_columns, grad_coarse_one, fine_rows // block_rows
    )
    sums_zero, grad_rows_zero, grad_ctx_zero = layer_backward(
        grad_out_zero,
        node_feats,
        message0,
        hidden0,
        pre_act0,
        weight_in[0],
        weight_out[0],
        fine_adjacency,
        fine_columns,
        (fine_rows + 2 * HALO) // block_rows,
    )
    rim_terms = jnp.concatenate([grad_ctx_zero[:HALO], grad_ctx_zero[HALO + fine_rows :]], axis=0)
    neighbour_terms = with_halo(rim_terms.astype(jnp.bfloat16), (("grp", 0),), HALO).astype(
        rim_terms.dtype
    )
    gathered_total = grad_rows_zero + grad_ctx_zero[HALO : HALO + fine_rows]
    gathered_total = gathered_total.at[:HALO].add(neighbour_terms[:HALO])
    gathered_total = gathered_total.at[fine_rows - HALO :].add(neighbour_terms[3 * HALO :])
    grad_feats = gathered_total.astype(jnp.bfloat16)
    stack_in = jnp.stack([sums_zero[0], sums_one[0], sums_two[0]])
    stack_out = jnp.stack([sums_zero[1], sums_one[1], sums_two[1]])
    stack_bias = jnp.stack([sums_zero[2], sums_one[2], sums_two[2]])
    stack_in, stack_out, stack_bias = all_sum((stack_in, stack_out, stack_bias))
    inv_root = 1.0 / math.sqrt(fine_rows * groups * lax.axis_size("slab"))
    return (node_out, grad_feats, stack_in * inv_root, stack_out * inv_root, stack_bias * inv_root)


def solution(mesh):
    placed = (
        P(("slab", "grp"), None),
        P(("slab", "grp"), None),
        P(("slab", "grp"), None, None),
        P(("slab", "grp"), None),
        P(("slab", "grp"), None, None),
        P(("slab", "grp"), None),
        P(("slab", "grp")),
        P(("slab", "grp")),
        P(("slab", "grp"), None, None),
        P(("slab", "grp"), None),
        P(("slab", "grp"), None, None),
        P(("slab", "grp"), None),
        P(("slab", "grp")),
        P(("slab", "grp")),
        P(("slab", "grp"), None, None),
        P(("slab", "grp"), None),
        P(),
        P(),
        P(),
    )
    return jax.shard_map(
        body,
        mesh=mesh,
        in_specs=placed,
        out_specs=(P(("slab", "grp"), None), P(("slab", "grp"), None), P(), P(), P()),
        check_vma=False,
    )
```

```python
import functools
import math

import jax
import jax.numpy as jnp
from jax import lax
from jax.experimental import pallas as pl
from jax.experimental.pallas import tpu as pltpu
from jax.sharding import PartitionSpec as P

HALO = 512


def with_halo(cells, sides, width):
    for axis, dim in sides:
        count = lax.axis_size(axis)
        ends = count - 1
        head = lax.slice_in_dim(cells, 0, width, axis=dim)
        tail = lax.slice_in_dim(cells, cells.shape[dim] - width, cells.shape[dim], axis=dim)
        cells = jnp.concatenate(
            [
                lax.ppermute(tail, axis, [(i, (i + 1) % count) for i in range(ends)]),
                cells,
                lax.ppermute(head, axis, [((i + 1) % count, i) for i in range(ends)]),
            ],
            axis=dim,
        )
    return cells


def _per_step(block_count):
    return min(block_count, 8)


def _apply_kernel(cols_ref, m_ref, q_ref, o_ref, *, k, per_step, blk):
    step = pl.program_id(0)
    for j in range(per_step):
        r = step * per_step + j
        pieces = [
            q_ref[pl.ds(pl.multiple_of(cols_ref[r * k + i] * blk, blk), blk), :] for i in range(k)
        ]
        stacked = jnp.concatenate(pieces, axis=0)
        res = jnp.dot(m_ref[j], stacked, preferred_element_type=jnp.float32)
        o_ref[j * blk : (j + 1) * blk, :] = res.astype(o_ref.dtype)


def block_apply(blocks, columns, context, out_dtype=jnp.bfloat16):
    block_count, block_rows, span = blocks.shape
    k = columns.shape[1]
    rows, feature = context.shape
    per_step = _per_step(block_count)
    kernel = functools.partial(_apply_kernel, k=k, per_step=per_step, blk=block_rows)
    return pl.pallas_call(
        kernel,
        out_shape=jax.ShapeDtypeStruct((block_count * block_rows, feature), out_dtype),
        grid_spec=pltpu.PrefetchScalarGridSpec(
            num_scalar_prefetch=1,
            grid=(block_count // per_step,),
            in_specs=[
                pl.BlockSpec((per_step, block_rows, span), lambda s, c: (s, 0, 0)),
                pl.BlockSpec((rows, feature), lambda s, c: (0, 0)),
            ],
            out_specs=pl.BlockSpec((per_step * block_rows, feature), lambda s, c: (s, 0)),
        ),
        cost_estimate=pl.CostEstimate(
            flops=2 * block_count * block_rows * span * feature,
            transcendentals=0,
            bytes_accessed=blocks.size * 2 + context.size * 2 + block_count * block_rows * feature * 4,
        ),
    )(columns.reshape(-1), blocks, context)


def _apply_t_kernel(cols_ref, m_ref, p_ref, o_ref, *, k, per_step, blk):
    step = pl.program_id(0)

    @pl.when(step == 0)
    def _():
        o_ref[...] = jnp.zeros_like(o_ref)

    for j in range(per_step):
        r = step * per_step + j
        spread = lax.dot_general(
            m_ref[j],
            p_ref[j * blk : (j + 1) * blk, :],
            (((0,), (0,)), ((), ())),
            preferred_element_type=jnp.float32,
        )
        for i in range(k):
            at = pl.multiple_of(cols_ref[r * k + i] * blk, blk)
            o_ref[pl.ds(at, blk), :] += spread[i * blk : (i + 1) * blk]


def block_transpose(blocks, columns, row_grads, targets):
    block_count, block_rows, span = blocks.shape
    k = columns.shape[1]
    feature = row_grads.shape[1]
    per_step = _per_step(block_count)
    kernel = functools.partial(_apply_t_kernel, k=k, per_step=per_step, blk=block_rows)
    return pl.pallas_call(
        kernel,
        out_shape=jax.ShapeDtypeStruct((targets * block_rows, feature), jnp.float32),
        grid_spec=pltpu.PrefetchScalarGridSpec(
            num_scalar_prefetch=1,
            grid=(block_count // per_step,),
            in_specs=[
                pl.BlockSpec((per_step, block_rows, span), lambda s, c: (s, 0, 0)),
                pl.BlockSpec((per_step * block_rows, feature), lambda s, c: (s, 0)),
            ],
            out_specs=pl.BlockSpec((targets * block_rows, feature), lambda s, c: (0, 0)),
        ),
        compiler_params=pltpu.CompilerParams(dimension_semantics=("arbitrary",)),
        cost_estimate=pl.CostEstimate(
            flops=2 * block_count * block_rows * span * feature,
            transcendentals=0,
            bytes_accessed=blocks.size * 2 + row_grads.size * 2 + targets * block_rows * feature * 4,
        ),
    )(columns.reshape(-1), blocks, row_grads.astype(jnp.bfloat16))


def grp_gather(rows):
    groups = lax.axis_size("grp")
    spread = jnp.broadcast_to(rows[None], (groups,) + rows.shape)
    return lax.all_to_all(spread, "grp", 0, 0, tiled=True).reshape(-1, rows.shape[1])


def grp_sum_scatter(values):
    groups = lax.axis_size("grp")
    pieces = values.astype(jnp.bfloat16).reshape(groups, -1, values.shape[1])
    got = lax.all_to_all(pieces, "grp", 0, 0, tiled=True)
    return jnp.sum(got.astype(jnp.float32), axis=0)


def all_sum(parts):
    axes = ("slab", "grp")
    devices = lax.axis_size("slab") * lax.axis_size("grp")
    flat = jnp.concatenate([p.reshape(-1) for p in parts])
    total = flat.shape[0]
    chunk = -(-total // devices)
    chunk = -(-chunk // 128) * 128
    flat = jnp.pad(flat, (0, devices * chunk - total)).reshape(devices, chunk)
    got = lax.all_to_all(flat, axes, 0, 0, tiled=True)
    mine = jnp.sum(got, axis=0, keepdims=True)
    back = lax.all_to_all(jnp.broadcast_to(mine, (devices, chunk)), axes, 0, 0, tiled=True)
    back = back.reshape(-1)[:total]
    out, at = [], 0
    for p in parts:
        out.append(back[at : at + p.size].reshape(p.shape))
        at += p.size
    return out


def restrict(blocks, columns, source, live_mask):
    pooled = block_apply(blocks, columns, source)
    return jnp.where(live_mask[:, None], pooled, jnp.zeros_like(pooled))


def layer_forward(node_rows, message, weight_in, weight_out, bias_row):
    joined = jnp.concatenate([node_rows, message], axis=1)
    pre_act = jnp.dot(joined, weight_in, preferred_element_type=jnp.float32) + bias_row
    hidden = jax.nn.silu(pre_act).astype(jnp.bfloat16)
    result = node_rows.astype(jnp.float32) + jnp.dot(
        hidden, weight_out, preferred_element_type=jnp.float32
    )
    return (result.astype(jnp.bfloat16), pre_act, hidden)


def layer_backward(
    cotan_rows, node_rows, message, hidden, pre_act, weight_in, weight_out, blocks, columns, targets
):
    grad_low = cotan_rows.astype(jnp.bfloat16)
    delta_out = lax.dot_general(
        hidden, grad_low, (((0,), (0,)), ((), ())), preferred_element_type=jnp.float32
    )
    grad_hidden = lax.dot_general(
        grad_low, weight_out, (((1,), (1,)), ((), ())), preferred_element_type=jnp.float32
    )
    sigmoid_pre = jax.nn.sigmoid(pre_act)
    grad_pre = grad_hidden * sigmoid_pre * (1.0 + pre_act * (1.0 - sigmoid_pre))
    grad_pre_low = grad_pre.astype(jnp.bfloat16)
    delta_bias = jnp.sum(grad_pre, axis=0)
    joined = jnp.concatenate([node_rows, message], axis=1)
    delta_in = lax.dot_general(
        joined, grad_pre_low, (((0,), (0,)), ((), ())), preferred_element_type=jnp.float32
    )
    grad_joined = lax.dot_general(
        grad_pre_low, weight_in, (((1,), (1,)), ((), ())), preferred_element_type=jnp.float32
    )
    feature = node_rows.shape[1]
    grad_rows = cotan_rows + grad_joined[:, :feature]
    grad_message = grad_joined[:, feature:].astype(jnp.bfloat16)
    grad_context = block_transpose(blocks, columns, grad_message, targets)
    return ((delta_in, delta_out, delta_bias), grad_rows, grad_context)


def pack_layout(owners, live_mask, groups, balance):
    slot_count = owners.shape[0]
    capacity = slot_count // groups
    target = owners // balance
    onehot = (
        (target[:, None] == jnp.arange(groups, dtype=jnp.int32)[None, :]) & live_mask[:, None]
    ).astype(jnp.int32)
    slot_ranks = jnp.sum(onehot * jnp.cumsum(onehot, axis=0), axis=1) - 1
    place_at = jnp.where(live_mask, target * capacity + slot_ranks, groups * capacity)
    row_table = (
        jnp.full((groups * capacity,), balance, jnp.int32)
        .at[place_at]
        .set(owners % balance, mode="drop")
    )
    return (place_at, row_table.reshape(groups, capacity))


def pack_values(values, place_at, groups):
    capacity = values.shape[0] // groups
    buffer = (
        jnp.zeros((groups * capacity, values.shape[1]), values.dtype)
        .at[place_at]
        .set(values, mode="drop")
    )
    return buffer.reshape(groups, capacity, values.shape[1])


def place_rows(received, row_table, balance):
    feature = received.shape[-1]
    flat = received.reshape(-1, feature)
    return (
        jnp.zeros((balance, feature), received.dtype)
        .at[row_table.reshape(-1)]
        .set(flat, mode="drop")
    )


def pick_rows(table, row_table):
    balance = table.shape[0]
    flat = row_table.reshape(-1)
    taken = jnp.take(table, jnp.clip(flat, 0, balance - 1), axis=0)
    taken = jnp.where((flat < balance)[:, None], taken, jnp.zeros_like(taken))
    return taken.reshape(row_table.shape[0], row_table.shape[1], table.shape[1])


def unpack_rows(received, place_at, live_mask):
    feature = received.shape[-1]
    flat = received.reshape(-1, feature)
    taken = jnp.take(flat, jnp.clip(place_at, 0, flat.shape[0] - 1), axis=0)
    return jnp.where(live_mask[:, None], taken, jnp.zeros_like(taken))


def body(
    node_feats,
    cotangent,
    fine_adjacency,
    fine_columns,
    pool_one,
    pool_one_columns,
    count_one,
    owner_one,
    adjacency_one,
    columns_one,
    pool_two,
    pool_two_columns,
    count_two,
    owner_two,
    adjacency_two,
    columns_two,
    weight_in,
    weight_out,
    biases,
):
    groups = lax.axis_size("grp")
    block_rows = fine_adjacency.shape[1]
    fine_rows, feature = node_feats.shape
    slots_one = owner_one.shape[0]
    balance_one = slots_one // 2
    slots_two = owner_two.shape[0]
    balance_two = slots_two // 2
    live_one = jnp.arange(slots_one) < count_one[0]
    live_two = jnp.arange(slots_two) < count_two[0]
    place_one, sent_one = pack_layout(owner_one, live_one, groups, balance_one)
    place_two, sent_two = pack_layout(owner_two, live_two, groups, balance_two)
    rows_one = lax.all_to_all(sent_one, "grp", split_axis=0, concat_axis=0, tiled=True)
    rows_two = lax.all_to_all(sent_two, "grp", split_axis=0, concat_axis=0, tiled=True)

    extended = with_halo(node_feats, (("grp", 0),), HALO)
    message0 = block_apply(fine_adjacency, fine_columns, extended)
    result0, pre_act0, hidden0 = layer_forward(
        node_feats, message0, weight_in[0], weight_out[0], biases[0]
    )
    pooled_one = restrict(
        pool_one, pool_one_columns, jnp.concatenate([result0, cotangent], axis=1), live_one
    )
    got_one = lax.all_to_all(
        pack_values(pooled_one, place_one, groups), "grp", split_axis=0, concat_axis=0, tiled=True
    )
    placed_one = place_rows(got_one, rows_one, balance_one)
    own_one, grad_up_one = placed_one[:, :feature], placed_one[:, feature:]
    context_one = grp_gather(own_one)
    message_one = block_apply(adjacency_one, columns_one, context_one)
    result1, pre_act1, hidden1 = layer_forward(
        own_one, message_one, weight_in[1], weight_out[1], biases[1]
    )
    pooled_two = restrict(
        pool_two, pool_two_columns, jnp.concatenate([result1, grad_up_one], axis=1), live_two
    )
    got_two = lax.all_to_all(
        pack_values(pooled_two, place_two, groups), "grp", split_axis=0, concat_axis=0, tiled=True
    )
    placed_two = place_rows(got_two, rows_two, balance_two)
    own_two, grad_out_two = placed_two[:, :feature], placed_two[:, feature:]
    context_two = grp_gather(own_two)
    message_two = block_apply(adjacency_two, columns_two, context_two)
    result2, pre_act2, hidden2 = layer_forward(
        own_two, message_two, weight_in[2], weight_out[2], biases[2]
    )
    sums_two, grad_rows_two, grad_ctx_two = layer_backward(
        grad_out_two.astype(jnp.float32),
        own_two,
        message_two,
        hidden2,
        pre_act2,
        weight_in[2],
        weight_out[2],
        adjacency_two,
        columns_two,
        groups * balance_two // block_rows,
    )
    grad_own_two = grad_rows_two + grp_sum_scatter(grad_ctx_two)
    returned_two = lax.all_to_all(
        pick_rows(jnp.concatenate([result2, grad_own_two.astype(jnp.bfloat16)], axis=1), rows_two),
        "grp",
        split_axis=0,
        concat_axis=0,
        tiled=True,
    )
    back_two = unpack_rows(returned_two, place_two, live_two)
    lifted_one = block_transpose(pool_two, pool_two_columns, back_two, balance_one // block_rows)
    up_one = (result1.astype(jnp.float32) + lifted_one[:, :feature]).astype(jnp.bfloat16)
    grad_out_one = grad_up_one.astype(jnp.float32) + lifted_one[:, feature:]
    sums_one, grad_rows_one, grad_ctx_one = layer_backward(
        grad_out_one,
        own_one,
        message_one,
        hidden1,
        pre_act1,
        weight_in[1],
        weight_out[1],
        adjacency_one,
        columns_one,
        groups * balance_one // block_rows,
    )
    grad_own_one = grad_rows_one + grp_sum_scatter(grad_ctx_one)
    returned_one = lax.all_to_all(
        pick_rows(jnp.concatenate([up_one, grad_own_one.astype(jnp.bfloat16)], axis=1), rows_one),
        "grp",
        split_axis=0,
        concat_axis=0,
        tiled=True,
    )
    back_one = unpack_rows(returned_one, place_one, live_one)
    lifted_zero = block_transpose(pool_one, pool_one_columns, back_one, fine_rows // block_rows)
    node_out = (result0.astype(jnp.float32) + lifted_zero[:, :feature]).astype(jnp.bfloat16)
    grad_out_zero = cotangent.astype(jnp.float32) + lifted_zero[:, feature:]
    sums_zero, grad_rows_zero, grad_ctx_zero = layer_backward(
        grad_out_zero,
        node_feats,
        message0,
        hidden0,
        pre_act0,
        weight_in[0],
        weight_out[0],
        fine_adjacency,
        fine_columns,
        (fine_rows + 2 * HALO) // block_rows,
    )
    rim_terms = jnp.concatenate([grad_ctx_zero[:HALO], grad_ctx_zero[HALO + fine_rows :]], axis=0)
    neighbour_terms = with_halo(rim_terms.astype(jnp.bfloat16), (("grp", 0),), HALO).astype(
        rim_terms.dtype
    )
    gathered_total = grad_rows_zero + grad_ctx_zero[HALO : HALO + fine_rows]
    gathered_total = gathered_total.at[:HALO].add(neighbour_terms[:HALO])
    gathered_total = gathered_total.at[fine_rows - HALO :].add(neighbour_terms[3 * HALO :])
    grad_feats = gathered_total.astype(jnp.bfloat16)
    stack_in = jnp.stack([sums_zero[0], sums_one[0], sums_two[0]])
    stack_out = jnp.stack([sums_zero[1], sums_one[1], sums_two[1]])
    stack_bias = jnp.stack([sums_zero[2], sums_one[2], sums_two[2]])
    stack_in, stack_out, stack_bias = all_sum((stack_in, stack_out, stack_bias))
    inv_root = 1.0 / math.sqrt(fine_rows * groups * lax.axis_size("slab"))
    return (node_out, grad_feats, stack_in * inv_root, stack_out * inv_root, stack_bias * inv_root)


def solution(mesh):
    placed = (
        P(("slab", "grp"), None),
        P(("slab", "grp"), None),
        P(("slab", "grp"), None, None),
        P(("slab", "grp"), None),
        P(("slab", "grp"), None, None),
        P(("slab", "grp"), None),
        P(("slab", "grp")),
        P(("slab", "grp")),
        P(("slab", "grp"), None, None),
        P(("slab", "grp"), None),
        P(("slab", "grp"), None, None),
        P(("slab", "grp"), None),
        P(("slab", "grp")),
        P(("slab", "grp")),
        P(("slab", "grp"), None, None),
        P(("slab", "grp"), None),
        P(),
        P(),
        P(),
    )
    return jax.shard_map(
        body,
        mesh=mesh,
        in_specs=placed,
        out_specs=(P(("slab", "grp"), None), P(("slab", "grp"), None), P(), P(), P()),
        check_vma=False,
    )
```

```python
import functools
import math

import jax
import jax.numpy as jnp
from jax import lax
from jax.experimental import pallas as pl
from jax.experimental.pallas import tpu as pltpu
from jax.sharding import PartitionSpec as P

HALO = 512


def with_halo(cells, sides, width):
    for axis, dim in sides:
        count = lax.axis_size(axis)
        ends = count - 1
        head = lax.slice_in_dim(cells, 0, width, axis=dim)
        tail = lax.slice_in_dim(cells, cells.shape[dim] - width, cells.shape[dim], axis=dim)
        cells = jnp.concatenate(
            [
                lax.ppermute(tail, axis, [(i, (i + 1) % count) for i in range(ends)]),
                cells,
                lax.ppermute(head, axis, [((i + 1) % count, i) for i in range(ends)]),
            ],
            axis=dim,
        )
    return cells


def halo_parts(cells, axis, width):
    count = lax.axis_size(axis)
    ends = count - 1
    head = cells[:width]
    tail = cells[cells.shape[0] - width :]
    before = lax.ppermute(tail, axis, [(i, (i + 1) % count) for i in range(ends)])
    after = lax.ppermute(head, axis, [((i + 1) % count, i) for i in range(ends)])
    return before, after


def _per_step(block_count):
    return min(block_count, 8)


def _apply_kernel(cols_ref, m_ref, *refs, k, per_step, blk, pieces_in):
    q_parts, (o_ref, q_ref) = refs[:pieces_in], refs[pieces_in:]
    step = pl.program_id(0)

    @pl.when(step == 0)
    def _():
        at = 0
        for part in q_parts:
            q_ref[at : at + part.shape[0], :] = part[...]
            at += part.shape[0]

    for j in range(per_step):
        r = step * per_step + j
        pieces = [
            q_ref[pl.ds(pl.multiple_of(cols_ref[r * k + i] * blk, blk), blk), :] for i in range(k)
        ]
        stacked = jnp.concatenate(pieces, axis=0)
        res = jnp.dot(m_ref[j], stacked, preferred_element_type=jnp.float32)
        o_ref[j * blk : (j + 1) * blk, :] = res.astype(o_ref.dtype)


def block_apply(blocks, columns, context, out_dtype=jnp.bfloat16):
    block_count, block_rows, span = blocks.shape
    k = columns.shape[1]
    parts = tuple(context) if isinstance(context, (tuple, list)) else (context,)
    feature = parts[0].shape[1]
    rows = sum(p.shape[0] for p in parts)
    per_step = _per_step(block_count)
    kernel = functools.partial(
        _apply_kernel, k=k, per_step=per_step, blk=block_rows, pieces_in=len(parts)
    )
    return pl.pallas_call(
        kernel,
        out_shape=jax.ShapeDtypeStruct((block_count * block_rows, feature), out_dtype),
        grid_spec=pltpu.PrefetchScalarGridSpec(
            num_scalar_prefetch=1,
            grid=(block_count // per_step,),
            in_specs=[pl.BlockSpec((per_step, block_rows, span), lambda s, c: (s, 0, 0))]
            + [pl.BlockSpec(p.shape, lambda s, c: (0, 0)) for p in parts],
            out_specs=pl.BlockSpec((per_step * block_rows, feature), lambda s, c: (s, 0)),
            scratch_shapes=[pltpu.VMEM((rows, feature), parts[0].dtype)],
        ),
        compiler_params=pltpu.CompilerParams(dimension_semantics=("arbitrary",)),
        cost_estimate=pl.CostEstimate(
            flops=2 * block_count * block_rows * span * feature,
            transcendentals=0,
            bytes_accessed=blocks.size * 2 + rows * feature * 2 + block_count * block_rows * feature * 2,
        ),
    )(columns.reshape(-1), blocks, *parts)


def _apply_t_kernel(cols_ref, m_ref, p_ref, o_ref, *, k, per_step, blk):
    step = pl.program_id(0)

    @pl.when(step == 0)
    def _():
        o_ref[...] = jnp.zeros_like(o_ref)

    for j in range(per_step):
        r = step * per_step + j
        spread = lax.dot_general(
            m_ref[j],
            p_ref[j * blk : (j + 1) * blk, :],
            (((0,), (0,)), ((), ())),
            preferred_element_type=jnp.float32,
        )
        for i in range(k):
            at = pl.multiple_of(cols_ref[r * k + i] * blk, blk)
            o_ref[pl.ds(at, blk), :] += spread[i * blk : (i + 1) * blk]


def block_transpose(blocks, columns, row_grads, targets):
    block_count, block_rows, span = blocks.shape
    k = columns.shape[1]
    feature = row_grads.shape[1]
    per_step = _per_step(block_count)
    kernel = functools.partial(_apply_t_kernel, k=k, per_step=per_step, blk=block_rows)
    return pl.pallas_call(
        kernel,
        out_shape=jax.ShapeDtypeStruct((targets * block_rows, feature), jnp.float32),
        grid_spec=pltpu.PrefetchScalarGridSpec(
            num_scalar_prefetch=1,
            grid=(block_count // per_step,),
            in_specs=[
                pl.BlockSpec((per_step, block_rows, span), lambda s, c: (s, 0, 0)),
                pl.BlockSpec((per_step * block_rows, feature), lambda s, c: (s, 0)),
            ],
            out_specs=pl.BlockSpec((targets * block_rows, feature), lambda s, c: (0, 0)),
        ),
        compiler_params=pltpu.CompilerParams(dimension_semantics=("arbitrary",)),
        cost_estimate=pl.CostEstimate(
            flops=2 * block_count * block_rows * span * feature,
            transcendentals=0,
            bytes_accessed=blocks.size * 2 + row_grads.size * 2 + targets * block_rows * feature * 4,
        ),
    )(columns.reshape(-1), blocks, row_grads.astype(jnp.bfloat16))


def grp_gather(rows):
    groups = lax.axis_size("grp")
    spread = jnp.broadcast_to(rows[None], (groups,) + rows.shape)
    return lax.all_to_all(spread, "grp", 0, 0, tiled=True).reshape(-1, rows.shape[1])


def grp_sum_scatter(values):
    groups = lax.axis_size("grp")
    pieces = values.astype(jnp.bfloat16).reshape(groups, -1, values.shape[1])
    got = lax.all_to_all(pieces, "grp", 0, 0, tiled=True)
    return jnp.sum(got.astype(jnp.float32), axis=0)


def all_sum(parts):
    axes = ("slab", "grp")
    devices = lax.axis_size("slab") * lax.axis_size("grp")
    flat = jnp.concatenate([p.reshape(-1) for p in parts])
    total = flat.shape[0]
    chunk = -(-total // devices)
    chunk = -(-chunk // 128) * 128
    flat = jnp.pad(flat, (0, devices * chunk - total)).reshape(devices, chunk)
    got = lax.all_to_all(flat, axes, 0, 0, tiled=True)
    mine = jnp.sum(got, axis=0, keepdims=True)
    back = lax.all_to_all(jnp.broadcast_to(mine, (devices, chunk)), axes, 0, 0, tiled=True)
    back = back.reshape(-1)[:total]
    out, at = [], 0
    for p in parts:
        out.append(back[at : at + p.size].reshape(p.shape))
        at += p.size
    return out


def restrict(blocks, columns, source, live_mask):
    pooled = block_apply(blocks, columns, source)
    return jnp.where(live_mask[:, None], pooled, jnp.zeros_like(pooled))


def layer_forward(node_rows, message, weight_in, weight_out, bias_row):
    joined = jnp.concatenate([node_rows, message], axis=1)
    pre_act = jnp.dot(joined, weight_in, preferred_element_type=jnp.float32) + bias_row
    hidden = jax.nn.silu(pre_act).astype(jnp.bfloat16)
    result = node_rows.astype(jnp.float32) + jnp.dot(
        hidden, weight_out, preferred_element_type=jnp.float32
    )
    return (result.astype(jnp.bfloat16), pre_act, hidden)


def layer_backward(
    cotan_rows, node_rows, message, hidden, pre_act, weight_in, weight_out, blocks, columns, targets
):
    grad_low = cotan_rows.astype(jnp.bfloat16)
    delta_out = lax.dot_general(
        hidden, grad_low, (((0,), (0,)), ((), ())), preferred_element_type=jnp.float32
    )
    grad_hidden = lax.dot_general(
        grad_low, weight_out, (((1,), (1,)), ((), ())), preferred_element_type=jnp.float32
    )
    sigmoid_pre = jax.nn.sigmoid(pre_act)
    grad_pre = grad_hidden * sigmoid_pre * (1.0 + pre_act * (1.0 - sigmoid_pre))
    grad_pre_low = grad_pre.astype(jnp.bfloat16)
    delta_bias = jnp.sum(grad_pre, axis=0)
    joined = jnp.concatenate([node_rows, message], axis=1)
    delta_in = lax.dot_general(
        joined, grad_pre_low, (((0,), (0,)), ((), ())), preferred_element_type=jnp.float32
    )
    grad_joined = lax.dot_general(
        grad_pre_low, weight_in, (((1,), (1,)), ((), ())), preferred_element_type=jnp.float32
    )
    feature = node_rows.shape[1]
    grad_rows = cotan_rows + grad_joined[:, :feature]
    grad_message = grad_joined[:, feature:].astype(jnp.bfloat16)
    grad_context = block_transpose(blocks, columns, grad_message, targets)
    return ((delta_in, delta_out, delta_bias), grad_rows, grad_context)


def pack_layout(owners, live_mask, groups, balance):
    slot_count = owners.shape[0]
    capacity = slot_count // groups
    target = owners // balance
    onehot = (
        (target[:, None] == jnp.arange(groups, dtype=jnp.int32)[None, :]) & live_mask[:, None]
    ).astype(jnp.int32)
    slot_ranks = jnp.sum(onehot * jnp.cumsum(onehot, axis=0), axis=1) - 1
    place_at = jnp.where(live_mask, target * capacity + slot_ranks, groups * capacity)
    row_table = (
        jnp.full((groups * capacity,), balance, jnp.int32)
        .at[place_at]
        .set(owners % balance, mode="drop")
    )
    return (place_at, row_table.reshape(groups, capacity))


def pack_values(values, place_at, groups):
    capacity = values.shape[0] // groups
    buffer = (
        jnp.zeros((groups * capacity, values.shape[1]), values.dtype)
        .at[place_at]
        .set(values, mode="drop")
    )
    return buffer.reshape(groups, capacity, values.shape[1])


def place_rows(received, row_table, balance):
    feature = received.shape[-1]
    flat = received.reshape(-1, feature)
    return (
        jnp.zeros((balance, feature), received.dtype)
        .at[row_table.reshape(-1)]
        .set(flat, mode="drop")
    )


def pick_rows(table, row_table):
    balance = table.shape[0]
    flat = row_table.reshape(-1)
    taken = jnp.take(table, jnp.clip(flat, 0, balance - 1), axis=0)
    taken = jnp.where((flat < balance)[:, None], taken, jnp.zeros_like(taken))
    return taken.reshape(row_table.shape[0], row_table.shape[1], table.shape[1])


def unpack_rows(received, place_at, live_mask):
    feature = received.shape[-1]
    flat = received.reshape(-1, feature)
    taken = jnp.take(flat, jnp.clip(place_at, 0, flat.shape[0] - 1), axis=0)
    return jnp.where(live_mask[:, None], taken, jnp.zeros_like(taken))


def body(
    node_feats,
    cotangent,
    fine_adjacency,
    fine_columns,
    pool_one,
    pool_one_columns,
    count_one,
    owner_one,
    adjacency_one,
    columns_one,
    pool_two,
    pool_two_columns,
    count_two,
    owner_two,
    adjacency_two,
    columns_two,
    weight_in,
    weight_out,
    biases,
):
    groups = lax.axis_size("grp")
    block_rows = fine_adjacency.shape[1]
    fine_rows, feature = node_feats.shape
    slots_one = owner_one.shape[0]
    balance_one = slots_one // 2
    slots_two = owner_two.shape[0]
    balance_two = slots_two // 2
    live_one = jnp.arange(slots_one) < count_one[0]
    live_two = jnp.arange(slots_two) < count_two[0]
    place_one, sent_one = pack_layout(owner_one, live_one, groups, balance_one)
    place_two, sent_two = pack_layout(owner_two, live_two, groups, balance_two)
    tables = lax.all_to_all(
        jnp.concatenate([sent_one, sent_two], axis=1), "grp", split_axis=0, concat_axis=0, tiled=True
    )
    rows_one, rows_two = tables[:, : sent_one.shape[1]], tables[:, sent_one.shape[1] :]

    before, after = halo_parts(node_feats, "grp", HALO)
    message0 = block_apply(fine_adjacency, fine_columns, (before, node_feats, after))
    result0, pre_act0, hidden0 = layer_forward(
        node_feats, message0, weight_in[0], weight_out[0], biases[0]
    )
    pooled_one = restrict(
        pool_one, pool_one_columns, jnp.concatenate([result0, cotangent], axis=1), live_one
    )
    got_one = lax.all_to_all(
        pack_values(pooled_one, place_one, groups), "grp", split_axis=0, concat_axis=0, tiled=True
    )
    placed_one = place_rows(got_one, rows_one, balance_one)
    own_one, grad_up_one = placed_one[:, :feature], placed_one[:, feature:]
    context_one = grp_gather(own_one)
    message_one = block_apply(adjacency_one, columns_one, context_one)
    result1, pre_act1, hidden1 = layer_forward(
        own_one, message_one, weight_in[1], weight_out[1], biases[1]
    )
    pooled_two = restrict(
        pool_two, pool_two_columns, jnp.concatenate([result1, grad_up_one], axis=1), live_two
    )
    got_two = lax.all_to_all(
        pack_values(pooled_two, place_two, groups), "grp", split_axis=0, concat_axis=0, tiled=True
    )
    placed_two = place_rows(got_two, rows_two, balance_two)
    own_two, grad_out_two = placed_two[:, :feature], placed_two[:, feature:]
    context_two = grp_gather(own_two)
    message_two = block_apply(adjacency_two, columns_two, context_two)
    result2, pre_act2, hidden2 = layer_forward(
        own_two, message_two, weight_in[2], weight_out[2], biases[2]
    )
    sums_two, grad_rows_two, grad_ctx_two = layer_backward(
        grad_out_two.astype(jnp.float32),
        own_two,
        message_two,
        hidden2,
        pre_act2,
        weight_in[2],
        weight_out[2],
        adjacency_two,
        columns_two,
        groups * balance_two // block_rows,
    )
    grad_own_two = grad_rows_two + grp_sum_scatter(grad_ctx_two)
    returned_two = lax.all_to_all(
        pick_rows(jnp.concatenate([result2, grad_own_two.astype(jnp.bfloat16)], axis=1), rows_two),
        "grp",
        split_axis=0,
        concat_axis=0,
        tiled=True,
    )
    back_two = unpack_rows(returned_two, place_two, live_two)
    lifted_one = block_transpose(pool_two, pool_two_columns, back_two, balance_one // block_rows)
    up_one = (result1.astype(jnp.float32) + lifted_one[:, :feature]).astype(jnp.bfloat16)
    grad_out_one = grad_up_one.astype(jnp.float32) + lifted_one[:, feature:]
    sums_one, grad_rows_one, grad_ctx_one = layer_backward(
        grad_out_one,
        own_one,
        message_one,
        hidden1,
        pre_act1,
        weight_in[1],
        weight_out[1],
        adjacency_one,
        columns_one,
        groups * balance_one // block_rows,
    )
    grad_own_one = grad_rows_one + grp_sum_scatter(grad_ctx_one)
    returned_one = lax.all_to_all(
        pick_rows(jnp.concatenate([up_one, grad_own_one.astype(jnp.bfloat16)], axis=1), rows_one),
        "grp",
        split_axis=0,
        concat_axis=0,
        tiled=True,
    )
    back_one = unpack_rows(returned_one, place_one, live_one)
    lifted_zero = block_transpose(pool_one, pool_one_columns, back_one, fine_rows // block_rows)
    node_out = (result0.astype(jnp.float32) + lifted_zero[:, :feature]).astype(jnp.bfloat16)
    grad_out_zero = cotangent.astype(jnp.float32) + lifted_zero[:, feature:]
    sums_zero, grad_rows_zero, grad_ctx_zero = layer_backward(
        grad_out_zero,
        node_feats,
        message0,
        hidden0,
        pre_act0,
        weight_in[0],
        weight_out[0],
        fine_adjacency,
        fine_columns,
        (fine_rows + 2 * HALO) // block_rows,
    )
    rim_terms = jnp.concatenate([grad_ctx_zero[:HALO], grad_ctx_zero[HALO + fine_rows :]], axis=0)
    neighbour_terms = with_halo(rim_terms.astype(jnp.bfloat16), (("grp", 0),), HALO).astype(
        rim_terms.dtype
    )
    gathered_total = grad_rows_zero + grad_ctx_zero[HALO : HALO + fine_rows]
    gathered_total = gathered_total.at[:HALO].add(neighbour_terms[:HALO])
    gathered_total = gathered_total.at[fine_rows - HALO :].add(neighbour_terms[3 * HALO :])
    grad_feats = gathered_total.astype(jnp.bfloat16)
    stack_in = jnp.stack([sums_zero[0], sums_one[0], sums_two[0]])
    stack_out = jnp.stack([sums_zero[1], sums_one[1], sums_two[1]])
    stack_bias = jnp.stack([sums_zero[2], sums_one[2], sums_two[2]])
    stack_in, stack_out, stack_bias = all_sum((stack_in, stack_out, stack_bias))
    inv_root = 1.0 / math.sqrt(fine_rows * groups * lax.axis_size("slab"))
    return (node_out, grad_feats, stack_in * inv_root, stack_out * inv_root, stack_bias * inv_root)


def solution(mesh):
    placed = (
        P(("slab", "grp"), None),
        P(("slab", "grp"), None),
        P(("slab", "grp"), None, None),
        P(("slab", "grp"), None),
        P(("slab", "grp"), None, None),
        P(("slab", "grp"), None),
        P(("slab", "grp")),
        P(("slab", "grp")),
        P(("slab", "grp"), None, None),
        P(("slab", "grp"), None),
        P(("slab", "grp"), None, None),
        P(("slab", "grp"), None),
        P(("slab", "grp")),
        P(("slab", "grp")),
        P(("slab", "grp"), None, None),
        P(("slab", "grp"), None),
        P(),
        P(),
        P(),
    )
    return jax.shard_map(
        body,
        mesh=mesh,
        in_specs=placed,
        out_specs=(P(("slab", "grp"), None), P(("slab", "grp"), None), P(), P(), P()),
        check_vma=False,
    )
```

```python
import functools
import math

import jax
import jax.numpy as jnp
from jax import lax
from jax.experimental import pallas as pl
from jax.experimental.pallas import tpu as pltpu
from jax.sharding import PartitionSpec as P

HALO = 512


def with_halo(cells, sides, width):
    for axis, dim in sides:
        count = lax.axis_size(axis)
        ends = count - 1
        head = lax.slice_in_dim(cells, 0, width, axis=dim)
        tail = lax.slice_in_dim(cells, cells.shape[dim] - width, cells.shape[dim], axis=dim)
        cells = jnp.concatenate(
            [
                lax.ppermute(tail, axis, [(i, (i + 1) % count) for i in range(ends)]),
                cells,
                lax.ppermute(head, axis, [((i + 1) % count, i) for i in range(ends)]),
            ],
            axis=dim,
        )
    return cells


def halo_parts(cells, axis, width):
    count = lax.axis_size(axis)
    ends = count - 1
    head = cells[:width]
    tail = cells[cells.shape[0] - width :]
    before = lax.ppermute(tail, axis, [(i, (i + 1) % count) for i in range(ends)])
    after = lax.ppermute(head, axis, [((i + 1) % count, i) for i in range(ends)])
    return before, after


def _per_step(block_count):
    return min(block_count, 8)


def _apply_kernel(cols_ref, m_ref, *refs, k, per_step, blk, pieces_in):
    q_parts, (o_ref, q_ref) = refs[:pieces_in], refs[pieces_in:]
    step = pl.program_id(0)

    @pl.when(step == 0)
    def _():
        at = 0
        for part in q_parts:
            q_ref[at : at + part.shape[0], :] = part[...]
            at += part.shape[0]

    for j in range(per_step):
        r = step * per_step + j
        pieces = [
            q_ref[pl.ds(pl.multiple_of(cols_ref[r * k + i] * blk, blk), blk), :] for i in range(k)
        ]
        stacked = jnp.concatenate(pieces, axis=0)
        res = jnp.dot(m_ref[j], stacked, preferred_element_type=jnp.float32)
        o_ref[j * blk : (j + 1) * blk, :] = res.astype(o_ref.dtype)


def block_apply(blocks, columns, context, out_dtype=jnp.bfloat16):
    block_count, block_rows, span = blocks.shape
    k = columns.shape[1]
    parts = tuple(context) if isinstance(context, (tuple, list)) else (context,)
    feature = parts[0].shape[1]
    rows = sum(p.shape[0] for p in parts)
    per_step = _per_step(block_count)
    kernel = functools.partial(
        _apply_kernel, k=k, per_step=per_step, blk=block_rows, pieces_in=len(parts)
    )
    return pl.pallas_call(
        kernel,
        out_shape=jax.ShapeDtypeStruct((block_count * block_rows, feature), out_dtype),
        grid_spec=pltpu.PrefetchScalarGridSpec(
            num_scalar_prefetch=1,
            grid=(block_count // per_step,),
            in_specs=[pl.BlockSpec((per_step, block_rows, span), lambda s, c: (s, 0, 0))]
            + [pl.BlockSpec(p.shape, lambda s, c: (0, 0)) for p in parts],
            out_specs=pl.BlockSpec((per_step * block_rows, feature), lambda s, c: (s, 0)),
            scratch_shapes=[pltpu.VMEM((rows, feature), parts[0].dtype)],
        ),
        compiler_params=pltpu.CompilerParams(dimension_semantics=("arbitrary",)),
        cost_estimate=pl.CostEstimate(
            flops=2 * block_count * block_rows * span * feature,
            transcendentals=0,
            bytes_accessed=blocks.size * 2 + rows * feature * 2 + block_count * block_rows * feature * 2,
        ),
    )(columns.reshape(-1), blocks, *parts)


def _apply_t_kernel(cols_ref, m_ref, p_ref, o_ref, *, k, per_step, blk):
    step = pl.program_id(0)

    @pl.when(step == 0)
    def _():
        o_ref[...] = jnp.zeros_like(o_ref)

    for j in range(per_step):
        r = step * per_step + j
        spread = lax.dot_general(
            m_ref[j],
            p_ref[j * blk : (j + 1) * blk, :],
            (((0,), (0,)), ((), ())),
            preferred_element_type=jnp.float32,
        )
        for i in range(k):
            at = pl.multiple_of(cols_ref[r * k + i] * blk, blk)
            o_ref[pl.ds(at, blk), :] += spread[i * blk : (i + 1) * blk]


def block_transpose(blocks, columns, row_grads, targets):
    block_count, block_rows, span = blocks.shape
    k = columns.shape[1]
    feature = row_grads.shape[1]
    per_step = _per_step(block_count)
    kernel = functools.partial(_apply_t_kernel, k=k, per_step=per_step, blk=block_rows)
    return pl.pallas_call(
        kernel,
        out_shape=jax.ShapeDtypeStruct((targets * block_rows, feature), jnp.float32),
        grid_spec=pltpu.PrefetchScalarGridSpec(
            num_scalar_prefetch=1,
            grid=(block_count // per_step,),
            in_specs=[
                pl.BlockSpec((per_step, block_rows, span), lambda s, c: (s, 0, 0)),
                pl.BlockSpec((per_step * block_rows, feature), lambda s, c: (s, 0)),
            ],
            out_specs=pl.BlockSpec((targets * block_rows, feature), lambda s, c: (0, 0)),
        ),
        compiler_params=pltpu.CompilerParams(dimension_semantics=("arbitrary",)),
        cost_estimate=pl.CostEstimate(
            flops=2 * block_count * block_rows * span * feature,
            transcendentals=0,
            bytes_accessed=blocks.size * 2 + row_grads.size * 2 + targets * block_rows * feature * 4,
        ),
    )(columns.reshape(-1), blocks, row_grads.astype(jnp.bfloat16))


def _exchange_kernel(x_ref, o_ref, send_sem, recv_sem, *, axis, n, broadcast):
    me = lax.axis_index(axis)
    barrier = pltpu.get_barrier_semaphore()
    for d in range(1, n):
        pl.semaphore_signal(
            barrier, inc=1, device_id={axis: lax.rem(me + d, n)}, device_id_type=pl.DeviceIdType.MESH
        )
    pl.semaphore_wait(barrier, n - 1)
    copies = []
    for d in range(1, n):
        peer = lax.rem(me + d, n)
        copy = pltpu.make_async_remote_copy(
            src_ref=x_ref if broadcast else x_ref.at[peer],
            dst_ref=o_ref.at[me],
            send_sem=send_sem.at[d],
            recv_sem=recv_sem.at[d],
            device_id={axis: peer},
            device_id_type=pl.DeviceIdType.MESH,
        )
        copy.start()
        copies.append(copy)
    o_ref[me] = x_ref[...] if broadcast else x_ref[me]
    for copy in copies:
        copy.wait()


def grp_exchange(chunks, site, broadcast=False):
    n = lax.axis_size("grp")
    shape = (n,) + chunks.shape if broadcast else chunks.shape
    kernel = functools.partial(_exchange_kernel, axis="grp", n=n, broadcast=broadcast)
    moved = chunks.size * chunks.dtype.itemsize * (n - 1 if broadcast else 1)
    return pl.pallas_call(
        kernel,
        out_shape=jax.ShapeDtypeStruct(shape, chunks.dtype),
        in_specs=[pl.BlockSpec(memory_space=pltpu.VMEM)],
        out_specs=pl.BlockSpec(memory_space=pltpu.VMEM),
        scratch_shapes=[pltpu.SemaphoreType.DMA((n,)), pltpu.SemaphoreType.DMA((n,))],
        compiler_params=pltpu.CompilerParams(collective_id=site, has_side_effects=True),
        cost_estimate=pl.CostEstimate(flops=0, transcendentals=0, bytes_accessed=2 * moved),
    )(chunks)


def grp_gather(rows, site):
    return grp_exchange(rows, site, broadcast=True).reshape(-1, rows.shape[1])


def grp_sum_scatter(values, site):
    groups = lax.axis_size("grp")
    pieces = values.astype(jnp.bfloat16).reshape(groups, -1, values.shape[1])
    got = grp_exchange(pieces, site)
    return jnp.sum(got.astype(jnp.float32), axis=0)


def all_sum(parts):
    axes = ("slab", "grp")
    devices = lax.axis_size("slab") * lax.axis_size("grp")
    flat = jnp.concatenate([p.reshape(-1) for p in parts])
    total = flat.shape[0]
    chunk = -(-total // devices)
    chunk = -(-chunk // 128) * 128
    flat = jnp.pad(flat, (0, devices * chunk - total)).reshape(devices, chunk)
    got = lax.all_to_all(flat, axes, 0, 0, tiled=True)
    mine = jnp.sum(got, axis=0, keepdims=True)
    back = lax.all_to_all(jnp.broadcast_to(mine, (devices, chunk)), axes, 0, 0, tiled=True)
    back = back.reshape(-1)[:total]
    out, at = [], 0
    for p in parts:
        out.append(back[at : at + p.size].reshape(p.shape))
        at += p.size
    return out


def restrict(blocks, columns, source, live_mask):
    pooled = block_apply(blocks, columns, source)
    return jnp.where(live_mask[:, None], pooled, jnp.zeros_like(pooled))


def layer_forward(node_rows, message, weight_in, weight_out, bias_row):
    joined = jnp.concatenate([node_rows, message], axis=1)
    pre_act = jnp.dot(joined, weight_in, preferred_element_type=jnp.float32) + bias_row
    hidden = jax.nn.silu(pre_act).astype(jnp.bfloat16)
    result = node_rows.astype(jnp.float32) + jnp.dot(
        hidden, weight_out, preferred_element_type=jnp.float32
    )
    return (result.astype(jnp.bfloat16), pre_act, hidden)


def layer_backward(
    cotan_rows, node_rows, message, hidden, pre_act, weight_in, weight_out, blocks, columns, targets
):
    grad_low = cotan_rows.astype(jnp.bfloat16)
    delta_out = lax.dot_general(
        hidden, grad_low, (((0,), (0,)), ((), ())), preferred_element_type=jnp.float32
    )
    grad_hidden = lax.dot_general(
        grad_low, weight_out, (((1,), (1,)), ((), ())), preferred_element_type=jnp.float32
    )
    sigmoid_pre = jax.nn.sigmoid(pre_act)
    grad_pre = grad_hidden * sigmoid_pre * (1.0 + pre_act * (1.0 - sigmoid_pre))
    grad_pre_low = grad_pre.astype(jnp.bfloat16)
    delta_bias = jnp.sum(grad_pre, axis=0)
    joined = jnp.concatenate([node_rows, message], axis=1)
    delta_in = lax.dot_general(
        joined, grad_pre_low, (((0,), (0,)), ((), ())), preferred_element_type=jnp.float32
    )
    grad_joined = lax.dot_general(
        grad_pre_low, weight_in, (((1,), (1,)), ((), ())), preferred_element_type=jnp.float32
    )
    feature = node_rows.shape[1]
    grad_rows = cotan_rows + grad_joined[:, :feature]
    grad_message = grad_joined[:, feature:].astype(jnp.bfloat16)
    grad_context = block_transpose(blocks, columns, grad_message, targets)
    return ((delta_in, delta_out, delta_bias), grad_rows, grad_context)


def pack_layout(owners, live_mask, groups, balance):
    slot_count = owners.shape[0]
    capacity = slot_count // groups
    target = owners // balance
    onehot = (
        (target[:, None] == jnp.arange(groups, dtype=jnp.int32)[None, :]) & live_mask[:, None]
    ).astype(jnp.int32)
    slot_ranks = jnp.sum(onehot * jnp.cumsum(onehot, axis=0), axis=1) - 1
    place_at = jnp.where(live_mask, target * capacity + slot_ranks, groups * capacity)
    row_table = (
        jnp.full((groups * capacity,), balance, jnp.int32)
        .at[place_at]
        .set(owners % balance, mode="drop")
    )
    return (place_at, row_table.reshape(groups, capacity))


def pack_values(values, place_at, groups):
    capacity = values.shape[0] // groups
    buffer = (
        jnp.zeros((groups * capacity, values.shape[1]), values.dtype)
        .at[place_at]
        .set(values, mode="drop")
    )
    return buffer.reshape(groups, capacity, values.shape[1])


def place_rows(received, row_table, balance):
    feature = received.shape[-1]
    flat = received.reshape(-1, feature)
    return (
        jnp.zeros((balance, feature), received.dtype)
        .at[row_table.reshape(-1)]
        .set(flat, mode="drop")
    )


def pick_rows(table, row_table):
    balance = table.shape[0]
    flat = row_table.reshape(-1)
    taken = jnp.take(table, jnp.clip(flat, 0, balance - 1), axis=0)
    taken = jnp.where((flat < balance)[:, None], taken, jnp.zeros_like(taken))
    return taken.reshape(row_table.shape[0], row_table.shape[1], table.shape[1])


def unpack_rows(received, place_at, live_mask):
    feature = received.shape[-1]
    flat = received.reshape(-1, feature)
    taken = jnp.take(flat, jnp.clip(place_at, 0, flat.shape[0] - 1), axis=0)
    return jnp.where(live_mask[:, None], taken, jnp.zeros_like(taken))


def body(
    node_feats,
    cotangent,
    fine_adjacency,
    fine_columns,
    pool_one,
    pool_one_columns,
    count_one,
    owner_one,
    adjacency_one,
    columns_one,
    pool_two,
    pool_two_columns,
    count_two,
    owner_two,
    adjacency_two,
    columns_two,
    weight_in,
    weight_out,
    biases,
):
    groups = lax.axis_size("grp")
    block_rows = fine_adjacency.shape[1]
    fine_rows, feature = node_feats.shape
    slots_one = owner_one.shape[0]
    balance_one = slots_one // 2
    slots_two = owner_two.shape[0]
    balance_two = slots_two // 2
    live_one = jnp.arange(slots_one) < count_one[0]
    live_two = jnp.arange(slots_two) < count_two[0]
    place_one, sent_one = pack_layout(owner_one, live_one, groups, balance_one)
    place_two, sent_two = pack_layout(owner_two, live_two, groups, balance_two)
    tables = lax.all_to_all(
        jnp.concatenate([sent_one, sent_two], axis=1), "grp", split_axis=0, concat_axis=0, tiled=True
    )
    rows_one, rows_two = tables[:, : sent_one.shape[1]], tables[:, sent_one.shape[1] :]

    before, after = halo_parts(node_feats, "grp", HALO)
    message0 = block_apply(fine_adjacency, fine_columns, (before, node_feats, after))
    result0, pre_act0, hidden0 = layer_forward(
        node_feats, message0, weight_in[0], weight_out[0], biases[0]
    )
    pooled_one = restrict(
        pool_one, pool_one_columns, jnp.concatenate([result0, cotangent], axis=1), live_one
    )
    got_one = grp_exchange(pack_values(pooled_one, place_one, groups), 0)
    placed_one = place_rows(got_one, rows_one, balance_one)
    own_one, grad_up_one = placed_one[:, :feature], placed_one[:, feature:]
    context_one = grp_gather(own_one, 1)
    message_one = block_apply(adjacency_one, columns_one, context_one)
    result1, pre_act1, hidden1 = layer_forward(
        own_one, message_one, weight_in[1], weight_out[1], biases[1]
    )
    pooled_two = restrict(
        pool_two, pool_two_columns, jnp.concatenate([result1, grad_up_one], axis=1), live_two
    )
    got_two = grp_exchange(pack_values(pooled_two, place_two, groups), 2)
    placed_two = place_rows(got_two, rows_two, balance_two)
    own_two, grad_out_two = placed_two[:, :feature], placed_two[:, feature:]
    context_two = grp_gather(own_two, 3)
    message_two = block_apply(adjacency_two, columns_two, context_two)
    result2, pre_act2, hidden2 = layer_forward(
        own_two, message_two, weight_in[2], weight_out[2], biases[2]
    )
    sums_two, grad_rows_two, grad_ctx_two = layer_backward(
        grad_out_two.astype(jnp.float32),
        own_two,
        message_two,
        hidden2,
        pre_act2,
        weight_in[2],
        weight_out[2],
        adjacency_two,
        columns_two,
        groups * balance_two // block_rows,
    )
    grad_own_two = grad_rows_two + grp_sum_scatter(grad_ctx_two, 4)
    returned_two = grp_exchange(
        pick_rows(jnp.concatenate([result2, grad_own_two.astype(jnp.bfloat16)], axis=1), rows_two), 5
    )
    back_two = unpack_rows(returned_two, place_two, live_two)
    lifted_one = block_transpose(pool_two, pool_two_columns, back_two, balance_one // block_rows)
    up_one = (result1.astype(jnp.float32) + lifted_one[:, :feature]).astype(jnp.bfloat16)
    grad_out_one = grad_up_one.astype(jnp.float32) + lifted_one[:, feature:]
    sums_one, grad_rows_one, grad_ctx_one = layer_backward(
        grad_out_one,
        own_one,
        message_one,
        hidden1,
        pre_act1,
        weight_in[1],
        weight_out[1],
        adjacency_one,
        columns_one,
        groups * balance_one // block_rows,
    )
    grad_own_one = grad_rows_one + grp_sum_scatter(grad_ctx_one, 6)
    returned_one = grp_exchange(
        pick_rows(jnp.concatenate([up_one, grad_own_one.astype(jnp.bfloat16)], axis=1), rows_one), 7
    )
    back_one = unpack_rows(returned_one, place_one, live_one)
    lifted_zero = block_transpose(pool_one, pool_one_columns, back_one, fine_rows // block_rows)
    node_out = (result0.astype(jnp.float32) + lifted_zero[:, :feature]).astype(jnp.bfloat16)
    grad_out_zero = cotangent.astype(jnp.float32) + lifted_zero[:, feature:]
    sums_zero, grad_rows_zero, grad_ctx_zero = layer_backward(
        grad_out_zero,
        node_feats,
        message0,
        hidden0,
        pre_act0,
        weight_in[0],
        weight_out[0],
        fine_adjacency,
        fine_columns,
        (fine_rows + 2 * HALO) // block_rows,
    )
    rim_terms = jnp.concatenate([grad_ctx_zero[:HALO], grad_ctx_zero[HALO + fine_rows :]], axis=0)
    neighbour_terms = with_halo(rim_terms.astype(jnp.bfloat16), (("grp", 0),), HALO).astype(
        rim_terms.dtype
    )
    gathered_total = grad_rows_zero + grad_ctx_zero[HALO : HALO + fine_rows]
    gathered_total = gathered_total.at[:HALO].add(neighbour_terms[:HALO])
    gathered_total = gathered_total.at[fine_rows - HALO :].add(neighbour_terms[3 * HALO :])
    grad_feats = gathered_total.astype(jnp.bfloat16)
    stack_in = jnp.stack([sums_zero[0], sums_one[0], sums_two[0]])
    stack_out = jnp.stack([sums_zero[1], sums_one[1], sums_two[1]])
    stack_bias = jnp.stack([sums_zero[2], sums_one[2], sums_two[2]])
    stack_in, stack_out, stack_bias = all_sum((stack_in, stack_out, stack_bias))
    inv_root = 1.0 / math.sqrt(fine_rows * groups * lax.axis_size("slab"))
    return (node_out, grad_feats, stack_in * inv_root, stack_out * inv_root, stack_bias * inv_root)


def solution(mesh):
    placed = (
        P(("slab", "grp"), None),
        P(("slab", "grp"), None),
        P(("slab", "grp"), None, None),
        P(("slab", "grp"), None),
        P(("slab", "grp"), None, None),
        P(("slab", "grp"), None),
        P(("slab", "grp")),
        P(("slab", "grp")),
        P(("slab", "grp"), None, None),
        P(("slab", "grp"), None),
        P(("slab", "grp"), None, None),
        P(("slab", "grp"), None),
        P(("slab", "grp")),
        P(("slab", "grp")),
        P(("slab", "grp"), None, None),
        P(("slab", "grp"), None),
        P(),
        P(),
        P(),
    )
    return jax.shard_map(
        body,
        mesh=mesh,
        in_specs=placed,
        out_specs=(P(("slab", "grp"), None), P(("slab", "grp"), None), P(), P(), P()),
        check_vma=False,
    )
```

```python
import functools
import math

import jax
import jax.numpy as jnp
from jax import lax
from jax.experimental import pallas as pl
from jax.experimental.pallas import tpu as pltpu
from jax.sharding import PartitionSpec as P

HALO = 512


def with_halo(cells, sides, width):
    for axis, dim in sides:
        count = lax.axis_size(axis)
        ends = count - 1
        head = lax.slice_in_dim(cells, 0, width, axis=dim)
        tail = lax.slice_in_dim(cells, cells.shape[dim] - width, cells.shape[dim], axis=dim)
        cells = jnp.concatenate(
            [
                lax.ppermute(tail, axis, [(i, (i + 1) % count) for i in range(ends)]),
                cells,
                lax.ppermute(head, axis, [((i + 1) % count, i) for i in range(ends)]),
            ],
            axis=dim,
        )
    return cells


def halo_parts(cells, axis, width):
    count = lax.axis_size(axis)
    ends = count - 1
    head = cells[:width]
    tail = cells[cells.shape[0] - width :]
    before = lax.ppermute(tail, axis, [(i, (i + 1) % count) for i in range(ends)])
    after = lax.ppermute(head, axis, [((i + 1) % count, i) for i in range(ends)])
    return before, after


def _per_step(block_count):
    return min(block_count, 8)


def _apply_kernel(cols_ref, m_ref, *refs, k, per_step, blk, pieces_in):
    q_parts, (o_ref, q_ref) = refs[:pieces_in], refs[pieces_in:]
    step = pl.program_id(0)

    @pl.when(step == 0)
    def _():
        at = 0
        for part in q_parts:
            q_ref[at : at + part.shape[0], :] = part[...]
            at += part.shape[0]

    for j in range(per_step):
        r = step * per_step + j
        pieces = [
            q_ref[pl.ds(pl.multiple_of(cols_ref[r * k + i] * blk, blk), blk), :] for i in range(k)
        ]
        stacked = jnp.concatenate(pieces, axis=0)
        res = jnp.dot(m_ref[j], stacked, preferred_element_type=jnp.float32)
        o_ref[j * blk : (j + 1) * blk, :] = res.astype(o_ref.dtype)


def block_apply(blocks, columns, context, out_dtype=jnp.bfloat16):
    block_count, block_rows, span = blocks.shape
    k = columns.shape[1]
    parts = tuple(context) if isinstance(context, (tuple, list)) else (context,)
    feature = parts[0].shape[1]
    rows = sum(p.shape[0] for p in parts)
    per_step = _per_step(block_count)
    kernel = functools.partial(
        _apply_kernel, k=k, per_step=per_step, blk=block_rows, pieces_in=len(parts)
    )
    return pl.pallas_call(
        kernel,
        out_shape=jax.ShapeDtypeStruct((block_count * block_rows, feature), out_dtype),
        grid_spec=pltpu.PrefetchScalarGridSpec(
            num_scalar_prefetch=1,
            grid=(block_count // per_step,),
            in_specs=[pl.BlockSpec((per_step, block_rows, span), lambda s, c: (s, 0, 0))]
            + [pl.BlockSpec(p.shape, lambda s, c: (0, 0)) for p in parts],
            out_specs=pl.BlockSpec((per_step * block_rows, feature), lambda s, c: (s, 0)),
            scratch_shapes=[pltpu.VMEM((rows, feature), parts[0].dtype)],
        ),
        compiler_params=pltpu.CompilerParams(dimension_semantics=("arbitrary",)),
        cost_estimate=pl.CostEstimate(
            flops=2 * block_count * block_rows * span * feature,
            transcendentals=0,
            bytes_accessed=blocks.size * 2 + rows * feature * 2 + block_count * block_rows * feature * 2,
        ),
    )(columns.reshape(-1), blocks, *parts)


def _apply_t_kernel(cols_ref, m_ref, p_ref, o_ref, *, k, per_step, blk):
    step = pl.program_id(0)

    @pl.when(step == 0)
    def _():
        o_ref[...] = jnp.zeros_like(o_ref)

    for j in range(per_step):
        r = step * per_step + j
        spread = lax.dot_general(
            m_ref[j],
            p_ref[j * blk : (j + 1) * blk, :],
            (((0,), (0,)), ((), ())),
            preferred_element_type=jnp.float32,
        )
        for i in range(k):
            at = pl.multiple_of(cols_ref[r * k + i] * blk, blk)
            o_ref[pl.ds(at, blk), :] += spread[i * blk : (i + 1) * blk]


def block_transpose(blocks, columns, row_grads, targets):
    block_count, block_rows, span = blocks.shape
    k = columns.shape[1]
    feature = row_grads.shape[1]
    per_step = _per_step(block_count)
    kernel = functools.partial(_apply_t_kernel, k=k, per_step=per_step, blk=block_rows)
    return pl.pallas_call(
        kernel,
        out_shape=jax.ShapeDtypeStruct((targets * block_rows, feature), jnp.float32),
        grid_spec=pltpu.PrefetchScalarGridSpec(
            num_scalar_prefetch=1,
            grid=(block_count // per_step,),
            in_specs=[
                pl.BlockSpec((per_step, block_rows, span), lambda s, c: (s, 0, 0)),
                pl.BlockSpec((per_step * block_rows, feature), lambda s, c: (s, 0)),
            ],
            out_specs=pl.BlockSpec((targets * block_rows, feature), lambda s, c: (0, 0)),
        ),
        compiler_params=pltpu.CompilerParams(dimension_semantics=("arbitrary",)),
        cost_estimate=pl.CostEstimate(
            flops=2 * block_count * block_rows * span * feature,
            transcendentals=0,
            bytes_accessed=blocks.size * 2 + row_grads.size * 2 + targets * block_rows * feature * 4,
        ),
    )(columns.reshape(-1), blocks, row_grads.astype(jnp.bfloat16))


def _exchange_kernel(x_ref, o_ref, send_sem, recv_sem, *, axis, n, broadcast):
    me = lax.axis_index(axis)
    barrier = pltpu.get_barrier_semaphore()
    for d in range(1, n):
        pl.semaphore_signal(
            barrier, inc=1, device_id={axis: lax.rem(me + d, n)}, device_id_type=pl.DeviceIdType.MESH
        )
    pl.semaphore_wait(barrier, n - 1)
    copies = []
    for d in range(1, n):
        peer = lax.rem(me + d, n)
        copy = pltpu.make_async_remote_copy(
            src_ref=x_ref if broadcast else x_ref.at[peer],
            dst_ref=o_ref.at[me],
            send_sem=send_sem.at[d],
            recv_sem=recv_sem.at[d],
            device_id={axis: peer},
            device_id_type=pl.DeviceIdType.MESH,
        )
        copy.start()
        copies.append(copy)
    o_ref[me] = x_ref[...] if broadcast else x_ref[me]
    for copy in copies:
        copy.wait()


def grp_exchange(chunks, site, broadcast=False):
    n = lax.axis_size("grp")
    shape = (n,) + chunks.shape if broadcast else chunks.shape
    kernel = functools.partial(_exchange_kernel, axis="grp", n=n, broadcast=broadcast)
    moved = chunks.size * chunks.dtype.itemsize * (n - 1 if broadcast else 1)
    return pl.pallas_call(
        kernel,
        out_shape=jax.ShapeDtypeStruct(shape, chunks.dtype),
        in_specs=[pl.BlockSpec(memory_space=pltpu.VMEM)],
        out_specs=pl.BlockSpec(memory_space=pltpu.VMEM),
        scratch_shapes=[pltpu.SemaphoreType.DMA((n,)), pltpu.SemaphoreType.DMA((n,))],
        compiler_params=pltpu.CompilerParams(collective_id=site, has_side_effects=True),
        cost_estimate=pl.CostEstimate(flops=0, transcendentals=0, bytes_accessed=2 * moved),
    )(chunks)


def grp_gather(rows, site):
    return grp_exchange(rows, site, broadcast=True).reshape(-1, rows.shape[1])


def grp_sum_scatter(values, site):
    groups = lax.axis_size("grp")
    pieces = values.astype(jnp.bfloat16).reshape(groups, -1, values.shape[1])
    got = grp_exchange(pieces, site)
    return jnp.sum(got.astype(jnp.float32), axis=0)


def all_sum(parts):
    axes = ("slab", "grp")
    devices = lax.axis_size("slab") * lax.axis_size("grp")
    flat = jnp.concatenate([p.reshape(-1) for p in parts])
    total = flat.shape[0]
    chunk = -(-total // devices)
    chunk = -(-chunk // 128) * 128
    flat = jnp.pad(flat, (0, devices * chunk - total)).reshape(devices, chunk)
    got = lax.all_to_all(flat, axes, 0, 0, tiled=True)
    mine = jnp.sum(got, axis=0, keepdims=True)
    back = lax.all_to_all(jnp.broadcast_to(mine, (devices, chunk)), axes, 0, 0, tiled=True)
    back = back.reshape(-1)[:total]
    out, at = [], 0
    for p in parts:
        out.append(back[at : at + p.size].reshape(p.shape))
        at += p.size
    return out


def restrict(blocks, columns, source, live_mask):
    pooled = block_apply(blocks, columns, source)
    return jnp.where(live_mask[:, None], pooled, jnp.zeros_like(pooled))


def layer_forward(node_rows, message, weight_in, weight_out, bias_row):
    joined = jnp.concatenate([node_rows, message], axis=1)
    pre_act = jnp.dot(joined, weight_in, preferred_element_type=jnp.float32) + bias_row
    hidden = jax.nn.silu(pre_act).astype(jnp.bfloat16)
    result = node_rows.astype(jnp.float32) + jnp.dot(
        hidden, weight_out, preferred_element_type=jnp.float32
    )
    return (result.astype(jnp.bfloat16), pre_act, hidden)


def layer_backward(
    cotan_rows, node_rows, message, hidden, pre_act, weight_in, weight_out, blocks, columns, targets
):
    grad_low = cotan_rows.astype(jnp.bfloat16)
    delta_out = lax.dot_general(
        hidden, grad_low, (((0,), (0,)), ((), ())), preferred_element_type=jnp.float32
    )
    grad_hidden = lax.dot_general(
        grad_low, weight_out, (((1,), (1,)), ((), ())), preferred_element_type=jnp.float32
    )
    sigmoid_pre = jax.nn.sigmoid(pre_act)
    grad_pre = grad_hidden * sigmoid_pre * (1.0 + pre_act * (1.0 - sigmoid_pre))
    grad_pre_low = grad_pre.astype(jnp.bfloat16)
    delta_bias = jnp.sum(grad_pre, axis=0)
    joined = jnp.concatenate([node_rows, message], axis=1)
    delta_in = lax.dot_general(
        joined, grad_pre_low, (((0,), (0,)), ((), ())), preferred_element_type=jnp.float32
    )
    grad_joined = lax.dot_general(
        grad_pre_low, weight_in, (((1,), (1,)), ((), ())), preferred_element_type=jnp.float32
    )
    feature = node_rows.shape[1]
    grad_rows = cotan_rows + grad_joined[:, :feature]
    grad_message = grad_joined[:, feature:].astype(jnp.bfloat16)
    grad_context = block_transpose(blocks, columns, grad_message, targets)
    return ((delta_in, delta_out, delta_bias), grad_rows, grad_context)


def pack_layout(owners, live_mask, groups, balance):
    slot_count = owners.shape[0]
    capacity = slot_count // groups
    target = owners // balance
    onehot = (
        (target[:, None] == jnp.arange(groups, dtype=jnp.int32)[None, :]) & live_mask[:, None]
    ).astype(jnp.int32)
    slot_ranks = jnp.sum(onehot * jnp.cumsum(onehot, axis=0), axis=1) - 1
    place_at = jnp.where(live_mask, target * capacity + slot_ranks, groups * capacity)
    row_table = (
        jnp.full((groups * capacity,), balance, jnp.int32)
        .at[place_at]
        .set(owners % balance, mode="drop")
    )
    return (place_at, row_table.reshape(groups, capacity))


def inverse_slots(place_at, groups):
    slot_count = place_at.shape[0]
    return (
        jnp.full((slot_count,), slot_count, jnp.int32)
        .at[place_at]
        .set(jnp.arange(slot_count, dtype=jnp.int32), mode="drop")
        .reshape(groups, slot_count // groups)
    )


def pack_values(values, source_of):
    taken = jnp.take(values, jnp.clip(source_of.reshape(-1), 0, values.shape[0] - 1), axis=0)
    return taken.reshape(source_of.shape + (values.shape[1],))


def inverse_rows(row_table, balance):
    flat = row_table.reshape(-1)
    return (
        jnp.full((balance,), flat.shape[0], jnp.int32)
        .at[flat]
        .set(jnp.arange(flat.shape[0], dtype=jnp.int32), mode="drop")
    )


def place_rows(received, position_of):
    flat = received.reshape(-1, received.shape[-1])
    taken = jnp.take(flat, jnp.clip(position_of, 0, flat.shape[0] - 1), axis=0)
    return jnp.where((position_of < flat.shape[0])[:, None], taken, jnp.zeros_like(taken))


def pick_rows(table, row_table):
    balance = table.shape[0]
    flat = row_table.reshape(-1)
    taken = jnp.take(table, jnp.clip(flat, 0, balance - 1), axis=0)
    taken = jnp.where((flat < balance)[:, None], taken, jnp.zeros_like(taken))
    return taken.reshape(row_table.shape[0], row_table.shape[1], table.shape[1])


def unpack_rows(received, place_at, live_mask):
    feature = received.shape[-1]
    flat = received.reshape(-1, feature)
    taken = jnp.take(flat, jnp.clip(place_at, 0, flat.shape[0] - 1), axis=0)
    return jnp.where(live_mask[:, None], taken, jnp.zeros_like(taken))


def body(
    node_feats,
    cotangent,
    fine_adjacency,
    fine_columns,
    pool_one,
    pool_one_columns,
    count_one,
    owner_one,
    adjacency_one,
    columns_one,
    pool_two,
    pool_two_columns,
    count_two,
    owner_two,
    adjacency_two,
    columns_two,
    weight_in,
    weight_out,
    biases,
):
    groups = lax.axis_size("grp")
    block_rows = fine_adjacency.shape[1]
    fine_rows, feature = node_feats.shape
    slots_one = owner_one.shape[0]
    balance_one = slots_one // 2
    slots_two = owner_two.shape[0]
    balance_two = slots_two // 2
    live_one = jnp.arange(slots_one) < count_one[0]
    live_two = jnp.arange(slots_two) < count_two[0]
    place_one, sent_one = pack_layout(owner_one, live_one, groups, balance_one)
    place_two, sent_two = pack_layout(owner_two, live_two, groups, balance_two)
    src_one = inverse_slots(place_one, groups)
    src_two = inverse_slots(place_two, groups)
    tables = lax.all_to_all(
        jnp.concatenate([sent_one, sent_two], axis=1), "grp", split_axis=0, concat_axis=0, tiled=True
    )
    rows_one, rows_two = tables[:, : sent_one.shape[1]], tables[:, sent_one.shape[1] :]

    before, after = halo_parts(node_feats, "grp", HALO)
    message0 = block_apply(fine_adjacency, fine_columns, (before, node_feats, after))
    result0, pre_act0, hidden0 = layer_forward(
        node_feats, message0, weight_in[0], weight_out[0], biases[0]
    )
    pooled_one = restrict(
        pool_one, pool_one_columns, jnp.concatenate([result0, cotangent], axis=1), live_one
    )
    got_one = lax.all_to_all(
        pack_values(pooled_one, src_one), "grp", split_axis=0, concat_axis=0, tiled=True
    )
    placed_one = place_rows(got_one, inverse_rows(rows_one, balance_one))
    own_one, grad_up_one = placed_one[:, :feature], placed_one[:, feature:]
    context_one = lax.all_to_all(
        jnp.broadcast_to(own_one[None], (groups,) + own_one.shape), "grp", 0, 0, tiled=True
    ).reshape(-1, feature)
    message_one = block_apply(adjacency_one, columns_one, context_one)
    result1, pre_act1, hidden1 = layer_forward(
        own_one, message_one, weight_in[1], weight_out[1], biases[1]
    )
    pooled_two = restrict(
        pool_two, pool_two_columns, jnp.concatenate([result1, grad_up_one], axis=1), live_two
    )
    got_two = grp_exchange(pack_values(pooled_two, src_two), 2)
    placed_two = place_rows(got_two, inverse_rows(rows_two, balance_two))
    own_two, grad_out_two = placed_two[:, :feature], placed_two[:, feature:]
    context_two = grp_gather(own_two, 3)
    message_two = block_apply(adjacency_two, columns_two, context_two)
    result2, pre_act2, hidden2 = layer_forward(
        own_two, message_two, weight_in[2], weight_out[2], biases[2]
    )
    sums_two, grad_rows_two, grad_ctx_two = layer_backward(
        grad_out_two.astype(jnp.float32),
        own_two,
        message_two,
        hidden2,
        pre_act2,
        weight_in[2],
        weight_out[2],
        adjacency_two,
        columns_two,
        groups * balance_two // block_rows,
    )
    grad_own_two = grad_rows_two + grp_sum_scatter(grad_ctx_two, 4)
    returned_two = grp_exchange(
        pick_rows(jnp.concatenate([result2, grad_own_two.astype(jnp.bfloat16)], axis=1), rows_two), 5
    )
    back_two = unpack_rows(returned_two, place_two, live_two)
    lifted_one = block_transpose(pool_two, pool_two_columns, back_two, balance_one // block_rows)
    up_one = (result1.astype(jnp.float32) + lifted_one[:, :feature]).astype(jnp.bfloat16)
    grad_out_one = grad_up_one.astype(jnp.float32) + lifted_one[:, feature:]
    sums_one, grad_rows_one, grad_ctx_one = layer_backward(
        grad_out_one,
        own_one,
        message_one,
        hidden1,
        pre_act1,
        weight_in[1],
        weight_out[1],
        adjacency_one,
        columns_one,
        groups * balance_one // block_rows,
    )
    grad_own_one = grad_rows_one + grp_sum_scatter(grad_ctx_one, 6)
    returned_one = grp_exchange(
        pick_rows(jnp.concatenate([up_one, grad_own_one.astype(jnp.bfloat16)], axis=1), rows_one), 7
    )
    back_one = unpack_rows(returned_one, place_one, live_one)
    lifted_zero = block_transpose(pool_one, pool_one_columns, back_one, fine_rows // block_rows)
    node_out = (result0.astype(jnp.float32) + lifted_zero[:, :feature]).astype(jnp.bfloat16)
    grad_out_zero = cotangent.astype(jnp.float32) + lifted_zero[:, feature:]
    sums_zero, grad_rows_zero, grad_ctx_zero = layer_backward(
        grad_out_zero,
        node_feats,
        message0,
        hidden0,
        pre_act0,
        weight_in[0],
        weight_out[0],
        fine_adjacency,
        fine_columns,
        (fine_rows + 2 * HALO) // block_rows,
    )
    rim_terms = jnp.concatenate([grad_ctx_zero[:HALO], grad_ctx_zero[HALO + fine_rows :]], axis=0)
    neighbour_terms = with_halo(rim_terms.astype(jnp.bfloat16), (("grp", 0),), HALO).astype(
        rim_terms.dtype
    )
    gathered_total = grad_rows_zero + grad_ctx_zero[HALO : HALO + fine_rows]
    gathered_total = gathered_total.at[:HALO].add(neighbour_terms[:HALO])
    gathered_total = gathered_total.at[fine_rows - HALO :].add(neighbour_terms[3 * HALO :])
    grad_feats = gathered_total.astype(jnp.bfloat16)
    stack_in = jnp.stack([sums_zero[0], sums_one[0], sums_two[0]])
    stack_out = jnp.stack([sums_zero[1], sums_one[1], sums_two[1]])
    stack_bias = jnp.stack([sums_zero[2], sums_one[2], sums_two[2]])
    stack_in, stack_out, stack_bias = all_sum((stack_in, stack_out, stack_bias))
    inv_root = 1.0 / math.sqrt(fine_rows * groups * lax.axis_size("slab"))
    return (node_out, grad_feats, stack_in * inv_root, stack_out * inv_root, stack_bias * inv_root)


def solution(mesh):
    placed = (
        P(("slab", "grp"), None),
        P(("slab", "grp"), None),
        P(("slab", "grp"), None, None),
        P(("slab", "grp"), None),
        P(("slab", "grp"), None, None),
        P(("slab", "grp"), None),
        P(("slab", "grp")),
        P(("slab", "grp")),
        P(("slab", "grp"), None, None),
        P(("slab", "grp"), None),
        P(("slab", "grp"), None, None),
        P(("slab", "grp"), None),
        P(("slab", "grp")),
        P(("slab", "grp")),
        P(("slab", "grp"), None, None),
        P(("slab", "grp"), None),
        P(),
        P(),
        P(),
    )
    return jax.shard_map(
        body,
        mesh=mesh,
        in_specs=placed,
        out_specs=(P(("slab", "grp"), None), P(("slab", "grp"), None), P(), P(), P()),
        check_vma=False,
    )
```

```python
import functools
import math

import jax
import jax.numpy as jnp
from jax import lax
from jax.experimental import pallas as pl
from jax.experimental.pallas import tpu as pltpu
from jax.sharding import PartitionSpec as P

HALO = 512


def with_halo(cells, sides, width):
    for axis, dim in sides:
        count = lax.axis_size(axis)
        ends = count - 1
        head = lax.slice_in_dim(cells, 0, width, axis=dim)
        tail = lax.slice_in_dim(cells, cells.shape[dim] - width, cells.shape[dim], axis=dim)
        cells = jnp.concatenate(
            [
                lax.ppermute(tail, axis, [(i, (i + 1) % count) for i in range(ends)]),
                cells,
                lax.ppermute(head, axis, [((i + 1) % count, i) for i in range(ends)]),
            ],
            axis=dim,
        )
    return cells


def halo_parts(cells, axis, width):
    count = lax.axis_size(axis)
    ends = count - 1
    head = cells[:width]
    tail = cells[cells.shape[0] - width :]
    before = lax.ppermute(tail, axis, [(i, (i + 1) % count) for i in range(ends)])
    after = lax.ppermute(head, axis, [((i + 1) % count, i) for i in range(ends)])
    return before, after


def _per_step(block_count):
    return min(block_count, 8)


def _apply_kernel(cols_ref, m_ref, *refs, k, per_step, blk, pieces_in):
    q_parts, (o_ref, q_ref) = refs[:pieces_in], refs[pieces_in:]
    step = pl.program_id(0)

    @pl.when(step == 0)
    def _():
        at = 0
        for part in q_parts:
            q_ref[at : at + part.shape[0], :] = part[...]
            at += part.shape[0]

    for j in range(per_step):
        r = step * per_step + j
        pieces = [
            q_ref[pl.ds(pl.multiple_of(cols_ref[r * k + i] * blk, blk), blk), :] for i in range(k)
        ]
        stacked = jnp.concatenate(pieces, axis=0)
        res = jnp.dot(m_ref[j], stacked, preferred_element_type=jnp.float32)
        o_ref[j * blk : (j + 1) * blk, :] = res.astype(o_ref.dtype)


def block_apply(blocks, columns, context, out_dtype=jnp.bfloat16):
    block_count, block_rows, span = blocks.shape
    k = columns.shape[1]
    parts = tuple(context) if isinstance(context, (tuple, list)) else (context,)
    feature = parts[0].shape[1]
    rows = sum(p.shape[0] for p in parts)
    per_step = _per_step(block_count)
    kernel = functools.partial(
        _apply_kernel, k=k, per_step=per_step, blk=block_rows, pieces_in=len(parts)
    )
    return pl.pallas_call(
        kernel,
        out_shape=jax.ShapeDtypeStruct((block_count * block_rows, feature), out_dtype),
        grid_spec=pltpu.PrefetchScalarGridSpec(
            num_scalar_prefetch=1,
            grid=(block_count // per_step,),
            in_specs=[pl.BlockSpec((per_step, block_rows, span), lambda s, c: (s, 0, 0))]
            + [pl.BlockSpec(p.shape, lambda s, c: (0, 0)) for p in parts],
            out_specs=pl.BlockSpec((per_step * block_rows, feature), lambda s, c: (s, 0)),
            scratch_shapes=[pltpu.VMEM((rows, feature), parts[0].dtype)],
        ),
        compiler_params=pltpu.CompilerParams(dimension_semantics=("arbitrary",)),
        cost_estimate=pl.CostEstimate(
            flops=2 * block_count * block_rows * span * feature,
            transcendentals=0,
            bytes_accessed=blocks.size * 2 + rows * feature * 2 + block_count * block_rows * feature * 2,
        ),
    )(columns.reshape(-1), blocks, *parts)


def _apply_t_kernel(cols_ref, m_ref, p_ref, o_ref, *, k, per_step, blk):
    step = pl.program_id(0)

    @pl.when(step == 0)
    def _():
        o_ref[...] = jnp.zeros_like(o_ref)

    for j in range(per_step):
        r = step * per_step + j
        spread = lax.dot_general(
            m_ref[j],
            p_ref[j * blk : (j + 1) * blk, :],
            (((0,), (0,)), ((), ())),
            preferred_element_type=jnp.float32,
        )
        for i in range(k):
            at = pl.multiple_of(cols_ref[r * k + i] * blk, blk)
            o_ref[pl.ds(at, blk), :] += spread[i * blk : (i + 1) * blk]


def block_transpose(blocks, columns, row_grads, targets):
    block_count, block_rows, span = blocks.shape
    k = columns.shape[1]
    feature = row_grads.shape[1]
    per_step = _per_step(block_count)
    kernel = functools.partial(_apply_t_kernel, k=k, per_step=per_step, blk=block_rows)
    return pl.pallas_call(
        kernel,
        out_shape=jax.ShapeDtypeStruct((targets * block_rows, feature), jnp.float32),
        grid_spec=pltpu.PrefetchScalarGridSpec(
            num_scalar_prefetch=1,
            grid=(block_count // per_step,),
            in_specs=[
                pl.BlockSpec((per_step, block_rows, span), lambda s, c: (s, 0, 0)),
                pl.BlockSpec((per_step * block_rows, feature), lambda s, c: (s, 0)),
            ],
            out_specs=pl.BlockSpec((targets * block_rows, feature), lambda s, c: (0, 0)),
        ),
        compiler_params=pltpu.CompilerParams(dimension_semantics=("arbitrary",)),
        cost_estimate=pl.CostEstimate(
            flops=2 * block_count * block_rows * span * feature,
            transcendentals=0,
            bytes_accessed=blocks.size * 2 + row_grads.size * 2 + targets * block_rows * feature * 4,
        ),
    )(columns.reshape(-1), blocks, row_grads.astype(jnp.bfloat16))


def _exchange_kernel(x_ref, o_ref, send_sem, recv_sem, *, axis, n, broadcast):
    me = lax.axis_index(axis)
    barrier = pltpu.get_barrier_semaphore()
    for d in range(1, n):
        pl.semaphore_signal(
            barrier, inc=1, device_id={axis: lax.rem(me + d, n)}, device_id_type=pl.DeviceIdType.MESH
        )
    pl.semaphore_wait(barrier, n - 1)
    copies = []
    for d in range(1, n):
        peer = lax.rem(me + d, n)
        copy = pltpu.make_async_remote_copy(
            src_ref=x_ref if broadcast else x_ref.at[peer],
            dst_ref=o_ref.at[me],
            send_sem=send_sem.at[d],
            recv_sem=recv_sem.at[d],
            device_id={axis: peer},
            device_id_type=pl.DeviceIdType.MESH,
        )
        copy.start()
        copies.append(copy)
    o_ref[me] = x_ref[...] if broadcast else x_ref[me]
    for copy in copies:
        copy.wait()


def grp_exchange(chunks, site, broadcast=False):
    n = lax.axis_size("grp")
    shape = (n,) + chunks.shape if broadcast else chunks.shape
    kernel = functools.partial(_exchange_kernel, axis="grp", n=n, broadcast=broadcast)
    moved = chunks.size * chunks.dtype.itemsize * (n - 1 if broadcast else 1)
    return pl.pallas_call(
        kernel,
        out_shape=jax.ShapeDtypeStruct(shape, chunks.dtype),
        in_specs=[pl.BlockSpec(memory_space=pltpu.VMEM)],
        out_specs=pl.BlockSpec(memory_space=pltpu.VMEM),
        scratch_shapes=[pltpu.SemaphoreType.DMA((n,)), pltpu.SemaphoreType.DMA((n,))],
        compiler_params=pltpu.CompilerParams(collective_id=site, has_side_effects=True),
        cost_estimate=pl.CostEstimate(flops=0, transcendentals=0, bytes_accessed=2 * moved),
    )(chunks)


def grp_gather(rows, site):
    return grp_exchange(rows, site, broadcast=True).reshape(-1, rows.shape[1])


def grp_sum_scatter(values, site):
    groups = lax.axis_size("grp")
    pieces = values.astype(jnp.bfloat16).reshape(groups, -1, values.shape[1])
    got = grp_exchange(pieces, site)
    return jnp.sum(got.astype(jnp.float32), axis=0)


def all_sum(parts):
    axes = ("slab", "grp")
    devices = lax.axis_size("slab") * lax.axis_size("grp")
    flat = jnp.concatenate([p.reshape(-1) for p in parts])
    total = flat.shape[0]
    chunk = -(-total // devices)
    chunk = -(-chunk // 128) * 128
    flat = jnp.pad(flat, (0, devices * chunk - total)).reshape(devices, chunk)
    got = lax.all_to_all(flat, axes, 0, 0, tiled=True)
    mine = jnp.sum(got, axis=0, keepdims=True)
    back = lax.all_to_all(jnp.broadcast_to(mine, (devices, chunk)), axes, 0, 0, tiled=True)
    back = back.reshape(-1)[:total]
    out, at = [], 0
    for p in parts:
        out.append(back[at : at + p.size].reshape(p.shape))
        at += p.size
    return out


def restrict(blocks, columns, source, live_mask):
    pooled = block_apply(blocks, columns, source)
    return jnp.where(live_mask[:, None], pooled, jnp.zeros_like(pooled))


def layer_forward(node_rows, message, weight_in, weight_out, bias_row):
    joined = jnp.concatenate([node_rows, message], axis=1)
    pre_act = jnp.dot(joined, weight_in, preferred_element_type=jnp.float32) + bias_row
    hidden = jax.nn.silu(pre_act).astype(jnp.bfloat16)
    result = node_rows.astype(jnp.float32) + jnp.dot(
        hidden, weight_out, preferred_element_type=jnp.float32
    )
    return (result.astype(jnp.bfloat16), pre_act, hidden)


def layer_backward(
    cotan_rows, node_rows, message, hidden, pre_act, weight_in, weight_out, blocks, columns, targets
):
    grad_low = cotan_rows.astype(jnp.bfloat16)
    delta_out = lax.dot_general(
        hidden, grad_low, (((0,), (0,)), ((), ())), preferred_element_type=jnp.float32
    )
    grad_hidden = lax.dot_general(
        grad_low, weight_out, (((1,), (1,)), ((), ())), preferred_element_type=jnp.float32
    )
    sigmoid_pre = jax.nn.sigmoid(pre_act)
    grad_pre = grad_hidden * sigmoid_pre * (1.0 + pre_act * (1.0 - sigmoid_pre))
    grad_pre_low = grad_pre.astype(jnp.bfloat16)
    delta_bias = jnp.sum(grad_pre, axis=0)
    joined = jnp.concatenate([node_rows, message], axis=1)
    delta_in = lax.dot_general(
        joined, grad_pre_low, (((0,), (0,)), ((), ())), preferred_element_type=jnp.float32
    )
    grad_joined = lax.dot_general(
        grad_pre_low, weight_in, (((1,), (1,)), ((), ())), preferred_element_type=jnp.float32
    )
    feature = node_rows.shape[1]
    grad_rows = cotan_rows + grad_joined[:, :feature]
    grad_message = grad_joined[:, feature:].astype(jnp.bfloat16)
    grad_context = block_transpose(blocks, columns, grad_message, targets)
    return ((delta_in, delta_out, delta_bias), grad_rows, grad_context)


def pack_layout(owners, live_mask, groups, balance):
    slot_count = owners.shape[0]
    capacity = slot_count // groups
    target = owners // balance
    onehot = (
        (target[:, None] == jnp.arange(groups, dtype=jnp.int32)[None, :]) & live_mask[:, None]
    ).astype(jnp.int32)
    slot_ranks = jnp.sum(onehot * jnp.cumsum(onehot, axis=0), axis=1) - 1
    place_at = jnp.where(live_mask, target * capacity + slot_ranks, groups * capacity)
    row_table = (
        jnp.full((groups * capacity,), balance, jnp.int32)
        .at[place_at]
        .set(owners % balance, mode="drop")
    )
    return (place_at, row_table.reshape(groups, capacity))


def pack_values(values, place_at, groups):
    capacity = values.shape[0] // groups
    buffer = (
        jnp.zeros((groups * capacity, values.shape[1]), values.dtype)
        .at[place_at]
        .set(values, mode="drop")
    )
    return buffer.reshape(groups, capacity, values.shape[1])


def place_rows(received, row_table, balance):
    feature = received.shape[-1]
    flat = received.reshape(-1, feature)
    return (
        jnp.zeros((balance, feature), received.dtype)
        .at[row_table.reshape(-1)]
        .set(flat, mode="drop")
    )


def pick_rows(table, row_table):
    balance = table.shape[0]
    flat = row_table.reshape(-1)
    taken = jnp.take(table, jnp.clip(flat, 0, balance - 1), axis=0)
    taken = jnp.where((flat < balance)[:, None], taken, jnp.zeros_like(taken))
    return taken.reshape(row_table.shape[0], row_table.shape[1], table.shape[1])


def unpack_rows(received, place_at, live_mask):
    feature = received.shape[-1]
    flat = received.reshape(-1, feature)
    taken = jnp.take(flat, jnp.clip(place_at, 0, flat.shape[0] - 1), axis=0)
    return jnp.where(live_mask[:, None], taken, jnp.zeros_like(taken))


def body(
    node_feats,
    cotangent,
    fine_adjacency,
    fine_columns,
    pool_one,
    pool_one_columns,
    count_one,
    owner_one,
    adjacency_one,
    columns_one,
    pool_two,
    pool_two_columns,
    count_two,
    owner_two,
    adjacency_two,
    columns_two,
    weight_in,
    weight_out,
    biases,
):
    groups = lax.axis_size("grp")
    block_rows = fine_adjacency.shape[1]
    fine_rows, feature = node_feats.shape
    slots_one = owner_one.shape[0]
    balance_one = slots_one // 2
    slots_two = owner_two.shape[0]
    balance_two = slots_two // 2
    live_one = jnp.arange(slots_one) < count_one[0]
    live_two = jnp.arange(slots_two) < count_two[0]
    place_one, sent_one = pack_layout(owner_one, live_one, groups, balance_one)
    place_two, sent_two = pack_layout(owner_two, live_two, groups, balance_two)
    tables = lax.all_to_all(
        jnp.concatenate([sent_one, sent_two], axis=1), "grp", split_axis=0, concat_axis=0, tiled=True
    )
    rows_one, rows_two = tables[:, : sent_one.shape[1]], tables[:, sent_one.shape[1] :]

    before, after = halo_parts(node_feats, "grp", HALO)
    message0 = block_apply(fine_adjacency, fine_columns, (before, node_feats, after))
    result0, pre_act0, hidden0 = layer_forward(
        node_feats, message0, weight_in[0], weight_out[0], biases[0]
    )
    pooled_one = restrict(
        pool_one, pool_one_columns, jnp.concatenate([result0, cotangent], axis=1), live_one
    )
    got_one = grp_exchange(pack_values(pooled_one, place_one, groups), 0)
    placed_one = place_rows(got_one, rows_one, balance_one)
    own_one, grad_up_one = placed_one[:, :feature], placed_one[:, feature:]
    context_one = lax.all_to_all(
        jnp.broadcast_to(own_one[None], (groups,) + own_one.shape), "grp", 0, 0, tiled=True
    ).reshape(-1, feature)
    message_one = block_apply(adjacency_one, columns_one, context_one)
    result1, pre_act1, hidden1 = layer_forward(
        own_one, message_one, weight_in[1], weight_out[1], biases[1]
    )
    pooled_two = restrict(
        pool_two, pool_two_columns, jnp.concatenate([result1, grad_up_one], axis=1), live_two
    )
    got_two = grp_exchange(pack_values(pooled_two, place_two, groups), 2)
    placed_two = place_rows(got_two, rows_two, balance_two)
    own_two, grad_out_two = placed_two[:, :feature], placed_two[:, feature:]
    context_two = grp_gather(own_two, 3)
    message_two = block_apply(adjacency_two, columns_two, context_two)
    result2, pre_act2, hidden2 = layer_forward(
        own_two, message_two, weight_in[2], weight_out[2], biases[2]
    )
    sums_two, grad_rows_two, grad_ctx_two = layer_backward(
        grad_out_two.astype(jnp.float32),
        own_two,
        message_two,
        hidden2,
        pre_act2,
        weight_in[2],
        weight_out[2],
        adjacency_two,
        columns_two,
        groups * balance_two // block_rows,
    )
    grad_own_two = grad_rows_two + grp_sum_scatter(grad_ctx_two, 4)
    returned_two = grp_exchange(
        pick_rows(jnp.concatenate([result2, grad_own_two.astype(jnp.bfloat16)], axis=1), rows_two), 5
    )
    back_two = unpack_rows(returned_two, place_two, live_two)
    lifted_one = block_transpose(pool_two, pool_two_columns, back_two, balance_one // block_rows)
    up_one = (result1.astype(jnp.float32) + lifted_one[:, :feature]).astype(jnp.bfloat16)
    grad_out_one = grad_up_one.astype(jnp.float32) + lifted_one[:, feature:]
    sums_one, grad_rows_one, grad_ctx_one = layer_backward(
        grad_out_one,
        own_one,
        message_one,
        hidden1,
        pre_act1,
        weight_in[1],
        weight_out[1],
        adjacency_one,
        columns_one,
        groups * balance_one // block_rows,
    )
    grad_own_one = grad_rows_one + grp_sum_scatter(grad_ctx_one, 6)
    returned_one = grp_exchange(
        pick_rows(jnp.concatenate([up_one, grad_own_one.astype(jnp.bfloat16)], axis=1), rows_one), 7
    )
    back_one = unpack_rows(returned_one, place_one, live_one)
    lifted_zero = block_transpose(pool_one, pool_one_columns, back_one, fine_rows // block_rows)
    node_out = (result0.astype(jnp.float32) + lifted_zero[:, :feature]).astype(jnp.bfloat16)
    grad_out_zero = cotangent.astype(jnp.float32) + lifted_zero[:, feature:]
    sums_zero, grad_rows_zero, grad_ctx_zero = layer_backward(
        grad_out_zero,
        node_feats,
        message0,
        hidden0,
        pre_act0,
        weight_in[0],
        weight_out[0],
        fine_adjacency,
        fine_columns,
        (fine_rows + 2 * HALO) // block_rows,
    )
    rim_terms = jnp.concatenate([grad_ctx_zero[:HALO], grad_ctx_zero[HALO + fine_rows :]], axis=0)
    neighbour_terms = with_halo(rim_terms.astype(jnp.bfloat16), (("grp", 0),), HALO).astype(
        rim_terms.dtype
    )
    rim_add = jnp.concatenate(
        [
            neighbour_terms[:HALO],
            jnp.zeros((fine_rows - 2 * HALO, feature), neighbour_terms.dtype),
            neighbour_terms[3 * HALO :],
        ],
        axis=0,
    )
    grad_feats = (grad_rows_zero + grad_ctx_zero[HALO : HALO + fine_rows] + rim_add).astype(
        jnp.bfloat16
    )
    stack_in = jnp.stack([sums_zero[0], sums_one[0], sums_two[0]])
    stack_out = jnp.stack([sums_zero[1], sums_one[1], sums_two[1]])
    stack_bias = jnp.stack([sums_zero[2], sums_one[2], sums_two[2]])
    stack_in, stack_out, stack_bias = all_sum((stack_in, stack_out, stack_bias))
    inv_root = 1.0 / math.sqrt(fine_rows * groups * lax.axis_size("slab"))
    return (node_out, grad_feats, stack_in * inv_root, stack_out * inv_root, stack_bias * inv_root)


def solution(mesh):
    placed = (
        P(("slab", "grp"), None),
        P(("slab", "grp"), None),
        P(("slab", "grp"), None, None),
        P(("slab", "grp"), None),
        P(("slab", "grp"), None, None),
        P(("slab", "grp"), None),
        P(("slab", "grp")),
        P(("slab", "grp")),
        P(("slab", "grp"), None, None),
        P(("slab", "grp"), None),
        P(("slab", "grp"), None, None),
        P(("slab", "grp"), None),
        P(("slab", "grp")),
        P(("slab", "grp")),
        P(("slab", "grp"), None, None),
        P(("slab", "grp"), None),
        P(),
        P(),
        P(),
    )
    return jax.shard_map(
        body,
        mesh=mesh,
        in_specs=placed,
        out_specs=(P(("slab", "grp"), None), P(("slab", "grp"), None), P(), P(), P()),
        check_vma=False,
    )
```

```python
import functools
import math

import jax
import jax.numpy as jnp
from jax import lax
from jax.experimental import pallas as pl
from jax.experimental.pallas import tpu as pltpu
from jax.sharding import PartitionSpec as P

HALO = 512


def with_halo(cells, sides, width):
    for axis, dim in sides:
        count = lax.axis_size(axis)
        ends = count - 1
        head = lax.slice_in_dim(cells, 0, width, axis=dim)
        tail = lax.slice_in_dim(cells, cells.shape[dim] - width, cells.shape[dim], axis=dim)
        cells = jnp.concatenate(
            [
                lax.ppermute(tail, axis, [(i, (i + 1) % count) for i in range(ends)]),
                cells,
                lax.ppermute(head, axis, [((i + 1) % count, i) for i in range(ends)]),
            ],
            axis=dim,
        )
    return cells


def halo_parts(cells, axis, width):
    count = lax.axis_size(axis)
    ends = count - 1
    head = cells[:width]
    tail = cells[cells.shape[0] - width :]
    before = lax.ppermute(tail, axis, [(i, (i + 1) % count) for i in range(ends)])
    after = lax.ppermute(head, axis, [((i + 1) % count, i) for i in range(ends)])
    return before, after


def _per_step(block_count):
    return min(block_count, 8)


def _apply_kernel(cols_ref, m_ref, *refs, k, per_step, blk, pieces_in):
    q_parts, (o_ref, q_ref) = refs[:pieces_in], refs[pieces_in:]
    step = pl.program_id(0)

    @pl.when(step == 0)
    def _():
        at = 0
        for part in q_parts:
            q_ref[at : at + part.shape[0], :] = part[...]
            at += part.shape[0]

    def one_block(j, carry):
        r = step * per_step + j
        pieces = [
            q_ref[pl.ds(pl.multiple_of(cols_ref[r * k + i] * blk, blk), blk), :] for i in range(k)
        ]
        stacked = jnp.concatenate(pieces, axis=0)
        res = jnp.dot(m_ref[j], stacked, preferred_element_type=jnp.float32)
        o_ref[pl.ds(pl.multiple_of(j * blk, blk), blk), :] = res.astype(o_ref.dtype)
        return carry

    lax.fori_loop(0, per_step, one_block, 0)


def block_apply(blocks, columns, context, out_dtype=jnp.bfloat16):
    block_count, block_rows, span = blocks.shape
    k = columns.shape[1]
    parts = tuple(context) if isinstance(context, (tuple, list)) else (context,)
    feature = parts[0].shape[1]
    rows = sum(p.shape[0] for p in parts)
    per_step = _per_step(block_count)
    kernel = functools.partial(
        _apply_kernel, k=k, per_step=per_step, blk=block_rows, pieces_in=len(parts)
    )
    return pl.pallas_call(
        kernel,
        out_shape=jax.ShapeDtypeStruct((block_count * block_rows, feature), out_dtype),
        grid_spec=pltpu.PrefetchScalarGridSpec(
            num_scalar_prefetch=1,
            grid=(block_count // per_step,),
            in_specs=[pl.BlockSpec((per_step, block_rows, span), lambda s, c: (s, 0, 0))]
            + [pl.BlockSpec(p.shape, lambda s, c: (0, 0)) for p in parts],
            out_specs=pl.BlockSpec((per_step * block_rows, feature), lambda s, c: (s, 0)),
            scratch_shapes=[pltpu.VMEM((rows, feature), parts[0].dtype)],
        ),
        compiler_params=pltpu.CompilerParams(dimension_semantics=("arbitrary",)),
        cost_estimate=pl.CostEstimate(
            flops=2 * block_count * block_rows * span * feature,
            transcendentals=0,
            bytes_accessed=blocks.size * 2 + rows * feature * 2 + block_count * block_rows * feature * 2,
        ),
    )(columns.reshape(-1), blocks, *parts)


def _apply_t_kernel(cols_ref, m_ref, p_ref, o_ref, *, k, per_step, blk):
    step = pl.program_id(0)

    @pl.when(step == 0)
    def _():
        o_ref[...] = jnp.zeros_like(o_ref)

    def one_block(j, carry):
        r = step * per_step + j
        spread = lax.dot_general(
            m_ref[j],
            p_ref[pl.ds(pl.multiple_of(j * blk, blk), blk), :],
            (((0,), (0,)), ((), ())),
            preferred_element_type=jnp.float32,
        )
        for i in range(k):
            at = pl.multiple_of(cols_ref[r * k + i] * blk, blk)
            o_ref[pl.ds(at, blk), :] += spread[i * blk : (i + 1) * blk]
        return carry

    lax.fori_loop(0, per_step, one_block, 0)


def block_transpose(blocks, columns, row_grads, targets):
    block_count, block_rows, span = blocks.shape
    k = columns.shape[1]
    feature = row_grads.shape[1]
    per_step = _per_step(block_count)
    kernel = functools.partial(_apply_t_kernel, k=k, per_step=per_step, blk=block_rows)
    return pl.pallas_call(
        kernel,
        out_shape=jax.ShapeDtypeStruct((targets * block_rows, feature), jnp.float32),
        grid_spec=pltpu.PrefetchScalarGridSpec(
            num_scalar_prefetch=1,
            grid=(block_count // per_step,),
            in_specs=[
                pl.BlockSpec((per_step, block_rows, span), lambda s, c: (s, 0, 0)),
                pl.BlockSpec((per_step * block_rows, feature), lambda s, c: (s, 0)),
            ],
            out_specs=pl.BlockSpec((targets * block_rows, feature), lambda s, c: (0, 0)),
        ),
        compiler_params=pltpu.CompilerParams(dimension_semantics=("arbitrary",)),
        cost_estimate=pl.CostEstimate(
            flops=2 * block_count * block_rows * span * feature,
            transcendentals=0,
            bytes_accessed=blocks.size * 2 + row_grads.size * 2 + targets * block_rows * feature * 4,
        ),
    )(columns.reshape(-1), blocks, row_grads.astype(jnp.bfloat16))


def _exchange_kernel(x_ref, o_ref, send_sem, recv_sem, *, axis, n, broadcast):
    me = lax.axis_index(axis)
    barrier = pltpu.get_barrier_semaphore()
    def greet(d, carry):
        pl.semaphore_signal(
            barrier, inc=1, device_id={axis: lax.rem(me + d, n)}, device_id_type=pl.DeviceIdType.MESH
        )
        return carry

    lax.fori_loop(1, n, greet, 0)
    pl.semaphore_wait(barrier, n - 1)

    def copy_to(d):
        peer = lax.rem(me + d, n)
        return pltpu.make_async_remote_copy(
            src_ref=x_ref if broadcast else x_ref.at[peer],
            dst_ref=o_ref.at[me],
            send_sem=send_sem.at[d],
            recv_sem=recv_sem.at[d],
            device_id={axis: peer},
            device_id_type=pl.DeviceIdType.MESH,
        )

    def start(d, carry):
        copy_to(d).start()
        return carry

    def finish(d, carry):
        copy_to(d).wait()
        return carry

    lax.fori_loop(1, n, start, 0)
    o_ref[me] = x_ref[...] if broadcast else x_ref[me]
    lax.fori_loop(1, n, finish, 0)


def grp_exchange(chunks, site, broadcast=False):
    n = lax.axis_size("grp")
    shape = (n,) + chunks.shape if broadcast else chunks.shape
    kernel = functools.partial(_exchange_kernel, axis="grp", n=n, broadcast=broadcast)
    moved = chunks.size * chunks.dtype.itemsize * (n - 1 if broadcast else 1)
    return pl.pallas_call(
        kernel,
        out_shape=jax.ShapeDtypeStruct(shape, chunks.dtype),
        in_specs=[pl.BlockSpec(memory_space=pltpu.VMEM)],
        out_specs=pl.BlockSpec(memory_space=pltpu.VMEM),
        scratch_shapes=[pltpu.SemaphoreType.DMA((n,)), pltpu.SemaphoreType.DMA((n,))],
        compiler_params=pltpu.CompilerParams(collective_id=site, has_side_effects=True),
        cost_estimate=pl.CostEstimate(flops=0, transcendentals=0, bytes_accessed=2 * moved),
    )(chunks)


def grp_gather(rows, site):
    return grp_exchange(rows, site, broadcast=True).reshape(-1, rows.shape[1])


def grp_sum_scatter(values, site):
    groups = lax.axis_size("grp")
    pieces = values.astype(jnp.bfloat16).reshape(groups, -1, values.shape[1])
    got = grp_exchange(pieces, site)
    return jnp.sum(got.astype(jnp.float32), axis=0)


def all_sum(parts):
    axes = ("slab", "grp")
    devices = lax.axis_size("slab") * lax.axis_size("grp")
    flat = jnp.concatenate([p.reshape(-1) for p in parts])
    total = flat.shape[0]
    chunk = -(-total // devices)
    chunk = -(-chunk // 128) * 128
    flat = jnp.pad(flat, (0, devices * chunk - total)).reshape(devices, chunk)
    got = lax.all_to_all(flat, axes, 0, 0, tiled=True)
    mine = jnp.sum(got, axis=0, keepdims=True)
    back = lax.all_to_all(jnp.broadcast_to(mine, (devices, chunk)), axes, 0, 0, tiled=True)
    back = back.reshape(-1)[:total]
    out, at = [], 0
    for p in parts:
        out.append(back[at : at + p.size].reshape(p.shape))
        at += p.size
    return out


def restrict(blocks, columns, source, live_mask):
    pooled = block_apply(blocks, columns, source)
    return jnp.where(live_mask[:, None], pooled, jnp.zeros_like(pooled))


def layer_forward(node_rows, message, weight_in, weight_out, bias_row):
    joined = jnp.concatenate([node_rows, message], axis=1)
    pre_act = jnp.dot(joined, weight_in, preferred_element_type=jnp.float32) + bias_row
    hidden = jax.nn.silu(pre_act).astype(jnp.bfloat16)
    result = node_rows.astype(jnp.float32) + jnp.dot(
        hidden, weight_out, preferred_element_type=jnp.float32
    )
    return (result.astype(jnp.bfloat16), pre_act, hidden)


def layer_backward(
    cotan_rows, node_rows, message, hidden, pre_act, weight_in, weight_out, blocks, columns, targets
):
    grad_low = cotan_rows.astype(jnp.bfloat16)
    delta_out = lax.dot_general(
        hidden, grad_low, (((0,), (0,)), ((), ())), preferred_element_type=jnp.float32
    )
    grad_hidden = lax.dot_general(
        grad_low, weight_out, (((1,), (1,)), ((), ())), preferred_element_type=jnp.float32
    )
    sigmoid_pre = jax.nn.sigmoid(pre_act)
    grad_pre = grad_hidden * sigmoid_pre * (1.0 + pre_act * (1.0 - sigmoid_pre))
    grad_pre_low = grad_pre.astype(jnp.bfloat16)
    delta_bias = jnp.sum(grad_pre, axis=0)
    joined = jnp.concatenate([node_rows, message], axis=1)
    delta_in = lax.dot_general(
        joined, grad_pre_low, (((0,), (0,)), ((), ())), preferred_element_type=jnp.float32
    )
    grad_joined = lax.dot_general(
        grad_pre_low, weight_in, (((1,), (1,)), ((), ())), preferred_element_type=jnp.float32
    )
    feature = node_rows.shape[1]
    grad_rows = cotan_rows + grad_joined[:, :feature]
    grad_message = grad_joined[:, feature:].astype(jnp.bfloat16)
    grad_context = block_transpose(blocks, columns, grad_message, targets)
    return ((delta_in, delta_out, delta_bias), grad_rows, grad_context)


def pack_layout(owners, live_mask, groups, balance):
    slot_count = owners.shape[0]
    capacity = slot_count // groups
    target = owners // balance
    onehot = (
        (target[:, None] == jnp.arange(groups, dtype=jnp.int32)[None, :]) & live_mask[:, None]
    ).astype(jnp.int32)
    slot_ranks = jnp.sum(onehot * jnp.cumsum(onehot, axis=0), axis=1) - 1
    place_at = jnp.where(live_mask, target * capacity + slot_ranks, groups * capacity)
    row_table = (
        jnp.full((groups * capacity,), balance, jnp.int32)
        .at[place_at]
        .set(owners % balance, mode="drop")
    )
    return (place_at, row_table.reshape(groups, capacity))


def pack_values(values, place_at, groups):
    capacity = values.shape[0] // groups
    buffer = (
        jnp.zeros((groups * capacity, values.shape[1]), values.dtype)
        .at[place_at]
        .set(values, mode="drop")
    )
    return buffer.reshape(groups, capacity, values.shape[1])


def place_rows(received, row_table, balance):
    feature = received.shape[-1]
    flat = received.reshape(-1, feature)
    return (
        jnp.zeros((balance, feature), received.dtype)
        .at[row_table.reshape(-1)]
        .set(flat, mode="drop")
    )


def pick_rows(table, row_table):
    balance = table.shape[0]
    flat = row_table.reshape(-1)
    taken = jnp.take(table, jnp.clip(flat, 0, balance - 1), axis=0)
    taken = jnp.where((flat < balance)[:, None], taken, jnp.zeros_like(taken))
    return taken.reshape(row_table.shape[0], row_table.shape[1], table.shape[1])


def unpack_rows(received, place_at, live_mask):
    feature = received.shape[-1]
    flat = received.reshape(-1, feature)
    taken = jnp.take(flat, jnp.clip(place_at, 0, flat.shape[0] - 1), axis=0)
    return jnp.where(live_mask[:, None], taken, jnp.zeros_like(taken))


def body(
    node_feats,
    cotangent,
    fine_adjacency,
    fine_columns,
    pool_one,
    pool_one_columns,
    count_one,
    owner_one,
    adjacency_one,
    columns_one,
    pool_two,
    pool_two_columns,
    count_two,
    owner_two,
    adjacency_two,
    columns_two,
    weight_in,
    weight_out,
    biases,
):
    groups = lax.axis_size("grp")
    block_rows = fine_adjacency.shape[1]
    fine_rows, feature = node_feats.shape
    slots_one = owner_one.shape[0]
    balance_one = slots_one // 2
    slots_two = owner_two.shape[0]
    balance_two = slots_two // 2
    live_one = jnp.arange(slots_one) < count_one[0]
    live_two = jnp.arange(slots_two) < count_two[0]
    place_one, sent_one = pack_layout(owner_one, live_one, groups, balance_one)
    place_two, sent_two = pack_layout(owner_two, live_two, groups, balance_two)
    tables = lax.all_to_all(
        jnp.concatenate([sent_one, sent_two], axis=1), "grp", split_axis=0, concat_axis=0, tiled=True
    )
    rows_one, rows_two = tables[:, : sent_one.shape[1]], tables[:, sent_one.shape[1] :]

    before, after = halo_parts(node_feats, "grp", HALO)
    message0 = block_apply(fine_adjacency, fine_columns, (before, node_feats, after))
    result0, pre_act0, hidden0 = layer_forward(
        node_feats, message0, weight_in[0], weight_out[0], biases[0]
    )
    pooled_one = restrict(
        pool_one, pool_one_columns, jnp.concatenate([result0, cotangent], axis=1), live_one
    )
    got_one = grp_exchange(pack_values(pooled_one, place_one, groups), 0)
    placed_one = place_rows(got_one, rows_one, balance_one)
    own_one, grad_up_one = placed_one[:, :feature], placed_one[:, feature:]
    context_one = lax.all_to_all(
        jnp.broadcast_to(own_one[None], (groups,) + own_one.shape), "grp", 0, 0, tiled=True
    ).reshape(-1, feature)
    message_one = block_apply(adjacency_one, columns_one, context_one)
    result1, pre_act1, hidden1 = layer_forward(
        own_one, message_one, weight_in[1], weight_out[1], biases[1]
    )
    pooled_two = restrict(
        pool_two, pool_two_columns, jnp.concatenate([result1, grad_up_one], axis=1), live_two
    )
    got_two = grp_exchange(pack_values(pooled_two, place_two, groups), 2)
    placed_two = place_rows(got_two, rows_two, balance_two)
    own_two, grad_out_two = placed_two[:, :feature], placed_two[:, feature:]
    context_two = grp_gather(own_two, 3)
    message_two = block_apply(adjacency_two, columns_two, context_two)
    result2, pre_act2, hidden2 = layer_forward(
        own_two, message_two, weight_in[2], weight_out[2], biases[2]
    )
    sums_two, grad_rows_two, grad_ctx_two = layer_backward(
        grad_out_two.astype(jnp.float32),
        own_two,
        message_two,
        hidden2,
        pre_act2,
        weight_in[2],
        weight_out[2],
        adjacency_two,
        columns_two,
        groups * balance_two // block_rows,
    )
    grad_own_two = grad_rows_two + grp_sum_scatter(grad_ctx_two, 4)
    returned_two = grp_exchange(
        pick_rows(jnp.concatenate([result2, grad_own_two.astype(jnp.bfloat16)], axis=1), rows_two), 5
    )
    back_two = unpack_rows(returned_two, place_two, live_two)
    lifted_one = block_transpose(pool_two, pool_two_columns, back_two, balance_one // block_rows)
    up_one = (result1.astype(jnp.float32) + lifted_one[:, :feature]).astype(jnp.bfloat16)
    grad_out_one = grad_up_one.astype(jnp.float32) + lifted_one[:, feature:]
    sums_one, grad_rows_one, grad_ctx_one = layer_backward(
        grad_out_one,
        own_one,
        message_one,
        hidden1,
        pre_act1,
        weight_in[1],
        weight_out[1],
        adjacency_one,
        columns_one,
        groups * balance_one // block_rows,
    )
    grad_own_one = grad_rows_one + grp_sum_scatter(grad_ctx_one, 6)
    returned_one = grp_exchange(
        pick_rows(jnp.concatenate([up_one, grad_own_one.astype(jnp.bfloat16)], axis=1), rows_one), 7
    )
    back_one = unpack_rows(returned_one, place_one, live_one)
    lifted_zero = block_transpose(pool_one, pool_one_columns, back_one, fine_rows // block_rows)
    node_out = (result0.astype(jnp.float32) + lifted_zero[:, :feature]).astype(jnp.bfloat16)
    grad_out_zero = cotangent.astype(jnp.float32) + lifted_zero[:, feature:]
    sums_zero, grad_rows_zero, grad_ctx_zero = layer_backward(
        grad_out_zero,
        node_feats,
        message0,
        hidden0,
        pre_act0,
        weight_in[0],
        weight_out[0],
        fine_adjacency,
        fine_columns,
        (fine_rows + 2 * HALO) // block_rows,
    )
    rim_terms = jnp.concatenate([grad_ctx_zero[:HALO], grad_ctx_zero[HALO + fine_rows :]], axis=0)
    neighbour_terms = with_halo(rim_terms.astype(jnp.bfloat16), (("grp", 0),), HALO).astype(
        rim_terms.dtype
    )
    gathered_total = grad_rows_zero + grad_ctx_zero[HALO : HALO + fine_rows]
    gathered_total = gathered_total.at[:HALO].add(neighbour_terms[:HALO])
    gathered_total = gathered_total.at[fine_rows - HALO :].add(neighbour_terms[3 * HALO :])
    grad_feats = gathered_total.astype(jnp.bfloat16)
    stack_in = jnp.stack([sums_zero[0], sums_one[0], sums_two[0]])
    stack_out = jnp.stack([sums_zero[1], sums_one[1], sums_two[1]])
    stack_bias = jnp.stack([sums_zero[2], sums_one[2], sums_two[2]])
    stack_in, stack_out, stack_bias = all_sum((stack_in, stack_out, stack_bias))
    inv_root = 1.0 / math.sqrt(fine_rows * groups * lax.axis_size("slab"))
    return (node_out, grad_feats, stack_in * inv_root, stack_out * inv_root, stack_bias * inv_root)


def solution(mesh):
    placed = (
        P(("slab", "grp"), None),
        P(("slab", "grp"), None),
        P(("slab", "grp"), None, None),
        P(("slab", "grp"), None),
        P(("slab", "grp"), None, None),
        P(("slab", "grp"), None),
        P(("slab", "grp")),
        P(("slab", "grp")),
        P(("slab", "grp"), None, None),
        P(("slab", "grp"), None),
        P(("slab", "grp"), None, None),
        P(("slab", "grp"), None),
        P(("slab", "grp")),
        P(("slab", "grp")),
        P(("slab", "grp"), None, None),
        P(("slab", "grp"), None),
        P(),
        P(),
        P(),
    )
    return jax.shard_map(
        body,
        mesh=mesh,
        in_specs=placed,
        out_specs=(P(("slab", "grp"), None), P(("slab", "grp"), None), P(), P(), P()),
        check_vma=False,
    )
```

```python
import functools
import math

import jax
import jax.numpy as jnp
from jax import lax
from jax.experimental import pallas as pl
from jax.experimental.pallas import tpu as pltpu
from jax.sharding import PartitionSpec as P

HALO = 512


def with_halo(cells, sides, width):
    for axis, dim in sides:
        count = lax.axis_size(axis)
        ends = count - 1
        head = lax.slice_in_dim(cells, 0, width, axis=dim)
        tail = lax.slice_in_dim(cells, cells.shape[dim] - width, cells.shape[dim], axis=dim)
        cells = jnp.concatenate(
            [
                lax.ppermute(tail, axis, [(i, (i + 1) % count) for i in range(ends)]),
                cells,
                lax.ppermute(head, axis, [((i + 1) % count, i) for i in range(ends)]),
            ],
            axis=dim,
        )
    return cells


def halo_parts(cells, axis, width):
    count = lax.axis_size(axis)
    ends = count - 1
    head = cells[:width]
    tail = cells[cells.shape[0] - width :]
    before = lax.ppermute(tail, axis, [(i, (i + 1) % count) for i in range(ends)])
    after = lax.ppermute(head, axis, [((i + 1) % count, i) for i in range(ends)])
    return before, after


def _per_step(block_count):
    return min(block_count, 8)


def _apply_kernel(cols_ref, m_ref, *refs, k, per_step, blk, pieces_in):
    q_parts, (o_ref, q_ref) = refs[:pieces_in], refs[pieces_in:]
    step = pl.program_id(0)

    @pl.when(step == 0)
    def _():
        at = 0
        for part in q_parts:
            q_ref[at : at + part.shape[0], :] = part[...]
            at += part.shape[0]

    for j in range(per_step):
        r = step * per_step + j
        pieces = [
            q_ref[pl.ds(pl.multiple_of(cols_ref[r * k + i] * blk, blk), blk), :] for i in range(k)
        ]
        stacked = jnp.concatenate(pieces, axis=0)
        res = jnp.dot(m_ref[j], stacked, preferred_element_type=jnp.float32)
        o_ref[j * blk : (j + 1) * blk, :] = res.astype(o_ref.dtype)


def block_apply(blocks, columns, context, out_dtype=jnp.bfloat16):
    block_count, block_rows, span = blocks.shape
    k = columns.shape[1]
    parts = tuple(context) if isinstance(context, (tuple, list)) else (context,)
    feature = parts[0].shape[1]
    rows = sum(p.shape[0] for p in parts)
    per_step = _per_step(block_count)
    kernel = functools.partial(
        _apply_kernel, k=k, per_step=per_step, blk=block_rows, pieces_in=len(parts)
    )
    return pl.pallas_call(
        kernel,
        out_shape=jax.ShapeDtypeStruct((block_count * block_rows, feature), out_dtype),
        grid_spec=pltpu.PrefetchScalarGridSpec(
            num_scalar_prefetch=1,
            grid=(block_count // per_step,),
            in_specs=[pl.BlockSpec((per_step, block_rows, span), lambda s, c: (s, 0, 0))]
            + [pl.BlockSpec(p.shape, lambda s, c: (0, 0)) for p in parts],
            out_specs=pl.BlockSpec((per_step * block_rows, feature), lambda s, c: (s, 0)),
            scratch_shapes=[pltpu.VMEM((rows, feature), parts[0].dtype)],
        ),
        compiler_params=pltpu.CompilerParams(dimension_semantics=("arbitrary",)),
        cost_estimate=pl.CostEstimate(
            flops=2 * block_count * block_rows * span * feature,
            transcendentals=0,
            bytes_accessed=blocks.size * 2 + rows * feature * 2 + block_count * block_rows * feature * 2,
        ),
    )(columns.reshape(-1), blocks, *parts)


def _apply_t_kernel(cols_ref, m_ref, p_ref, o_ref, *, k, per_step, blk):
    step = pl.program_id(0)

    @pl.when(step == 0)
    def _():
        o_ref[...] = jnp.zeros_like(o_ref)

    for j in range(per_step):
        r = step * per_step + j
        spread = lax.dot_general(
            m_ref[j],
            p_ref[j * blk : (j + 1) * blk, :],
            (((0,), (0,)), ((), ())),
            preferred_element_type=jnp.float32,
        )
        for i in range(k):
            at = pl.multiple_of(cols_ref[r * k + i] * blk, blk)
            o_ref[pl.ds(at, blk), :] += spread[i * blk : (i + 1) * blk]


def block_transpose(blocks, columns, row_grads, targets):
    block_count, block_rows, span = blocks.shape
    k = columns.shape[1]
    feature = row_grads.shape[1]
    per_step = _per_step(block_count)
    kernel = functools.partial(_apply_t_kernel, k=k, per_step=per_step, blk=block_rows)
    return pl.pallas_call(
        kernel,
        out_shape=jax.ShapeDtypeStruct((targets * block_rows, feature), jnp.float32),
        grid_spec=pltpu.PrefetchScalarGridSpec(
            num_scalar_prefetch=1,
            grid=(block_count // per_step,),
            in_specs=[
                pl.BlockSpec((per_step, block_rows, span), lambda s, c: (s, 0, 0)),
                pl.BlockSpec((per_step * block_rows, feature), lambda s, c: (s, 0)),
            ],
            out_specs=pl.BlockSpec((targets * block_rows, feature), lambda s, c: (0, 0)),
        ),
        compiler_params=pltpu.CompilerParams(dimension_semantics=("arbitrary",)),
        cost_estimate=pl.CostEstimate(
            flops=2 * block_count * block_rows * span * feature,
            transcendentals=0,
            bytes_accessed=blocks.size * 2 + row_grads.size * 2 + targets * block_rows * feature * 4,
        ),
    )(columns.reshape(-1), blocks, row_grads.astype(jnp.bfloat16))


def _exchange_kernel(x_ref, o_ref, send_sem, recv_sem, *, axis, n, broadcast):
    me = lax.axis_index(axis)
    barrier = pltpu.get_barrier_semaphore()
    def greet(d, carry):
        pl.semaphore_signal(
            barrier, inc=1, device_id={axis: lax.rem(me + d, n)}, device_id_type=pl.DeviceIdType.MESH
        )
        return carry

    lax.fori_loop(1, n, greet, 0)
    pl.semaphore_wait(barrier, n - 1)

    def copy_to(d):
        peer = lax.rem(me + d, n)
        return pltpu.make_async_remote_copy(
            src_ref=x_ref if broadcast else x_ref.at[peer],
            dst_ref=o_ref.at[me],
            send_sem=send_sem.at[d],
            recv_sem=recv_sem.at[d],
            device_id={axis: peer},
            device_id_type=pl.DeviceIdType.MESH,
        )

    def start(d, carry):
        copy_to(d).start()
        return carry

    def finish(d, carry):
        copy_to(d).wait()
        return carry

    lax.fori_loop(1, n, start, 0)
    o_ref[me] = x_ref[...] if broadcast else x_ref[me]
    lax.fori_loop(1, n, finish, 0)


def grp_exchange(chunks, site, broadcast=False):
    n = lax.axis_size("grp")
    shape = (n,) + chunks.shape if broadcast else chunks.shape
    kernel = functools.partial(_exchange_kernel, axis="grp", n=n, broadcast=broadcast)
    moved = chunks.size * chunks.dtype.itemsize * (n - 1 if broadcast else 1)
    return pl.pallas_call(
        kernel,
        out_shape=jax.ShapeDtypeStruct(shape, chunks.dtype),
        in_specs=[pl.BlockSpec(memory_space=pltpu.VMEM)],
        out_specs=pl.BlockSpec(memory_space=pltpu.VMEM),
        scratch_shapes=[pltpu.SemaphoreType.DMA((n,)), pltpu.SemaphoreType.DMA((n,))],
        compiler_params=pltpu.CompilerParams(collective_id=site, has_side_effects=True),
        cost_estimate=pl.CostEstimate(flops=0, transcendentals=0, bytes_accessed=2 * moved),
    )(chunks)


def grp_gather(rows, site):
    return grp_exchange(rows, site, broadcast=True).reshape(-1, rows.shape[1])


def grp_sum_scatter(values, site):
    groups = lax.axis_size("grp")
    pieces = values.astype(jnp.bfloat16).reshape(groups, -1, values.shape[1])
    got = grp_exchange(pieces, site)
    return jnp.sum(got.astype(jnp.float32), axis=0)


def all_sum(parts):
    axes = ("slab", "grp")
    devices = lax.axis_size("slab") * lax.axis_size("grp")
    flat = jnp.concatenate([p.reshape(-1) for p in parts])
    total = flat.shape[0]
    chunk = -(-total // devices)
    chunk = -(-chunk // 128) * 128
    flat = jnp.pad(flat, (0, devices * chunk - total)).reshape(devices, chunk)
    got = lax.all_to_all(flat, axes, 0, 0, tiled=True)
    mine = jnp.sum(got, axis=0, keepdims=True)
    back = lax.all_to_all(jnp.broadcast_to(mine, (devices, chunk)), axes, 0, 0, tiled=True)
    back = back.reshape(-1)[:total]
    out, at = [], 0
    for p in parts:
        out.append(back[at : at + p.size].reshape(p.shape))
        at += p.size
    return out


def restrict(blocks, columns, source, live_mask):
    pooled = block_apply(blocks, columns, source)
    return jnp.where(live_mask[:, None], pooled, jnp.zeros_like(pooled))


def layer_forward(node_rows, message, weight_in, weight_out, bias_row):
    joined = jnp.concatenate([node_rows, message], axis=1)
    pre_act = jnp.dot(joined, weight_in, preferred_element_type=jnp.float32) + bias_row
    hidden = jax.nn.silu(pre_act).astype(jnp.bfloat16)
    result = node_rows.astype(jnp.float32) + jnp.dot(
        hidden, weight_out, preferred_element_type=jnp.float32
    )
    return (result.astype(jnp.bfloat16), pre_act, hidden)


def layer_backward(
    cotan_rows, node_rows, message, hidden, pre_act, weight_in, weight_out, blocks, columns, targets
):
    grad_low = cotan_rows.astype(jnp.bfloat16)
    delta_out = lax.dot_general(
        hidden, grad_low, (((0,), (0,)), ((), ())), preferred_element_type=jnp.float32
    )
    grad_hidden = lax.dot_general(
        grad_low, weight_out, (((1,), (1,)), ((), ())), preferred_element_type=jnp.float32
    )
    sigmoid_pre = jax.nn.sigmoid(pre_act)
    grad_pre = grad_hidden * sigmoid_pre * (1.0 + pre_act * (1.0 - sigmoid_pre))
    grad_pre_low = grad_pre.astype(jnp.bfloat16)
    delta_bias = jnp.sum(grad_pre, axis=0)
    joined = jnp.concatenate([node_rows, message], axis=1)
    delta_in = lax.dot_general(
        joined, grad_pre_low, (((0,), (0,)), ((), ())), preferred_element_type=jnp.float32
    )
    grad_joined = lax.dot_general(
        grad_pre_low, weight_in, (((1,), (1,)), ((), ())), preferred_element_type=jnp.float32
    )
    feature = node_rows.shape[1]
    grad_rows = cotan_rows + grad_joined[:, :feature]
    grad_message = grad_joined[:, feature:].astype(jnp.bfloat16)
    grad_context = block_transpose(blocks, columns, grad_message, targets)
    return ((delta_in, delta_out, delta_bias), grad_rows, grad_context)


def pack_layout(owners, live_mask, groups, balance):
    slot_count = owners.shape[0]
    capacity = slot_count // groups
    target = owners // balance
    onehot = (
        (target[:, None] == jnp.arange(groups, dtype=jnp.int32)[None, :]) & live_mask[:, None]
    ).astype(jnp.int32)
    slot_ranks = jnp.sum(onehot * jnp.cumsum(onehot, axis=0), axis=1) - 1
    place_at = jnp.where(live_mask, target * capacity + slot_ranks, groups * capacity)
    row_table = (
        jnp.full((groups * capacity,), balance, jnp.int32)
        .at[place_at]
        .set(owners % balance, mode="drop")
    )
    return (place_at, row_table.reshape(groups, capacity))


def pack_values(values, place_at, groups):
    capacity = values.shape[0] // groups
    buffer = (
        jnp.zeros((groups * capacity, values.shape[1]), values.dtype)
        .at[place_at]
        .set(values, mode="drop")
    )
    return buffer.reshape(groups, capacity, values.shape[1])


def place_rows(received, row_table, balance):
    feature = received.shape[-1]
    flat = received.reshape(-1, feature)
    return (
        jnp.zeros((balance, feature), received.dtype)
        .at[row_table.reshape(-1)]
        .set(flat, mode="drop")
    )


def pick_rows(table, row_table):
    balance = table.shape[0]
    flat = row_table.reshape(-1)
    taken = jnp.take(table, jnp.clip(flat, 0, balance - 1), axis=0)
    taken = jnp.where((flat < balance)[:, None], taken, jnp.zeros_like(taken))
    return taken.reshape(row_table.shape[0], row_table.shape[1], table.shape[1])


def unpack_rows(received, place_at, live_mask):
    feature = received.shape[-1]
    flat = received.reshape(-1, feature)
    taken = jnp.take(flat, jnp.clip(place_at, 0, flat.shape[0] - 1), axis=0)
    return jnp.where(live_mask[:, None], taken, jnp.zeros_like(taken))


def body(
    node_feats,
    cotangent,
    fine_adjacency,
    fine_columns,
    pool_one,
    pool_one_columns,
    count_one,
    owner_one,
    adjacency_one,
    columns_one,
    pool_two,
    pool_two_columns,
    count_two,
    owner_two,
    adjacency_two,
    columns_two,
    weight_in,
    weight_out,
    biases,
):
    groups = lax.axis_size("grp")
    block_rows = fine_adjacency.shape[1]
    fine_rows, feature = node_feats.shape
    slots_one = owner_one.shape[0]
    balance_one = slots_one // 2
    slots_two = owner_two.shape[0]
    balance_two = slots_two // 2
    live_one = jnp.arange(slots_one) < count_one[0]
    live_two = jnp.arange(slots_two) < count_two[0]
    place_one, sent_one = pack_layout(owner_one, live_one, groups, balance_one)
    place_two, sent_two = pack_layout(owner_two, live_two, groups, balance_two)
    tables = lax.all_to_all(
        jnp.concatenate([sent_one, sent_two], axis=1), "grp", split_axis=0, concat_axis=0, tiled=True
    )
    rows_one, rows_two = tables[:, : sent_one.shape[1]], tables[:, sent_one.shape[1] :]

    before, after = halo_parts(node_feats, "grp", HALO)
    message0 = block_apply(fine_adjacency, fine_columns, (before, node_feats, after))
    result0, pre_act0, hidden0 = layer_forward(
        node_feats, message0, weight_in[0], weight_out[0], biases[0]
    )
    pooled_one = restrict(
        pool_one, pool_one_columns, jnp.concatenate([result0, cotangent], axis=1), live_one
    )
    got_one = grp_exchange(pack_values(pooled_one, place_one, groups), 0)
    placed_one = place_rows(got_one, rows_one, balance_one)
    own_one, grad_up_one = placed_one[:, :feature], placed_one[:, feature:]
    context_one = lax.all_to_all(
        jnp.broadcast_to(own_one[None], (groups,) + own_one.shape), "grp", 0, 0, tiled=True
    ).reshape(-1, feature)
    message_one = block_apply(adjacency_one, columns_one, context_one)
    result1, pre_act1, hidden1 = layer_forward(
        own_one, message_one, weight_in[1], weight_out[1], biases[1]
    )
    pooled_two = restrict(
        pool_two, pool_two_columns, jnp.concatenate([result1, grad_up_one], axis=1), live_two
    )
    got_two = grp_exchange(pack_values(pooled_two, place_two, groups), 2)
    placed_two = place_rows(got_two, rows_two, balance_two)
    own_two, grad_out_two = placed_two[:, :feature], placed_two[:, feature:]
    context_two = grp_gather(own_two, 3)
    message_two = block_apply(adjacency_two, columns_two, context_two)
    result2, pre_act2, hidden2 = layer_forward(
        own_two, message_two, weight_in[2], weight_out[2], biases[2]
    )
    sums_two, grad_rows_two, grad_ctx_two = layer_backward(
        grad_out_two.astype(jnp.float32),
        own_two,
        message_two,
        hidden2,
        pre_act2,
        weight_in[2],
        weight_out[2],
        adjacency_two,
        columns_two,
        groups * balance_two // block_rows,
    )
    grad_own_two = grad_rows_two + grp_sum_scatter(grad_ctx_two, 4)
    returned_two = grp_exchange(
        pick_rows(jnp.concatenate([result2, grad_own_two.astype(jnp.bfloat16)], axis=1), rows_two), 5
    )
    back_two = unpack_rows(returned_two, place_two, live_two)
    lifted_one = block_transpose(pool_two, pool_two_columns, back_two, balance_one // block_rows)
    up_one = (result1.astype(jnp.float32) + lifted_one[:, :feature]).astype(jnp.bfloat16)
    grad_out_one = grad_up_one.astype(jnp.float32) + lifted_one[:, feature:]
    sums_one, grad_rows_one, grad_ctx_one = layer_backward(
        grad_out_one,
        own_one,
        message_one,
        hidden1,
        pre_act1,
        weight_in[1],
        weight_out[1],
        adjacency_one,
        columns_one,
        groups * balance_one // block_rows,
    )
    grad_own_one = grad_rows_one + grp_sum_scatter(grad_ctx_one, 6)
    returned_one = grp_exchange(
        pick_rows(jnp.concatenate([up_one, grad_own_one.astype(jnp.bfloat16)], axis=1), rows_one), 7
    )
    back_one = unpack_rows(returned_one, place_one, live_one)
    lifted_zero = block_transpose(pool_one, pool_one_columns, back_one, fine_rows // block_rows)
    node_out = (result0.astype(jnp.float32) + lifted_zero[:, :feature]).astype(jnp.bfloat16)
    grad_out_zero = cotangent.astype(jnp.float32) + lifted_zero[:, feature:]
    sums_zero, grad_rows_zero, grad_ctx_zero = layer_backward(
        grad_out_zero,
        node_feats,
        message0,
        hidden0,
        pre_act0,
        weight_in[0],
        weight_out[0],
        fine_adjacency,
        fine_columns,
        (fine_rows + 2 * HALO) // block_rows,
    )
    rim_terms = jnp.concatenate([grad_ctx_zero[:HALO], grad_ctx_zero[HALO + fine_rows :]], axis=0)
    neighbour_terms = with_halo(rim_terms.astype(jnp.bfloat16), (("grp", 0),), HALO).astype(
        rim_terms.dtype
    )
    gathered_total = grad_rows_zero + grad_ctx_zero[HALO : HALO + fine_rows]
    gathered_total = gathered_total.at[:HALO].add(neighbour_terms[:HALO])
    gathered_total = gathered_total.at[fine_rows - HALO :].add(neighbour_terms[3 * HALO :])
    grad_feats = gathered_total.astype(jnp.bfloat16)
    stack_in = jnp.stack([sums_zero[0], sums_one[0], sums_two[0]])
    stack_out = jnp.stack([sums_zero[1], sums_one[1], sums_two[1]])
    stack_bias = jnp.stack([sums_zero[2], sums_one[2], sums_two[2]])
    stack_in, stack_out, stack_bias = all_sum((stack_in, stack_out, stack_bias))
    inv_root = 1.0 / math.sqrt(fine_rows * groups * lax.axis_size("slab"))
    return (node_out, grad_feats, stack_in * inv_root, stack_out * inv_root, stack_bias * inv_root)


def solution(mesh):
    placed = (
        P(("slab", "grp"), None),
        P(("slab", "grp"), None),
        P(("slab", "grp"), None, None),
        P(("slab", "grp"), None),
        P(("slab", "grp"), None, None),
        P(("slab", "grp"), None),
        P(("slab", "grp")),
        P(("slab", "grp")),
        P(("slab", "grp"), None, None),
        P(("slab", "grp"), None),
        P(("slab", "grp"), None, None),
        P(("slab", "grp"), None),
        P(("slab", "grp")),
        P(("slab", "grp")),
        P(("slab", "grp"), None, None),
        P(("slab", "grp"), None),
        P(),
        P(),
        P(),
    )
    return jax.shard_map(
        body,
        mesh=mesh,
        in_specs=placed,
        out_specs=(P(("slab", "grp"), None), P(("slab", "grp"), None), P(), P(), P()),
        check_vma=False,
    )
```

```python
import functools
import math

import jax
import jax.numpy as jnp
from jax import lax
from jax.experimental import pallas as pl
from jax.experimental.pallas import tpu as pltpu
from jax.sharding import PartitionSpec as P

HALO = 512


def with_halo(cells, sides, width):
    for axis, dim in sides:
        count = lax.axis_size(axis)
        ends = count - 1
        head = lax.slice_in_dim(cells, 0, width, axis=dim)
        tail = lax.slice_in_dim(cells, cells.shape[dim] - width, cells.shape[dim], axis=dim)
        cells = jnp.concatenate(
            [
                lax.ppermute(tail, axis, [(i, (i + 1) % count) for i in range(ends)]),
                cells,
                lax.ppermute(head, axis, [((i + 1) % count, i) for i in range(ends)]),
            ],
            axis=dim,
        )
    return cells


def halo_parts(cells, axis, width):
    count = lax.axis_size(axis)
    ends = count - 1
    head = cells[:width]
    tail = cells[cells.shape[0] - width :]
    before = lax.ppermute(tail, axis, [(i, (i + 1) % count) for i in range(ends)])
    after = lax.ppermute(head, axis, [((i + 1) % count, i) for i in range(ends)])
    return before, after


def _per_step(block_count):
    return min(block_count, 8)


def _apply_kernel(cols_ref, m_ref, *refs, k, per_step, blk, pieces_in):
    q_parts, (o_ref, q_ref) = refs[:pieces_in], refs[pieces_in:]
    step = pl.program_id(0)

    @pl.when(step == 0)
    def _():
        at = 0
        for part in q_parts:
            q_ref[at : at + part.shape[0], :] = part[...]
            at += part.shape[0]

    for j in range(per_step):
        r = step * per_step + j
        pieces = [
            q_ref[pl.ds(pl.multiple_of(cols_ref[r * k + i] * blk, blk), blk), :] for i in range(k)
        ]
        stacked = jnp.concatenate(pieces, axis=0)
        res = jnp.dot(m_ref[j], stacked, preferred_element_type=jnp.float32)
        o_ref[j * blk : (j + 1) * blk, :] = res.astype(o_ref.dtype)


def _apply_kernel_rolled(cols_ref, m_ref, *refs, k, per_step, blk, pieces_in):
    q_parts, (o_ref, q_ref) = refs[:pieces_in], refs[pieces_in:]
    step = pl.program_id(0)

    @pl.when(step == 0)
    def _():
        at = 0
        for part in q_parts:
            q_ref[at : at + part.shape[0], :] = part[...]
            at += part.shape[0]

    def one_block(j, carry):
        r = step * per_step + j
        pieces = [
            q_ref[pl.ds(pl.multiple_of(cols_ref[r * k + i] * blk, blk), blk), :] for i in range(k)
        ]
        stacked = jnp.concatenate(pieces, axis=0)
        res = jnp.dot(m_ref[j], stacked, preferred_element_type=jnp.float32)
        o_ref[pl.ds(pl.multiple_of(j * blk, blk), blk), :] = res.astype(o_ref.dtype)
        return carry

    lax.fori_loop(0, per_step, one_block, 0)


def block_apply(blocks, columns, context, out_dtype=jnp.bfloat16):
    block_count, block_rows, span = blocks.shape
    k = columns.shape[1]
    parts = tuple(context) if isinstance(context, (tuple, list)) else (context,)
    feature = parts[0].shape[1]
    rows = sum(p.shape[0] for p in parts)
    per_step = _per_step(block_count)
    body_of = _apply_kernel_rolled if block_count <= 4 else _apply_kernel
    kernel = functools.partial(body_of, k=k, per_step=per_step, blk=block_rows, pieces_in=len(parts))
    return pl.pallas_call(
        kernel,
        out_shape=jax.ShapeDtypeStruct((block_count * block_rows, feature), out_dtype),
        grid_spec=pltpu.PrefetchScalarGridSpec(
            num_scalar_prefetch=1,
            grid=(block_count // per_step,),
            in_specs=[pl.BlockSpec((per_step, block_rows, span), lambda s, c: (s, 0, 0))]
            + [pl.BlockSpec(p.shape, lambda s, c: (0, 0)) for p in parts],
            out_specs=pl.BlockSpec((per_step * block_rows, feature), lambda s, c: (s, 0)),
            scratch_shapes=[pltpu.VMEM((rows, feature), parts[0].dtype)],
        ),
        compiler_params=pltpu.CompilerParams(dimension_semantics=("arbitrary",)),
        cost_estimate=pl.CostEstimate(
            flops=2 * block_count * block_rows * span * feature,
            transcendentals=0,
            bytes_accessed=blocks.size * 2 + rows * feature * 2 + block_count * block_rows * feature * 2,
        ),
    )(columns.reshape(-1), blocks, *parts)


def _apply_t_kernel(cols_ref, m_ref, p_ref, o_ref, *, k, per_step, blk):
    step = pl.program_id(0)

    @pl.when(step == 0)
    def _():
        o_ref[...] = jnp.zeros_like(o_ref)

    for j in range(per_step):
        r = step * per_step + j
        spread = lax.dot_general(
            m_ref[j],
            p_ref[j * blk : (j + 1) * blk, :],
            (((0,), (0,)), ((), ())),
            preferred_element_type=jnp.float32,
        )
        for i in range(k):
            at = pl.multiple_of(cols_ref[r * k + i] * blk, blk)
            o_ref[pl.ds(at, blk), :] += spread[i * blk : (i + 1) * blk]


def _apply_t_kernel_rolled(cols_ref, m_ref, p_ref, o_ref, *, k, per_step, blk):
    step = pl.program_id(0)

    @pl.when(step == 0)
    def _():
        o_ref[...] = jnp.zeros_like(o_ref)

    def one_block(j, carry):
        r = step * per_step + j
        spread = lax.dot_general(
            m_ref[j],
            p_ref[pl.ds(pl.multiple_of(j * blk, blk), blk), :],
            (((0,), (0,)), ((), ())),
            preferred_element_type=jnp.float32,
        )
        for i in range(k):
            at = pl.multiple_of(cols_ref[r * k + i] * blk, blk)
            o_ref[pl.ds(at, blk), :] += spread[i * blk : (i + 1) * blk]
        return carry

    lax.fori_loop(0, per_step, one_block, 0)


def block_transpose(blocks, columns, row_grads, targets):
    block_count, block_rows, span = blocks.shape
    k = columns.shape[1]
    feature = row_grads.shape[1]
    per_step = _per_step(block_count)
    body_of = _apply_t_kernel_rolled if block_count <= 4 else _apply_t_kernel
    kernel = functools.partial(body_of, k=k, per_step=per_step, blk=block_rows)
    return pl.pallas_call(
        kernel,
        out_shape=jax.ShapeDtypeStruct((targets * block_rows, feature), jnp.float32),
        grid_spec=pltpu.PrefetchScalarGridSpec(
            num_scalar_prefetch=1,
            grid=(block_count // per_step,),
            in_specs=[
                pl.BlockSpec((per_step, block_rows, span), lambda s, c: (s, 0, 0)),
                pl.BlockSpec((per_step * block_rows, feature), lambda s, c: (s, 0)),
            ],
            out_specs=pl.BlockSpec((targets * block_rows, feature), lambda s, c: (0, 0)),
        ),
        compiler_params=pltpu.CompilerParams(dimension_semantics=("arbitrary",)),
        cost_estimate=pl.CostEstimate(
            flops=2 * block_count * block_rows * span * feature,
            transcendentals=0,
            bytes_accessed=blocks.size * 2 + row_grads.size * 2 + targets * block_rows * feature * 4,
        ),
    )(columns.reshape(-1), blocks, row_grads.astype(jnp.bfloat16))


def _exchange_kernel(x_ref, o_ref, send_sem, recv_sem, *, axis, n, broadcast):
    me = lax.axis_index(axis)
    barrier = pltpu.get_barrier_semaphore()
    def greet(d, carry):
        pl.semaphore_signal(
            barrier, inc=1, device_id={axis: lax.rem(me + d, n)}, device_id_type=pl.DeviceIdType.MESH
        )
        return carry

    lax.fori_loop(1, n, greet, 0)
    pl.semaphore_wait(barrier, n - 1)

    def copy_to(d):
        peer = lax.rem(me + d, n)
        return pltpu.make_async_remote_copy(
            src_ref=x_ref if broadcast else x_ref.at[peer],
            dst_ref=o_ref.at[me],
            send_sem=send_sem.at[d],
            recv_sem=recv_sem.at[d],
            device_id={axis: peer},
            device_id_type=pl.DeviceIdType.MESH,
        )

    def start(d, carry):
        copy_to(d).start()
        return carry

    def finish(d, carry):
        copy_to(d).wait()
        return carry

    lax.fori_loop(1, n, start, 0)
    o_ref[me] = x_ref[...] if broadcast else x_ref[me]
    lax.fori_loop(1, n, finish, 0)


def grp_exchange(chunks, site, broadcast=False):
    n = lax.axis_size("grp")
    shape = (n,) + chunks.shape if broadcast else chunks.shape
    kernel = functools.partial(_exchange_kernel, axis="grp", n=n, broadcast=broadcast)
    moved = chunks.size * chunks.dtype.itemsize * (n - 1 if broadcast else 1)
    return pl.pallas_call(
        kernel,
        out_shape=jax.ShapeDtypeStruct(shape, chunks.dtype),
        in_specs=[pl.BlockSpec(memory_space=pltpu.VMEM)],
        out_specs=pl.BlockSpec(memory_space=pltpu.VMEM),
        scratch_shapes=[pltpu.SemaphoreType.DMA((n,)), pltpu.SemaphoreType.DMA((n,))],
        compiler_params=pltpu.CompilerParams(collective_id=site, has_side_effects=True),
        cost_estimate=pl.CostEstimate(flops=0, transcendentals=0, bytes_accessed=2 * moved),
    )(chunks)


def grp_gather(rows, site):
    return grp_exchange(rows, site, broadcast=True).reshape(-1, rows.shape[1])


def grp_sum_scatter(values, site):
    groups = lax.axis_size("grp")
    pieces = values.astype(jnp.bfloat16).reshape(groups, -1, values.shape[1])
    got = grp_exchange(pieces, site)
    return jnp.sum(got.astype(jnp.float32), axis=0)


def all_sum(parts):
    axes = ("slab", "grp")
    devices = lax.axis_size("slab") * lax.axis_size("grp")
    flat = jnp.concatenate([p.reshape(-1) for p in parts])
    total = flat.shape[0]
    chunk = -(-total // devices)
    chunk = -(-chunk // 128) * 128
    flat = jnp.pad(flat, (0, devices * chunk - total)).reshape(devices, chunk)
    got = lax.all_to_all(flat, axes, 0, 0, tiled=True)
    mine = jnp.sum(got, axis=0, keepdims=True)
    back = lax.all_to_all(jnp.broadcast_to(mine, (devices, chunk)), axes, 0, 0, tiled=True)
    back = back.reshape(-1)[:total]
    out, at = [], 0
    for p in parts:
        out.append(back[at : at + p.size].reshape(p.shape))
        at += p.size
    return out


def restrict(blocks, columns, source, live_mask):
    pooled = block_apply(blocks, columns, source)
    return jnp.where(live_mask[:, None], pooled, jnp.zeros_like(pooled))


def layer_forward(node_rows, message, weight_in, weight_out, bias_row):
    joined = jnp.concatenate([node_rows, message], axis=1)
    pre_act = jnp.dot(joined, weight_in, preferred_element_type=jnp.float32) + bias_row
    hidden = jax.nn.silu(pre_act).astype(jnp.bfloat16)
    result = node_rows.astype(jnp.float32) + jnp.dot(
        hidden, weight_out, preferred_element_type=jnp.float32
    )
    return (result.astype(jnp.bfloat16), pre_act, hidden)


def layer_backward(
    cotan_rows, node_rows, message, hidden, pre_act, weight_in, weight_out, blocks, columns, targets
):
    grad_low = cotan_rows.astype(jnp.bfloat16)
    delta_out = lax.dot_general(
        hidden, grad_low, (((0,), (0,)), ((), ())), preferred_element_type=jnp.float32
    )
    grad_hidden = lax.dot_general(
        grad_low, weight_out, (((1,), (1,)), ((), ())), preferred_element_type=jnp.float32
    )
    sigmoid_pre = jax.nn.sigmoid(pre_act)
    grad_pre = grad_hidden * sigmoid_pre * (1.0 + pre_act * (1.0 - sigmoid_pre))
    grad_pre_low = grad_pre.astype(jnp.bfloat16)
    delta_bias = jnp.sum(grad_pre, axis=0)
    joined = jnp.concatenate([node_rows, message], axis=1)
    delta_in = lax.dot_general(
        joined, grad_pre_low, (((0,), (0,)), ((), ())), preferred_element_type=jnp.float32
    )
    grad_joined = lax.dot_general(
        grad_pre_low, weight_in, (((1,), (1,)), ((), ())), preferred_element_type=jnp.float32
    )
    feature = node_rows.shape[1]
    grad_rows = cotan_rows + grad_joined[:, :feature]
    grad_message = grad_joined[:, feature:].astype(jnp.bfloat16)
    grad_context = block_transpose(blocks, columns, grad_message, targets)
    return ((delta_in, delta_out, delta_bias), grad_rows, grad_context)


def pack_layout(owners, live_mask, groups, balance):
    slot_count = owners.shape[0]
    capacity = slot_count // groups
    target = owners // balance
    onehot = (
        (target[:, None] == jnp.arange(groups, dtype=jnp.int32)[None, :]) & live_mask[:, None]
    ).astype(jnp.int32)
    slot_ranks = jnp.sum(onehot * jnp.cumsum(onehot, axis=0), axis=1) - 1
    place_at = jnp.where(live_mask, target * capacity + slot_ranks, groups * capacity)
    row_table = (
        jnp.full((groups * capacity,), balance, jnp.int32)
        .at[place_at]
        .set(owners % balance, mode="drop")
    )
    return (place_at, row_table.reshape(groups, capacity))


def pack_values(values, place_at, groups):
    capacity = values.shape[0] // groups
    buffer = (
        jnp.zeros((groups * capacity, values.shape[1]), values.dtype)
        .at[place_at]
        .set(values, mode="drop")
    )
    return buffer.reshape(groups, capacity, values.shape[1])


def place_rows(received, row_table, balance):
    feature = received.shape[-1]
    flat = received.reshape(-1, feature)
    return (
        jnp.zeros((balance, feature), received.dtype)
        .at[row_table.reshape(-1)]
        .set(flat, mode="drop")
    )


def pick_rows(table, row_table):
    balance = table.shape[0]
    flat = row_table.reshape(-1)
    taken = jnp.take(table, jnp.clip(flat, 0, balance - 1), axis=0)
    taken = jnp.where((flat < balance)[:, None], taken, jnp.zeros_like(taken))
    return taken.reshape(row_table.shape[0], row_table.shape[1], table.shape[1])


def unpack_rows(received, place_at, live_mask):
    feature = received.shape[-1]
    flat = received.reshape(-1, feature)
    taken = jnp.take(flat, jnp.clip(place_at, 0, flat.shape[0] - 1), axis=0)
    return jnp.where(live_mask[:, None], taken, jnp.zeros_like(taken))


def body(
    node_feats,
    cotangent,
    fine_adjacency,
    fine_columns,
    pool_one,
    pool_one_columns,
    count_one,
    owner_one,
    adjacency_one,
    columns_one,
    pool_two,
    pool_two_columns,
    count_two,
    owner_two,
    adjacency_two,
    columns_two,
    weight_in,
    weight_out,
    biases,
):
    groups = lax.axis_size("grp")
    block_rows = fine_adjacency.shape[1]
    fine_rows, feature = node_feats.shape
    slots_one = owner_one.shape[0]
    balance_one = slots_one // 2
    slots_two = owner_two.shape[0]
    balance_two = slots_two // 2
    live_one = jnp.arange(slots_one) < count_one[0]
    live_two = jnp.arange(slots_two) < count_two[0]
    place_one, sent_one = pack_layout(owner_one, live_one, groups, balance_one)
    place_two, sent_two = pack_layout(owner_two, live_two, groups, balance_two)
    tables = lax.all_to_all(
        jnp.concatenate([sent_one, sent_two], axis=1), "grp", split_axis=0, concat_axis=0, tiled=True
    )
    rows_one, rows_two = tables[:, : sent_one.shape[1]], tables[:, sent_one.shape[1] :]

    before, after = halo_parts(node_feats, "grp", HALO)
    message0 = block_apply(fine_adjacency, fine_columns, (before, node_feats, after))
    result0, pre_act0, hidden0 = layer_forward(
        node_feats, message0, weight_in[0], weight_out[0], biases[0]
    )
    pooled_one = restrict(
        pool_one, pool_one_columns, jnp.concatenate([result0, cotangent], axis=1), live_one
    )
    got_one = grp_exchange(pack_values(pooled_one, place_one, groups), 0)
    placed_one = place_rows(got_one, rows_one, balance_one)
    own_one, grad_up_one = placed_one[:, :feature], placed_one[:, feature:]
    context_one = lax.all_to_all(
        jnp.broadcast_to(own_one[None], (groups,) + own_one.shape), "grp", 0, 0, tiled=True
    ).reshape(-1, feature)
    message_one = block_apply(adjacency_one, columns_one, context_one)
    result1, pre_act1, hidden1 = layer_forward(
        own_one, message_one, weight_in[1], weight_out[1], biases[1]
    )
    pooled_two = restrict(
        pool_two, pool_two_columns, jnp.concatenate([result1, grad_up_one], axis=1), live_two
    )
    got_two = grp_exchange(pack_values(pooled_two, place_two, groups), 2)
    placed_two = place_rows(got_two, rows_two, balance_two)
    own_two, grad_out_two = placed_two[:, :feature], placed_two[:, feature:]
    context_two = grp_gather(own_two, 3)
    message_two = block_apply(adjacency_two, columns_two, context_two)
    result2, pre_act2, hidden2 = layer_forward(
        own_two, message_two, weight_in[2], weight_out[2], biases[2]
    )
    sums_two, grad_rows_two, grad_ctx_two = layer_backward(
        grad_out_two.astype(jnp.float32),
        own_two,
        message_two,
        hidden2,
        pre_act2,
        weight_in[2],
        weight_out[2],
        adjacency_two,
        columns_two,
        groups * balance_two // block_rows,
    )
    grad_own_two = grad_rows_two + grp_sum_scatter(grad_ctx_two, 4)
    returned_two = grp_exchange(
        pick_rows(jnp.concatenate([result2, grad_own_two.astype(jnp.bfloat16)], axis=1), rows_two), 5
    )
    back_two = unpack_rows(returned_two, place_two, live_two)
    lifted_one = block_transpose(pool_two, pool_two_columns, back_two, balance_one // block_rows)
    up_one = (result1.astype(jnp.float32) + lifted_one[:, :feature]).astype(jnp.bfloat16)
    grad_out_one = grad_up_one.astype(jnp.float32) + lifted_one[:, feature:]
    sums_one, grad_rows_one, grad_ctx_one = layer_backward(
        grad_out_one,
        own_one,
        message_one,
        hidden1,
        pre_act1,
        weight_in[1],
        weight_out[1],
        adjacency_one,
        columns_one,
        groups * balance_one // block_rows,
    )
    grad_own_one = grad_rows_one + grp_sum_scatter(grad_ctx_one, 6)
    returned_one = grp_exchange(
        pick_rows(jnp.concatenate([up_one, grad_own_one.astype(jnp.bfloat16)], axis=1), rows_one), 7
    )
    back_one = unpack_rows(returned_one, place_one, live_one)
    lifted_zero = block_transpose(pool_one, pool_one_columns, back_one, fine_rows // block_rows)
    node_out = (result0.astype(jnp.float32) + lifted_zero[:, :feature]).astype(jnp.bfloat16)
    grad_out_zero = cotangent.astype(jnp.float32) + lifted_zero[:, feature:]
    sums_zero, grad_rows_zero, grad_ctx_zero = layer_backward(
        grad_out_zero,
        node_feats,
        message0,
        hidden0,
        pre_act0,
        weight_in[0],
        weight_out[0],
        fine_adjacency,
        fine_columns,
        (fine_rows + 2 * HALO) // block_rows,
    )
    rim_terms = jnp.concatenate([grad_ctx_zero[:HALO], grad_ctx_zero[HALO + fine_rows :]], axis=0)
    neighbour_terms = with_halo(rim_terms.astype(jnp.bfloat16), (("grp", 0),), HALO).astype(
        rim_terms.dtype
    )
    gathered_total = grad_rows_zero + grad_ctx_zero[HALO : HALO + fine_rows]
    gathered_total = gathered_total.at[:HALO].add(neighbour_terms[:HALO])
    gathered_total = gathered_total.at[fine_rows - HALO :].add(neighbour_terms[3 * HALO :])
    grad_feats = gathered_total.astype(jnp.bfloat16)
    stack_in = jnp.stack([sums_zero[0], sums_one[0], sums_two[0]])
    stack_out = jnp.stack([sums_zero[1], sums_one[1], sums_two[1]])
    stack_bias = jnp.stack([sums_zero[2], sums_one[2], sums_two[2]])
    stack_in, stack_out, stack_bias = all_sum((stack_in, stack_out, stack_bias))
    inv_root = 1.0 / math.sqrt(fine_rows * groups * lax.axis_size("slab"))
    return (node_out, grad_feats, stack_in * inv_root, stack_out * inv_root, stack_bias * inv_root)


def solution(mesh):
    placed = (
        P(("slab", "grp"), None),
        P(("slab", "grp"), None),
        P(("slab", "grp"), None, None),
        P(("slab", "grp"), None),
        P(("slab", "grp"), None, None),
        P(("slab", "grp"), None),
        P(("slab", "grp")),
        P(("slab", "grp")),
        P(("slab", "grp"), None, None),
        P(("slab", "grp"), None),
        P(("slab", "grp"), None, None),
        P(("slab", "grp"), None),
        P(("slab", "grp")),
        P(("slab", "grp")),
        P(("slab", "grp"), None, None),
        P(("slab", "grp"), None),
        P(),
        P(),
        P(),
    )
    return jax.shard_map(
        body,
        mesh=mesh,
        in_specs=placed,
        out_specs=(P(("slab", "grp"), None), P(("slab", "grp"), None), P(), P(), P()),
        check_vma=False,
    )
```

```python
import functools
import math

import jax
import jax.numpy as jnp
from jax import lax
from jax.experimental import pallas as pl
from jax.experimental.pallas import tpu as pltpu
from jax.sharding import PartitionSpec as P

HALO = 512


def with_halo(cells, sides, width):
    for axis, dim in sides:
        count = lax.axis_size(axis)
        ends = count - 1
        head = lax.slice_in_dim(cells, 0, width, axis=dim)
        tail = lax.slice_in_dim(cells, cells.shape[dim] - width, cells.shape[dim], axis=dim)
        cells = jnp.concatenate(
            [
                lax.ppermute(tail, axis, [(i, (i + 1) % count) for i in range(ends)]),
                cells,
                lax.ppermute(head, axis, [((i + 1) % count, i) for i in range(ends)]),
            ],
            axis=dim,
        )
    return cells


def halo_parts(cells, axis, width):
    count = lax.axis_size(axis)
    ends = count - 1
    head = cells[:width]
    tail = cells[cells.shape[0] - width :]
    before = lax.ppermute(tail, axis, [(i, (i + 1) % count) for i in range(ends)])
    after = lax.ppermute(head, axis, [((i + 1) % count, i) for i in range(ends)])
    return before, after


def _per_step(block_count):
    return min(block_count, 8)


def _apply_kernel(cols_ref, m_ref, *refs, k, per_step, blk, pieces_in):
    q_parts, (o_ref, q_ref) = refs[:pieces_in], refs[pieces_in:]
    step = pl.program_id(0)

    @pl.when(step == 0)
    def _():
        at = 0
        for part in q_parts:
            q_ref[at : at + part.shape[0], :] = part[...]
            at += part.shape[0]

    for j in range(per_step):
        r = step * per_step + j
        pieces = [
            q_ref[pl.ds(pl.multiple_of(cols_ref[r * k + i] * blk, blk), blk), :] for i in range(k)
        ]
        stacked = jnp.concatenate(pieces, axis=0)
        res = jnp.dot(m_ref[j], stacked, preferred_element_type=jnp.float32)
        o_ref[j * blk : (j + 1) * blk, :] = res.astype(o_ref.dtype)


def block_apply(blocks, columns, context, out_dtype=jnp.bfloat16):
    block_count, block_rows, span = blocks.shape
    k = columns.shape[1]
    parts = tuple(context) if isinstance(context, (tuple, list)) else (context,)
    feature = parts[0].shape[1]
    rows = sum(p.shape[0] for p in parts)
    per_step = _per_step(block_count)
    kernel = functools.partial(
        _apply_kernel, k=k, per_step=per_step, blk=block_rows, pieces_in=len(parts)
    )
    return pl.pallas_call(
        kernel,
        out_shape=jax.ShapeDtypeStruct((block_count * block_rows, feature), out_dtype),
        grid_spec=pltpu.PrefetchScalarGridSpec(
            num_scalar_prefetch=1,
            grid=(block_count // per_step,),
            in_specs=[pl.BlockSpec((per_step, block_rows, span), lambda s, c: (s, 0, 0))]
            + [pl.BlockSpec(p.shape, lambda s, c: (0, 0)) for p in parts],
            out_specs=pl.BlockSpec((per_step * block_rows, feature), lambda s, c: (s, 0)),
            scratch_shapes=[pltpu.VMEM((rows, feature), parts[0].dtype)],
        ),
        compiler_params=pltpu.CompilerParams(dimension_semantics=("arbitrary",)),
        cost_estimate=pl.CostEstimate(
            flops=2 * block_count * block_rows * span * feature,
            transcendentals=0,
            bytes_accessed=blocks.size * 2 + rows * feature * 2 + block_count * block_rows * feature * 2,
        ),
    )(columns.reshape(-1), blocks, *parts)


def _apply_t_kernel(cols_ref, m_ref, p_ref, o_ref, *, k, per_step, blk):
    step = pl.program_id(0)

    @pl.when(step == 0)
    def _():
        o_ref[...] = jnp.zeros_like(o_ref)

    for j in range(per_step):
        r = step * per_step + j
        spread = lax.dot_general(
            m_ref[j],
            p_ref[j * blk : (j + 1) * blk, :],
            (((0,), (0,)), ((), ())),
            preferred_element_type=jnp.float32,
        )
        for i in range(k):
            at = pl.multiple_of(cols_ref[r * k + i] * blk, blk)
            o_ref[pl.ds(at, blk), :] += spread[i * blk : (i + 1) * blk]


def block_transpose(blocks, columns, row_grads, targets):
    block_count, block_rows, span = blocks.shape
    k = columns.shape[1]
    feature = row_grads.shape[1]
    per_step = _per_step(block_count)
    kernel = functools.partial(_apply_t_kernel, k=k, per_step=per_step, blk=block_rows)
    return pl.pallas_call(
        kernel,
        out_shape=jax.ShapeDtypeStruct((targets * block_rows, feature), jnp.float32),
        grid_spec=pltpu.PrefetchScalarGridSpec(
            num_scalar_prefetch=1,
            grid=(block_count // per_step,),
            in_specs=[
                pl.BlockSpec((per_step, block_rows, span), lambda s, c: (s, 0, 0)),
                pl.BlockSpec((per_step * block_rows, feature), lambda s, c: (s, 0)),
            ],
            out_specs=pl.BlockSpec((targets * block_rows, feature), lambda s, c: (0, 0)),
        ),
        compiler_params=pltpu.CompilerParams(dimension_semantics=("arbitrary",)),
        cost_estimate=pl.CostEstimate(
            flops=2 * block_count * block_rows * span * feature,
            transcendentals=0,
            bytes_accessed=blocks.size * 2 + row_grads.size * 2 + targets * block_rows * feature * 4,
        ),
    )(columns.reshape(-1), blocks, row_grads.astype(jnp.bfloat16))


def _exchange_kernel(*refs, axis, n, broadcast, count):
    x_refs, o_refs = refs[:count], refs[count : 2 * count]
    send_sem, recv_sem = refs[2 * count :]
    me = lax.axis_index(axis)
    barrier = pltpu.get_barrier_semaphore()

    def greet(d, carry):
        pl.semaphore_signal(
            barrier, inc=1, device_id={axis: lax.rem(me + d, n)}, device_id_type=pl.DeviceIdType.MESH
        )
        return carry

    lax.fori_loop(1, n, greet, 0)
    pl.semaphore_wait(barrier, n - 1)

    def copy_to(d, t):
        peer = lax.rem(me + d, n)
        return pltpu.make_async_remote_copy(
            src_ref=x_refs[t] if broadcast else x_refs[t].at[peer],
            dst_ref=o_refs[t].at[me],
            send_sem=send_sem.at[t, d],
            recv_sem=recv_sem.at[t, d],
            device_id={axis: peer},
            device_id_type=pl.DeviceIdType.MESH,
        )

    def start(d, carry):
        for t in range(count):
            copy_to(d, t).start()
        return carry

    def finish(d, carry):
        for t in range(count):
            copy_to(d, t).wait()
        return carry

    lax.fori_loop(1, n, start, 0)
    for t in range(count):
        o_refs[t][me] = x_refs[t][...] if broadcast else x_refs[t][me]
    lax.fori_loop(1, n, finish, 0)


def grp_exchange(chunks, site, broadcast=False):
    n = lax.axis_size("grp")
    arrays = tuple(chunks) if isinstance(chunks, (tuple, list)) else (chunks,)
    shapes = [(n,) + c.shape if broadcast else c.shape for c in arrays]
    kernel = functools.partial(
        _exchange_kernel, axis="grp", n=n, broadcast=broadcast, count=len(arrays)
    )
    moved = sum(c.size * c.dtype.itemsize for c in arrays) * (n - 1 if broadcast else 1)
    out = pl.pallas_call(
        kernel,
        out_shape=tuple(jax.ShapeDtypeStruct(s, c.dtype) for s, c in zip(shapes, arrays)),
        in_specs=[pl.BlockSpec(memory_space=pltpu.VMEM)] * len(arrays),
        out_specs=tuple(pl.BlockSpec(memory_space=pltpu.VMEM) for _ in arrays),
        scratch_shapes=[
            pltpu.SemaphoreType.DMA((len(arrays), n)),
            pltpu.SemaphoreType.DMA((len(arrays), n)),
        ],
        compiler_params=pltpu.CompilerParams(collective_id=site, has_side_effects=True),
        cost_estimate=pl.CostEstimate(flops=0, transcendentals=0, bytes_accessed=2 * moved),
    )(*arrays)
    return out if isinstance(chunks, (tuple, list)) else out[0]


def grp_gather(rows, site):
    return grp_exchange(rows, site, broadcast=True).reshape(-1, rows.shape[1])


def grp_sum_scatter(values, site):
    groups = lax.axis_size("grp")
    pieces = values.astype(jnp.bfloat16).reshape(groups, -1, values.shape[1])
    got = grp_exchange(pieces, site)
    return jnp.sum(got.astype(jnp.float32), axis=0)


def all_sum(parts):
    axes = ("slab", "grp")
    devices = lax.axis_size("slab") * lax.axis_size("grp")
    flat = jnp.concatenate([p.reshape(-1) for p in parts])
    total = flat.shape[0]
    chunk = -(-total // devices)
    chunk = -(-chunk // 128) * 128
    flat = jnp.pad(flat, (0, devices * chunk - total)).reshape(devices, chunk)
    got = lax.all_to_all(flat, axes, 0, 0, tiled=True)
    mine = jnp.sum(got, axis=0, keepdims=True)
    back = lax.all_to_all(jnp.broadcast_to(mine, (devices, chunk)), axes, 0, 0, tiled=True)
    back = back.reshape(-1)[:total]
    out, at = [], 0
    for p in parts:
        out.append(back[at : at + p.size].reshape(p.shape))
        at += p.size
    return out


def restrict(blocks, columns, source, live_mask):
    pooled = block_apply(blocks, columns, source)
    return jnp.where(live_mask[:, None], pooled, jnp.zeros_like(pooled))


def layer_forward(node_rows, message, weight_in, weight_out, bias_row):
    joined = jnp.concatenate([node_rows, message], axis=1)
    pre_act = jnp.dot(joined, weight_in, preferred_element_type=jnp.float32) + bias_row
    hidden = jax.nn.silu(pre_act).astype(jnp.bfloat16)
    result = node_rows.astype(jnp.float32) + jnp.dot(
        hidden, weight_out, preferred_element_type=jnp.float32
    )
    return (result.astype(jnp.bfloat16), pre_act, hidden)


def layer_backward(
    cotan_rows, node_rows, message, hidden, pre_act, weight_in, weight_out, blocks, columns, targets
):
    grad_low = cotan_rows.astype(jnp.bfloat16)
    delta_out = lax.dot_general(
        hidden, grad_low, (((0,), (0,)), ((), ())), preferred_element_type=jnp.float32
    )
    grad_hidden = lax.dot_general(
        grad_low, weight_out, (((1,), (1,)), ((), ())), preferred_element_type=jnp.float32
    )
    sigmoid_pre = jax.nn.sigmoid(pre_act)
    grad_pre = grad_hidden * sigmoid_pre * (1.0 + pre_act * (1.0 - sigmoid_pre))
    grad_pre_low = grad_pre.astype(jnp.bfloat16)
    delta_bias = jnp.sum(grad_pre, axis=0)
    joined = jnp.concatenate([node_rows, message], axis=1)
    delta_in = lax.dot_general(
        joined, grad_pre_low, (((0,), (0,)), ((), ())), preferred_element_type=jnp.float32
    )
    grad_joined = lax.dot_general(
        grad_pre_low, weight_in, (((1,), (1,)), ((), ())), preferred_element_type=jnp.float32
    )
    feature = node_rows.shape[1]
    grad_rows = cotan_rows + grad_joined[:, :feature]
    grad_message = grad_joined[:, feature:].astype(jnp.bfloat16)
    grad_context = block_transpose(blocks, columns, grad_message, targets)
    return ((delta_in, delta_out, delta_bias), grad_rows, grad_context)


def pack_layout(owners, live_mask, groups, balance):
    slot_count = owners.shape[0]
    capacity = slot_count // groups
    target = owners // balance
    onehot = (
        (target[:, None] == jnp.arange(groups, dtype=jnp.int32)[None, :]) & live_mask[:, None]
    ).astype(jnp.int32)
    slot_ranks = jnp.sum(onehot * jnp.cumsum(onehot, axis=0), axis=1) - 1
    place_at = jnp.where(live_mask, target * capacity + slot_ranks, groups * capacity)
    row_table = (
        jnp.full((groups * capacity,), balance, jnp.int32)
        .at[place_at]
        .set(owners % balance, mode="drop")
    )
    return (place_at, row_table.reshape(groups, capacity))


def pack_values(values, place_at, groups):
    capacity = values.shape[0] // groups
    buffer = (
        jnp.zeros((groups * capacity, values.shape[1]), values.dtype)
        .at[place_at]
        .set(values, mode="drop")
    )
    return buffer.reshape(groups, capacity, values.shape[1])


def place_rows(received, row_table, balance):
    feature = received.shape[-1]
    flat = received.reshape(-1, feature)
    return (
        jnp.zeros((balance, feature), received.dtype)
        .at[row_table.reshape(-1)]
        .set(flat, mode="drop")
    )


def pick_rows(table, row_table):
    balance = table.shape[0]
    flat = row_table.reshape(-1)
    taken = jnp.take(table, jnp.clip(flat, 0, balance - 1), axis=0)
    taken = jnp.where((flat < balance)[:, None], taken, jnp.zeros_like(taken))
    return taken.reshape(row_table.shape[0], row_table.shape[1], table.shape[1])


def unpack_rows(received, place_at, live_mask):
    feature = received.shape[-1]
    flat = received.reshape(-1, feature)
    taken = jnp.take(flat, jnp.clip(place_at, 0, flat.shape[0] - 1), axis=0)
    return jnp.where(live_mask[:, None], taken, jnp.zeros_like(taken))


def body(
    node_feats,
    cotangent,
    fine_adjacency,
    fine_columns,
    pool_one,
    pool_one_columns,
    count_one,
    owner_one,
    adjacency_one,
    columns_one,
    pool_two,
    pool_two_columns,
    count_two,
    owner_two,
    adjacency_two,
    columns_two,
    weight_in,
    weight_out,
    biases,
):
    groups = lax.axis_size("grp")
    block_rows = fine_adjacency.shape[1]
    fine_rows, feature = node_feats.shape
    slots_one = owner_one.shape[0]
    balance_one = slots_one // 2
    slots_two = owner_two.shape[0]
    balance_two = slots_two // 2
    live_one = jnp.arange(slots_one) < count_one[0]
    live_two = jnp.arange(slots_two) < count_two[0]
    place_one, sent_one = pack_layout(owner_one, live_one, groups, balance_one)
    place_two, sent_two = pack_layout(owner_two, live_two, groups, balance_two)

    before, after = halo_parts(node_feats, "grp", HALO)
    message0 = block_apply(fine_adjacency, fine_columns, (before, node_feats, after))
    result0, pre_act0, hidden0 = layer_forward(
        node_feats, message0, weight_in[0], weight_out[0], biases[0]
    )
    pooled_one = restrict(
        pool_one, pool_one_columns, jnp.concatenate([result0, cotangent], axis=1), live_one
    )
    table_width = sent_one.shape[1] + sent_two.shape[1]
    lanes = -(-table_width // 128) * 128
    tables = jnp.pad(jnp.concatenate([sent_one, sent_two], axis=1), ((0, 0), (0, lanes - table_width)))
    got_one, got_tables = grp_exchange(
        (
            pack_values(pooled_one, place_one, groups),
            jnp.broadcast_to(tables[:, None, :], (groups, 8, lanes)),
        ),
        0,
    )
    rows_one = got_tables[:, 0, : sent_one.shape[1]]
    rows_two = got_tables[:, 0, sent_one.shape[1] : table_width]
    placed_one = place_rows(got_one, rows_one, balance_one)
    own_one, grad_up_one = placed_one[:, :feature], placed_one[:, feature:]
    context_one = lax.all_to_all(
        jnp.broadcast_to(own_one[None], (groups,) + own_one.shape), "grp", 0, 0, tiled=True
    ).reshape(-1, feature)
    message_one = block_apply(adjacency_one, columns_one, context_one)
    result1, pre_act1, hidden1 = layer_forward(
        own_one, message_one, weight_in[1], weight_out[1], biases[1]
    )
    pooled_two = restrict(
        pool_two, pool_two_columns, jnp.concatenate([result1, grad_up_one], axis=1), live_two
    )
    got_two = grp_exchange(pack_values(pooled_two, place_two, groups), 2)
    placed_two = place_rows(got_two, rows_two, balance_two)
    own_two, grad_out_two = placed_two[:, :feature], placed_two[:, feature:]
    context_two = grp_gather(own_two, 3)
    message_two = block_apply(adjacency_two, columns_two, context_two)
    result2, pre_act2, hidden2 = layer_forward(
        own_two, message_two, weight_in[2], weight_out[2], biases[2]
    )
    sums_two, grad_rows_two, grad_ctx_two = layer_backward(
        grad_out_two.astype(jnp.float32),
        own_two,
        message_two,
        hidden2,
        pre_act2,
        weight_in[2],
        weight_out[2],
        adjacency_two,
        columns_two,
        groups * balance_two // block_rows,
    )
    grad_own_two = grad_rows_two + grp_sum_scatter(grad_ctx_two, 4)
    returned_two = grp_exchange(
        pick_rows(jnp.concatenate([result2, grad_own_two.astype(jnp.bfloat16)], axis=1), rows_two), 5
    )
    back_two = unpack_rows(returned_two, place_two, live_two)
    lifted_one = block_transpose(pool_two, pool_two_columns, back_two, balance_one // block_rows)
    up_one = (result1.astype(jnp.float32) + lifted_one[:, :feature]).astype(jnp.bfloat16)
    grad_out_one = grad_up_one.astype(jnp.float32) + lifted_one[:, feature:]
    sums_one, grad_rows_one, grad_ctx_one = layer_backward(
        grad_out_one,
        own_one,
        message_one,
        hidden1,
        pre_act1,
        weight_in[1],
        weight_out[1],
        adjacency_one,
        columns_one,
        groups * balance_one // block_rows,
    )
    grad_own_one = grad_rows_one + grp_sum_scatter(grad_ctx_one, 6)
    returned_one = grp_exchange(
        pick_rows(jnp.concatenate([up_one, grad_own_one.astype(jnp.bfloat16)], axis=1), rows_one), 7
    )
    back_one = unpack_rows(returned_one, place_one, live_one)
    lifted_zero = block_transpose(pool_one, pool_one_columns, back_one, fine_rows // block_rows)
    node_out = (result0.astype(jnp.float32) + lifted_zero[:, :feature]).astype(jnp.bfloat16)
    grad_out_zero = cotangent.astype(jnp.float32) + lifted_zero[:, feature:]
    sums_zero, grad_rows_zero, grad_ctx_zero = layer_backward(
        grad_out_zero,
        node_feats,
        message0,
        hidden0,
        pre_act0,
        weight_in[0],
        weight_out[0],
        fine_adjacency,
        fine_columns,
        (fine_rows + 2 * HALO) // block_rows,
    )
    rim_terms = jnp.concatenate([grad_ctx_zero[:HALO], grad_ctx_zero[HALO + fine_rows :]], axis=0)
    neighbour_terms = with_halo(rim_terms.astype(jnp.bfloat16), (("grp", 0),), HALO).astype(
        rim_terms.dtype
    )
    gathered_total = grad_rows_zero + grad_ctx_zero[HALO : HALO + fine_rows]
    gathered_total = gathered_total.at[:HALO].add(neighbour_terms[:HALO])
    gathered_total = gathered_total.at[fine_rows - HALO :].add(neighbour_terms[3 * HALO :])
    grad_feats = gathered_total.astype(jnp.bfloat16)
    stack_in = jnp.stack([sums_zero[0], sums_one[0], sums_two[0]])
    stack_out = jnp.stack([sums_zero[1], sums_one[1], sums_two[1]])
    stack_bias = jnp.stack([sums_zero[2], sums_one[2], sums_two[2]])
    stack_in, stack_out, stack_bias = all_sum((stack_in, stack_out, stack_bias))
    inv_root = 1.0 / math.sqrt(fine_rows * groups * lax.axis_size("slab"))
    return (node_out, grad_feats, stack_in * inv_root, stack_out * inv_root, stack_bias * inv_root)


def solution(mesh):
    placed = (
        P(("slab", "grp"), None),
        P(("slab", "grp"), None),
        P(("slab", "grp"), None, None),
        P(("slab", "grp"), None),
        P(("slab", "grp"), None, None),
        P(("slab", "grp"), None),
        P(("slab", "grp")),
        P(("slab", "grp")),
        P(("slab", "grp"), None, None),
        P(("slab", "grp"), None),
        P(("slab", "grp"), None, None),
        P(("slab", "grp"), None),
        P(("slab", "grp")),
        P(("slab", "grp")),
        P(("slab", "grp"), None, None),
        P(("slab", "grp"), None),
        P(),
        P(),
        P(),
    )
    return jax.shard_map(
        body,
        mesh=mesh,
        in_specs=placed,
        out_specs=(P(("slab", "grp"), None), P(("slab", "grp"), None), P(), P(), P()),
        check_vma=False,
    )
```

```python
import functools
import math

import jax
import jax.numpy as jnp
from jax import lax
from jax.experimental import pallas as pl
from jax.experimental.pallas import tpu as pltpu
from jax.sharding import PartitionSpec as P

HALO = 512


def with_halo(cells, sides, width):
    for axis, dim in sides:
        count = lax.axis_size(axis)
        ends = count - 1
        head = lax.slice_in_dim(cells, 0, width, axis=dim)
        tail = lax.slice_in_dim(cells, cells.shape[dim] - width, cells.shape[dim], axis=dim)
        cells = jnp.concatenate(
            [
                lax.ppermute(tail, axis, [(i, (i + 1) % count) for i in range(ends)]),
                cells,
                lax.ppermute(head, axis, [((i + 1) % count, i) for i in range(ends)]),
            ],
            axis=dim,
        )
    return cells


def halo_parts(cells, axis, width):
    count = lax.axis_size(axis)
    ends = count - 1
    head = cells[:width]
    tail = cells[cells.shape[0] - width :]
    before = lax.ppermute(tail, axis, [(i, (i + 1) % count) for i in range(ends)])
    after = lax.ppermute(head, axis, [((i + 1) % count, i) for i in range(ends)])
    return before, after


def _per_step(block_count):
    return min(block_count, 8)


def _apply_kernel(cols_ref, m_ref, *refs, k, per_step, blk, pieces_in):
    q_parts, (o_ref, q_ref) = refs[:pieces_in], refs[pieces_in:]
    step = pl.program_id(0)

    @pl.when(step == 0)
    def _():
        at = 0
        for part in q_parts:
            q_ref[at : at + part.shape[0], :] = part[...]
            at += part.shape[0]

    for j in range(per_step):
        r = step * per_step + j
        pieces = [
            q_ref[pl.ds(pl.multiple_of(cols_ref[r * k + i] * blk, blk), blk), :] for i in range(k)
        ]
        stacked = jnp.concatenate(pieces, axis=0)
        res = jnp.dot(m_ref[j], stacked, preferred_element_type=jnp.float32)
        o_ref[j * blk : (j + 1) * blk, :] = res.astype(o_ref.dtype)


def block_apply(blocks, columns, context, out_dtype=jnp.bfloat16):
    block_count, block_rows, span = blocks.shape
    k = columns.shape[1]
    parts = tuple(context) if isinstance(context, (tuple, list)) else (context,)
    feature = parts[0].shape[1]
    rows = sum(p.shape[0] for p in parts)
    per_step = _per_step(block_count)
    kernel = functools.partial(
        _apply_kernel, k=k, per_step=per_step, blk=block_rows, pieces_in=len(parts)
    )
    return pl.pallas_call(
        kernel,
        out_shape=jax.ShapeDtypeStruct((block_count * block_rows, feature), out_dtype),
        grid_spec=pltpu.PrefetchScalarGridSpec(
            num_scalar_prefetch=1,
            grid=(block_count // per_step,),
            in_specs=[pl.BlockSpec((per_step, block_rows, span), lambda s, c: (s, 0, 0))]
            + [pl.BlockSpec(p.shape, lambda s, c: (0, 0)) for p in parts],
            out_specs=pl.BlockSpec((per_step * block_rows, feature), lambda s, c: (s, 0)),
            scratch_shapes=[pltpu.VMEM((rows, feature), parts[0].dtype)],
        ),
        compiler_params=pltpu.CompilerParams(dimension_semantics=("arbitrary",)),
        cost_estimate=pl.CostEstimate(
            flops=2 * block_count * block_rows * span * feature,
            transcendentals=0,
            bytes_accessed=blocks.size * 2 + rows * feature * 2 + block_count * block_rows * feature * 2,
        ),
    )(columns.reshape(-1), blocks, *parts)


def _apply_t_kernel(cols_ref, m_ref, p_ref, o_ref, *, k, per_step, blk):
    step = pl.program_id(0)

    @pl.when(step == 0)
    def _():
        o_ref[...] = jnp.zeros_like(o_ref)

    for j in range(per_step):
        r = step * per_step + j
        spread = lax.dot_general(
            m_ref[j],
            p_ref[j * blk : (j + 1) * blk, :],
            (((0,), (0,)), ((), ())),
            preferred_element_type=jnp.float32,
        )
        for i in range(k):
            at = pl.multiple_of(cols_ref[r * k + i] * blk, blk)
            o_ref[pl.ds(at, blk), :] += spread[i * blk : (i + 1) * blk]


def block_transpose(blocks, columns, row_grads, targets):
    block_count, block_rows, span = blocks.shape
    k = columns.shape[1]
    feature = row_grads.shape[1]
    per_step = _per_step(block_count)
    kernel = functools.partial(_apply_t_kernel, k=k, per_step=per_step, blk=block_rows)
    return pl.pallas_call(
        kernel,
        out_shape=jax.ShapeDtypeStruct((targets * block_rows, feature), jnp.float32),
        grid_spec=pltpu.PrefetchScalarGridSpec(
            num_scalar_prefetch=1,
            grid=(block_count // per_step,),
            in_specs=[
                pl.BlockSpec((per_step, block_rows, span), lambda s, c: (s, 0, 0)),
                pl.BlockSpec((per_step * block_rows, feature), lambda s, c: (s, 0)),
            ],
            out_specs=pl.BlockSpec((targets * block_rows, feature), lambda s, c: (0, 0)),
        ),
        compiler_params=pltpu.CompilerParams(dimension_semantics=("arbitrary",)),
        cost_estimate=pl.CostEstimate(
            flops=2 * block_count * block_rows * span * feature,
            transcendentals=0,
            bytes_accessed=blocks.size * 2 + row_grads.size * 2 + targets * block_rows * feature * 4,
        ),
    )(columns.reshape(-1), blocks, row_grads.astype(jnp.bfloat16))


def _exchange_kernel(*refs, axis, n, broadcast, count):
    x_refs, o_refs = refs[:count], refs[count : 2 * count]
    send_sem, recv_sem = refs[2 * count :]
    me = lax.axis_index(axis)
    barrier = pltpu.get_barrier_semaphore()

    def greet(d, carry):
        pl.semaphore_signal(
            barrier, inc=1, device_id={axis: lax.rem(me + d, n)}, device_id_type=pl.DeviceIdType.MESH
        )
        return carry

    lax.fori_loop(1, n, greet, 0)
    pl.semaphore_wait(barrier, n - 1)

    def copy_to(d, t):
        peer = lax.rem(me + d, n)
        return pltpu.make_async_remote_copy(
            src_ref=x_refs[t] if broadcast else x_refs[t].at[peer],
            dst_ref=o_refs[t].at[me],
            send_sem=send_sem.at[t, d],
            recv_sem=recv_sem.at[t, d],
            device_id={axis: peer},
            device_id_type=pl.DeviceIdType.MESH,
        )

    def start(d, carry):
        for t in range(count):
            copy_to(d, t).start()
        return carry

    def finish(d, carry):
        for t in range(count):
            copy_to(d, t).wait()
        return carry

    lax.fori_loop(1, n, start, 0)
    for t in range(count):
        o_refs[t][me] = x_refs[t][...] if broadcast else x_refs[t][me]
    lax.fori_loop(1, n, finish, 0)


def grp_exchange(chunks, site, broadcast=False):
    n = lax.axis_size("grp")
    arrays = tuple(chunks) if isinstance(chunks, (tuple, list)) else (chunks,)
    shapes = [(n,) + c.shape if broadcast else c.shape for c in arrays]
    kernel = functools.partial(
        _exchange_kernel, axis="grp", n=n, broadcast=broadcast, count=len(arrays)
    )
    moved = sum(c.size * c.dtype.itemsize for c in arrays) * (n - 1 if broadcast else 1)
    out = pl.pallas_call(
        kernel,
        out_shape=tuple(jax.ShapeDtypeStruct(s, c.dtype) for s, c in zip(shapes, arrays)),
        in_specs=[pl.BlockSpec(memory_space=pltpu.VMEM)] * len(arrays),
        out_specs=tuple(pl.BlockSpec(memory_space=pltpu.VMEM) for _ in arrays),
        scratch_shapes=[
            pltpu.SemaphoreType.DMA((len(arrays), n)),
            pltpu.SemaphoreType.DMA((len(arrays), n)),
        ],
        compiler_params=pltpu.CompilerParams(collective_id=site, has_side_effects=True),
        cost_estimate=pl.CostEstimate(flops=0, transcendentals=0, bytes_accessed=2 * moved),
    )(*arrays)
    return out if isinstance(chunks, (tuple, list)) else out[0]


def grp_gather(rows, site):
    return grp_exchange(rows, site, broadcast=True).reshape(-1, rows.shape[1])


def grp_sum_scatter(values, site):
    groups = lax.axis_size("grp")
    pieces = values.astype(jnp.bfloat16).reshape(groups, -1, values.shape[1])
    got = grp_exchange(pieces, site)
    return jnp.sum(got.astype(jnp.float32), axis=0)


def all_sum(parts):
    axes = ("slab", "grp")
    devices = lax.axis_size("slab") * lax.axis_size("grp")
    flat = jnp.concatenate([p.reshape(-1) for p in parts])
    total = flat.shape[0]
    chunk = -(-total // devices)
    chunk = -(-chunk // 128) * 128
    flat = jnp.pad(flat, (0, devices * chunk - total)).reshape(devices, chunk)
    got = lax.all_to_all(flat, axes, 0, 0, tiled=True)
    mine = jnp.sum(got, axis=0, keepdims=True)
    back = lax.all_to_all(jnp.broadcast_to(mine, (devices, chunk)), axes, 0, 0, tiled=True)
    back = back.reshape(-1)[:total]
    out, at = [], 0
    for p in parts:
        out.append(back[at : at + p.size].reshape(p.shape))
        at += p.size
    return out


def restrict(blocks, columns, source, live_mask):
    pooled = block_apply(blocks, columns, source)
    return jnp.where(live_mask[:, None], pooled, jnp.zeros_like(pooled))


def layer_forward(node_rows, message, weight_in, weight_out, bias_row):
    joined = jnp.concatenate([node_rows, message], axis=1)
    pre_act = jnp.dot(joined, weight_in, preferred_element_type=jnp.float32) + bias_row
    hidden = jax.nn.silu(pre_act).astype(jnp.bfloat16)
    result = node_rows.astype(jnp.float32) + jnp.dot(
        hidden, weight_out, preferred_element_type=jnp.float32
    )
    return (result.astype(jnp.bfloat16), pre_act, hidden)


def layer_backward(
    cotan_rows, node_rows, message, hidden, pre_act, weight_in, weight_out, blocks, columns, targets
):
    grad_low = cotan_rows.astype(jnp.bfloat16)
    delta_out = lax.dot_general(
        hidden, grad_low, (((0,), (0,)), ((), ())), preferred_element_type=jnp.float32
    )
    grad_hidden = lax.dot_general(
        grad_low, weight_out, (((1,), (1,)), ((), ())), preferred_element_type=jnp.float32
    )
    sigmoid_pre = jax.nn.sigmoid(pre_act)
    grad_pre = grad_hidden * sigmoid_pre * (1.0 + pre_act * (1.0 - sigmoid_pre))
    grad_pre_low = grad_pre.astype(jnp.bfloat16)
    delta_bias = jnp.sum(grad_pre, axis=0)
    delta_in = jnp.concatenate(
        [
            lax.dot_general(
                part, grad_pre_low, (((0,), (0,)), ((), ())), preferred_element_type=jnp.float32
            )
            for part in (node_rows, message)
        ],
        axis=0,
    )
    grad_joined = lax.dot_general(
        grad_pre_low, weight_in, (((1,), (1,)), ((), ())), preferred_element_type=jnp.float32
    )
    feature = node_rows.shape[1]
    grad_rows = cotan_rows + grad_joined[:, :feature]
    grad_message = grad_joined[:, feature:].astype(jnp.bfloat16)
    grad_context = block_transpose(blocks, columns, grad_message, targets)
    return ((delta_in, delta_out, delta_bias), grad_rows, grad_context)


def pack_layout(owners, live_mask, groups, balance):
    slot_count = owners.shape[0]
    capacity = slot_count // groups
    target = owners // balance
    onehot = (
        (target[:, None] == jnp.arange(groups, dtype=jnp.int32)[None, :]) & live_mask[:, None]
    ).astype(jnp.int32)
    slot_ranks = jnp.sum(onehot * jnp.cumsum(onehot, axis=0), axis=1) - 1
    place_at = jnp.where(live_mask, target * capacity + slot_ranks, groups * capacity)
    row_table = (
        jnp.full((groups * capacity,), balance, jnp.int32)
        .at[place_at]
        .set(owners % balance, mode="drop")
    )
    return (place_at, row_table.reshape(groups, capacity))


def pack_values(values, place_at, groups):
    capacity = values.shape[0] // groups
    buffer = (
        jnp.zeros((groups * capacity, values.shape[1]), values.dtype)
        .at[place_at]
        .set(values, mode="drop")
    )
    return buffer.reshape(groups, capacity, values.shape[1])


def place_rows(received, row_table, balance):
    feature = received.shape[-1]
    flat = received.reshape(-1, feature)
    return (
        jnp.zeros((balance, feature), received.dtype)
        .at[row_table.reshape(-1)]
        .set(flat, mode="drop")
    )


def pick_rows(table, row_table):
    balance = table.shape[0]
    flat = row_table.reshape(-1)
    taken = jnp.take(table, jnp.clip(flat, 0, balance - 1), axis=0)
    taken = jnp.where((flat < balance)[:, None], taken, jnp.zeros_like(taken))
    return taken.reshape(row_table.shape[0], row_table.shape[1], table.shape[1])


def unpack_rows(received, place_at, live_mask):
    feature = received.shape[-1]
    flat = received.reshape(-1, feature)
    taken = jnp.take(flat, jnp.clip(place_at, 0, flat.shape[0] - 1), axis=0)
    return jnp.where(live_mask[:, None], taken, jnp.zeros_like(taken))


def body(
    node_feats,
    cotangent,
    fine_adjacency,
    fine_columns,
    pool_one,
    pool_one_columns,
    count_one,
    owner_one,
    adjacency_one,
    columns_one,
    pool_two,
    pool_two_columns,
    count_two,
    owner_two,
    adjacency_two,
    columns_two,
    weight_in,
    weight_out,
    biases,
):
    groups = lax.axis_size("grp")
    block_rows = fine_adjacency.shape[1]
    fine_rows, feature = node_feats.shape
    slots_one = owner_one.shape[0]
    balance_one = slots_one // 2
    slots_two = owner_two.shape[0]
    balance_two = slots_two // 2
    live_one = jnp.arange(slots_one) < count_one[0]
    live_two = jnp.arange(slots_two) < count_two[0]
    place_one, sent_one = pack_layout(owner_one, live_one, groups, balance_one)
    place_two, sent_two = pack_layout(owner_two, live_two, groups, balance_two)

    before, after = halo_parts(node_feats, "grp", HALO)
    message0 = block_apply(fine_adjacency, fine_columns, (before, node_feats, after))
    result0, pre_act0, hidden0 = layer_forward(
        node_feats, message0, weight_in[0], weight_out[0], biases[0]
    )
    pooled_one = restrict(
        pool_one, pool_one_columns, jnp.concatenate([result0, cotangent], axis=1), live_one
    )
    table_width = sent_one.shape[1] + sent_two.shape[1]
    lanes = -(-table_width // 128) * 128
    tables = jnp.pad(jnp.concatenate([sent_one, sent_two], axis=1), ((0, 0), (0, lanes - table_width)))
    got_one, got_tables = grp_exchange(
        (
            pack_values(pooled_one, place_one, groups),
            jnp.broadcast_to(tables[:, None, :], (groups, 8, lanes)),
        ),
        0,
    )
    rows_one = got_tables[:, 0, : sent_one.shape[1]]
    rows_two = got_tables[:, 0, sent_one.shape[1] : table_width]
    placed_one = place_rows(got_one, rows_one, balance_one)
    own_one, grad_up_one = placed_one[:, :feature], placed_one[:, feature:]
    context_one = lax.all_to_all(
        jnp.broadcast_to(own_one[None], (groups,) + own_one.shape), "grp", 0, 0, tiled=True
    ).reshape(-1, feature)
    message_one = block_apply(adjacency_one, columns_one, context_one)
    result1, pre_act1, hidden1 = layer_forward(
        own_one, message_one, weight_in[1], weight_out[1], biases[1]
    )
    pooled_two = restrict(
        pool_two, pool_two_columns, jnp.concatenate([result1, grad_up_one], axis=1), live_two
    )
    got_two = grp_exchange(pack_values(pooled_two, place_two, groups), 2)
    placed_two = place_rows(got_two, rows_two, balance_two)
    own_two, grad_out_two = placed_two[:, :feature], placed_two[:, feature:]
    context_two = grp_gather(own_two, 3)
    message_two = block_apply(adjacency_two, columns_two, context_two)
    result2, pre_act2, hidden2 = layer_forward(
        own_two, message_two, weight_in[2], weight_out[2], biases[2]
    )
    sums_two, grad_rows_two, grad_ctx_two = layer_backward(
        grad_out_two.astype(jnp.float32),
        own_two,
        message_two,
        hidden2,
        pre_act2,
        weight_in[2],
        weight_out[2],
        adjacency_two,
        columns_two,
        groups * balance_two // block_rows,
    )
    grad_own_two = grad_rows_two + grp_sum_scatter(grad_ctx_two, 4)
    returned_two = grp_exchange(
        pick_rows(jnp.concatenate([result2, grad_own_two.astype(jnp.bfloat16)], axis=1), rows_two), 5
    )
    back_two = unpack_rows(returned_two, place_two, live_two)
    lifted_one = block_transpose(pool_two, pool_two_columns, back_two, balance_one // block_rows)
    up_one = (result1.astype(jnp.float32) + lifted_one[:, :feature]).astype(jnp.bfloat16)
    grad_out_one = grad_up_one.astype(jnp.float32) + lifted_one[:, feature:]
    sums_one, grad_rows_one, grad_ctx_one = layer_backward(
        grad_out_one,
        own_one,
        message_one,
        hidden1,
        pre_act1,
        weight_in[1],
        weight_out[1],
        adjacency_one,
        columns_one,
        groups * balance_one // block_rows,
    )
    grad_own_one = grad_rows_one + grp_sum_scatter(grad_ctx_one, 6)
    returned_one = grp_exchange(
        pick_rows(jnp.concatenate([up_one, grad_own_one.astype(jnp.bfloat16)], axis=1), rows_one), 7
    )
    back_one = unpack_rows(returned_one, place_one, live_one)
    lifted_zero = block_transpose(pool_one, pool_one_columns, back_one, fine_rows // block_rows)
    node_out = (result0.astype(jnp.float32) + lifted_zero[:, :feature]).astype(jnp.bfloat16)
    grad_out_zero = cotangent.astype(jnp.float32) + lifted_zero[:, feature:]
    sums_zero, grad_rows_zero, grad_ctx_zero = layer_backward(
        grad_out_zero,
        node_feats,
        message0,
        hidden0,
        pre_act0,
        weight_in[0],
        weight_out[0],
        fine_adjacency,
        fine_columns,
        (fine_rows + 2 * HALO) // block_rows,
    )
    rim_terms = jnp.concatenate([grad_ctx_zero[:HALO], grad_ctx_zero[HALO + fine_rows :]], axis=0)
    neighbour_terms = with_halo(rim_terms.astype(jnp.bfloat16), (("grp", 0),), HALO).astype(
        rim_terms.dtype
    )
    gathered_total = grad_rows_zero + grad_ctx_zero[HALO : HALO + fine_rows]
    gathered_total = gathered_total.at[:HALO].add(neighbour_terms[:HALO])
    gathered_total = gathered_total.at[fine_rows - HALO :].add(neighbour_terms[3 * HALO :])
    grad_feats = gathered_total.astype(jnp.bfloat16)
    stack_in = jnp.stack([sums_zero[0], sums_one[0], sums_two[0]])
    stack_out = jnp.stack([sums_zero[1], sums_one[1], sums_two[1]])
    stack_bias = jnp.stack([sums_zero[2], sums_one[2], sums_two[2]])
    stack_in, stack_out, stack_bias = all_sum((stack_in, stack_out, stack_bias))
    inv_root = 1.0 / math.sqrt(fine_rows * groups * lax.axis_size("slab"))
    return (node_out, grad_feats, stack_in * inv_root, stack_out * inv_root, stack_bias * inv_root)


def solution(mesh):
    placed = (
        P(("slab", "grp"), None),
        P(("slab", "grp"), None),
        P(("slab", "grp"), None, None),
        P(("slab", "grp"), None),
        P(("slab", "grp"), None, None),
        P(("slab", "grp"), None),
        P(("slab", "grp")),
        P(("slab", "grp")),
        P(("slab", "grp"), None, None),
        P(("slab", "grp"), None),
        P(("slab", "grp"), None, None),
        P(("slab", "grp"), None),
        P(("slab", "grp")),
        P(("slab", "grp")),
        P(("slab", "grp"), None, None),
        P(("slab", "grp"), None),
        P(),
        P(),
        P(),
    )
    return jax.shard_map(
        body,
        mesh=mesh,
        in_specs=placed,
        out_specs=(P(("slab", "grp"), None), P(("slab", "grp"), None), P(), P(), P()),
        check_vma=False,
    )
```

```python
import functools
import math

import jax
import jax.numpy as jnp
from jax import lax
from jax.experimental import pallas as pl
from jax.experimental.pallas import tpu as pltpu
from jax.sharding import PartitionSpec as P

HALO = 512


def with_halo(cells, sides, width):
    for axis, dim in sides:
        count = lax.axis_size(axis)
        ends = count - 1
        head = lax.slice_in_dim(cells, 0, width, axis=dim)
        tail = lax.slice_in_dim(cells, cells.shape[dim] - width, cells.shape[dim], axis=dim)
        cells = jnp.concatenate(
            [
                lax.ppermute(tail, axis, [(i, (i + 1) % count) for i in range(ends)]),
                cells,
                lax.ppermute(head, axis, [((i + 1) % count, i) for i in range(ends)]),
            ],
            axis=dim,
        )
    return cells


def halo_parts(cells, axis, width):
    count = lax.axis_size(axis)
    ends = count - 1
    head = cells[:width]
    tail = cells[cells.shape[0] - width :]
    before = lax.ppermute(tail, axis, [(i, (i + 1) % count) for i in range(ends)])
    after = lax.ppermute(head, axis, [((i + 1) % count, i) for i in range(ends)])
    return before, after


def _per_step(block_count):
    return min(block_count, 8)


def _apply_kernel(cols_ref, m_ref, *refs, k, per_step, blk, pieces_in):
    q_parts, (o_ref, q_ref) = refs[:pieces_in], refs[pieces_in:]
    step = pl.program_id(0)

    @pl.when(step == 0)
    def _():
        at = 0
        for part in q_parts:
            q_ref[at : at + part.shape[0], :] = part[...]
            at += part.shape[0]

    for j in range(per_step):
        r = step * per_step + j
        pieces = [
            q_ref[pl.ds(pl.multiple_of(cols_ref[r * k + i] * blk, blk), blk), :] for i in range(k)
        ]
        stacked = jnp.concatenate(pieces, axis=0)
        res = jnp.dot(m_ref[j], stacked, preferred_element_type=jnp.float32)
        o_ref[j * blk : (j + 1) * blk, :] = res.astype(o_ref.dtype)


def block_apply(blocks, columns, context, out_dtype=jnp.bfloat16):
    block_count, block_rows, span = blocks.shape
    k = columns.shape[1]
    parts = tuple(context) if isinstance(context, (tuple, list)) else (context,)
    feature = parts[0].shape[1]
    rows = sum(p.shape[0] for p in parts)
    per_step = _per_step(block_count)
    kernel = functools.partial(
        _apply_kernel, k=k, per_step=per_step, blk=block_rows, pieces_in=len(parts)
    )
    return pl.pallas_call(
        kernel,
        out_shape=jax.ShapeDtypeStruct((block_count * block_rows, feature), out_dtype),
        grid_spec=pltpu.PrefetchScalarGridSpec(
            num_scalar_prefetch=1,
            grid=(block_count // per_step,),
            in_specs=[pl.BlockSpec((per_step, block_rows, span), lambda s, c: (s, 0, 0))]
            + [pl.BlockSpec(p.shape, lambda s, c: (0, 0)) for p in parts],
            out_specs=pl.BlockSpec((per_step * block_rows, feature), lambda s, c: (s, 0)),
            scratch_shapes=[pltpu.VMEM((rows, feature), parts[0].dtype)],
        ),
        compiler_params=pltpu.CompilerParams(dimension_semantics=("arbitrary",)),
        cost_estimate=pl.CostEstimate(
            flops=2 * block_count * block_rows * span * feature,
            transcendentals=0,
            bytes_accessed=blocks.size * 2 + rows * feature * 2 + block_count * block_rows * feature * 2,
        ),
    )(columns.reshape(-1), blocks, *parts)


def _apply_t_kernel(cols_ref, m_ref, p_ref, o_ref, *, k, per_step, blk):
    step = pl.program_id(0)

    @pl.when(step == 0)
    def _():
        o_ref[...] = jnp.zeros_like(o_ref)

    for j in range(per_step):
        r = step * per_step + j
        spread = lax.dot_general(
            m_ref[j],
            p_ref[j * blk : (j + 1) * blk, :],
            (((0,), (0,)), ((), ())),
            preferred_element_type=jnp.float32,
        )
        for i in range(k):
            at = pl.multiple_of(cols_ref[r * k + i] * blk, blk)
            o_ref[pl.ds(at, blk), :] += spread[i * blk : (i + 1) * blk]


def block_transpose(blocks, columns, row_grads, targets):
    block_count, block_rows, span = blocks.shape
    k = columns.shape[1]
    feature = row_grads.shape[1]
    per_step = _per_step(block_count)
    kernel = functools.partial(_apply_t_kernel, k=k, per_step=per_step, blk=block_rows)
    return pl.pallas_call(
        kernel,
        out_shape=jax.ShapeDtypeStruct((targets * block_rows, feature), jnp.float32),
        grid_spec=pltpu.PrefetchScalarGridSpec(
            num_scalar_prefetch=1,
            grid=(block_count // per_step,),
            in_specs=[
                pl.BlockSpec((per_step, block_rows, span), lambda s, c: (s, 0, 0)),
                pl.BlockSpec((per_step * block_rows, feature), lambda s, c: (s, 0)),
            ],
            out_specs=pl.BlockSpec((targets * block_rows, feature), lambda s, c: (0, 0)),
        ),
        compiler_params=pltpu.CompilerParams(dimension_semantics=("arbitrary",)),
        cost_estimate=pl.CostEstimate(
            flops=2 * block_count * block_rows * span * feature,
            transcendentals=0,
            bytes_accessed=blocks.size * 2 + row_grads.size * 2 + targets * block_rows * feature * 4,
        ),
    )(columns.reshape(-1), blocks, row_grads.astype(jnp.bfloat16))


def _exchange_kernel(*refs, axis, n, broadcast, count):
    x_refs, o_refs = refs[:count], refs[count : 2 * count]
    send_sem, recv_sem = refs[2 * count :]
    me = lax.axis_index(axis)
    barrier = pltpu.get_barrier_semaphore()

    def greet(d, carry):
        pl.semaphore_signal(
            barrier, inc=1, device_id={axis: lax.rem(me + d, n)}, device_id_type=pl.DeviceIdType.MESH
        )
        return carry

    lax.fori_loop(1, n, greet, 0)
    pl.semaphore_wait(barrier, n - 1)

    def copy_to(d, t):
        peer = lax.rem(me + d, n)
        return pltpu.make_async_remote_copy(
            src_ref=x_refs[t] if broadcast else x_refs[t].at[peer],
            dst_ref=o_refs[t].at[me],
            send_sem=send_sem.at[t, d],
            recv_sem=recv_sem.at[t, d],
            device_id={axis: peer},
            device_id_type=pl.DeviceIdType.MESH,
        )

    def start(d, carry):
        for t in range(count):
            copy_to(d, t).start()
        return carry

    def finish(d, carry):
        for t in range(count):
            copy_to(d, t).wait()
        return carry

    lax.fori_loop(1, n, start, 0)
    for t in range(count):
        o_refs[t][me] = x_refs[t][...] if broadcast else x_refs[t][me]
    lax.fori_loop(1, n, finish, 0)


def grp_exchange(chunks, site, broadcast=False):
    n = lax.axis_size("grp")
    arrays = tuple(chunks) if isinstance(chunks, (tuple, list)) else (chunks,)
    shapes = [(n,) + c.shape if broadcast else c.shape for c in arrays]
    kernel = functools.partial(
        _exchange_kernel, axis="grp", n=n, broadcast=broadcast, count=len(arrays)
    )
    moved = sum(c.size * c.dtype.itemsize for c in arrays) * (n - 1 if broadcast else 1)
    out = pl.pallas_call(
        kernel,
        out_shape=tuple(jax.ShapeDtypeStruct(s, c.dtype) for s, c in zip(shapes, arrays)),
        in_specs=[pl.BlockSpec(memory_space=pltpu.VMEM)] * len(arrays),
        out_specs=tuple(pl.BlockSpec(memory_space=pltpu.VMEM) for _ in arrays),
        scratch_shapes=[
            pltpu.SemaphoreType.DMA((len(arrays), n)),
            pltpu.SemaphoreType.DMA((len(arrays), n)),
        ],
        compiler_params=pltpu.CompilerParams(collective_id=site, has_side_effects=True),
        cost_estimate=pl.CostEstimate(flops=0, transcendentals=0, bytes_accessed=2 * moved),
    )(*arrays)
    return out if isinstance(chunks, (tuple, list)) else out[0]


def grp_gather(rows, site):
    return grp_exchange(rows, site, broadcast=True).reshape(-1, rows.shape[1])


def grp_sum_scatter(values, site):
    groups = lax.axis_size("grp")
    pieces = values.astype(jnp.bfloat16).reshape(groups, -1, values.shape[1])
    got = grp_exchange(pieces, site)
    return jnp.sum(got.astype(jnp.float32), axis=0)


def all_sum(parts):
    axes = ("slab", "grp")
    devices = lax.axis_size("slab") * lax.axis_size("grp")
    flat = jnp.concatenate([p.reshape(-1) for p in parts])
    total = flat.shape[0]
    chunk = -(-total // devices)
    chunk = -(-chunk // 128) * 128
    flat = jnp.pad(flat, (0, devices * chunk - total)).reshape(devices, chunk)
    got = lax.all_to_all(flat, axes, 0, 0, tiled=True)
    mine = jnp.sum(got, axis=0, keepdims=True)
    back = lax.all_to_all(jnp.broadcast_to(mine, (devices, chunk)), axes, 0, 0, tiled=True)
    back = back.reshape(-1)[:total]
    out, at = [], 0
    for p in parts:
        out.append(back[at : at + p.size].reshape(p.shape))
        at += p.size
    return out


def restrict(blocks, columns, source, live_mask):
    pooled = block_apply(blocks, columns, source)
    return jnp.where(live_mask[:, None], pooled, jnp.zeros_like(pooled))


def layer_forward(node_rows, message, weight_in, weight_out, bias_row):
    joined = jnp.concatenate([node_rows, message], axis=1)
    pre_act = jnp.dot(joined, weight_in, preferred_element_type=jnp.float32) + bias_row
    hidden = jax.nn.silu(pre_act).astype(jnp.bfloat16)
    result = node_rows.astype(jnp.float32) + jnp.dot(
        hidden, weight_out, preferred_element_type=jnp.float32
    )
    return (result.astype(jnp.bfloat16), pre_act, hidden)


def layer_backward(
    cotan_rows, node_rows, message, hidden, pre_act, weight_in, weight_out, blocks, columns, targets
):
    grad_low = cotan_rows.astype(jnp.bfloat16)
    delta_out = lax.dot_general(
        hidden, grad_low, (((0,), (0,)), ((), ())), preferred_element_type=jnp.float32
    )
    grad_hidden = lax.dot_general(
        grad_low, weight_out, (((1,), (1,)), ((), ())), preferred_element_type=jnp.float32
    )
    sigmoid_pre = jax.nn.sigmoid(pre_act)
    grad_pre = grad_hidden * sigmoid_pre * (1.0 + pre_act * (1.0 - sigmoid_pre))
    grad_pre_low = grad_pre.astype(jnp.bfloat16)
    delta_bias = jnp.sum(grad_pre, axis=0)
    joined = jnp.concatenate([node_rows, message], axis=1)
    delta_in = lax.dot_general(
        joined, grad_pre_low, (((0,), (0,)), ((), ())), preferred_element_type=jnp.float32
    )
    grad_joined = lax.dot_general(
        grad_pre_low, weight_in, (((1,), (1,)), ((), ())), preferred_element_type=jnp.float32
    )
    feature = node_rows.shape[1]
    grad_rows = cotan_rows + grad_joined[:, :feature]
    grad_message = grad_joined[:, feature:].astype(jnp.bfloat16)
    grad_context = block_transpose(blocks, columns, grad_message, targets)
    return ((delta_in, delta_out, delta_bias), grad_rows, grad_context)


def pack_layout(owners, live_mask, groups, balance):
    slot_count = owners.shape[0]
    capacity = slot_count // groups
    target = owners // balance
    onehot = (
        (target[:, None] == jnp.arange(groups, dtype=jnp.int32)[None, :]) & live_mask[:, None]
    ).astype(jnp.int32)
    slot_ranks = jnp.sum(onehot * jnp.cumsum(onehot, axis=0), axis=1) - 1
    place_at = jnp.where(live_mask, target * capacity + slot_ranks, groups * capacity)
    row_table = (
        jnp.full((groups * capacity,), balance, jnp.int32)
        .at[place_at]
        .set(owners % balance, mode="drop")
    )
    return (place_at, row_table.reshape(groups, capacity))


def pack_values(values, place_at, groups):
    capacity = values.shape[0] // groups
    buffer = (
        jnp.zeros((groups * capacity, values.shape[1]), values.dtype)
        .at[place_at]
        .set(values, mode="drop")
    )
    return buffer.reshape(groups, capacity, values.shape[1])


def place_rows(received, row_table, balance):
    feature = received.shape[-1]
    flat = received.reshape(-1, feature)
    return (
        jnp.zeros((balance, feature), received.dtype)
        .at[row_table.reshape(-1)]
        .set(flat, mode="drop")
    )


def pick_rows(table, row_table):
    balance = table.shape[0]
    flat = row_table.reshape(-1)
    taken = jnp.take(table, jnp.clip(flat, 0, balance - 1), axis=0)
    taken = jnp.where((flat < balance)[:, None], taken, jnp.zeros_like(taken))
    return taken.reshape(row_table.shape[0], row_table.shape[1], table.shape[1])


def unpack_rows(received, place_at, live_mask):
    feature = received.shape[-1]
    flat = received.reshape(-1, feature)
    taken = jnp.take(flat, jnp.clip(place_at, 0, flat.shape[0] - 1), axis=0)
    return jnp.where(live_mask[:, None], taken, jnp.zeros_like(taken))


def body(
    node_feats,
    cotangent,
    fine_adjacency,
    fine_columns,
    pool_one,
    pool_one_columns,
    count_one,
    owner_one,
    adjacency_one,
    columns_one,
    pool_two,
    pool_two_columns,
    count_two,
    owner_two,
    adjacency_two,
    columns_two,
    weight_in,
    weight_out,
    biases,
):
    groups = lax.axis_size("grp")
    block_rows = fine_adjacency.shape[1]
    fine_rows, feature = node_feats.shape
    slots_one = owner_one.shape[0]
    balance_one = slots_one // 2
    slots_two = owner_two.shape[0]
    balance_two = slots_two // 2
    live_one = jnp.arange(slots_one) < count_one[0]
    live_two = jnp.arange(slots_two) < count_two[0]
    place_one, sent_one = pack_layout(owner_one, live_one, groups, balance_one)
    place_two, sent_two = pack_layout(owner_two, live_two, groups, balance_two)

    before, after = halo_parts(node_feats, "grp", HALO)
    message0 = block_apply(fine_adjacency, fine_columns, (before, node_feats, after))
    result0, pre_act0, hidden0 = layer_forward(
        node_feats, message0, weight_in[0], weight_out[0], biases[0]
    )
    pooled_one = restrict(
        pool_one, pool_one_columns, jnp.concatenate([result0, cotangent], axis=1), live_one
    )
    table_width = sent_one.shape[1] + sent_two.shape[1]
    lanes = -(-table_width // 128) * 128
    tables = jnp.pad(jnp.concatenate([sent_one, sent_two], axis=1), ((0, 0), (0, lanes - table_width)))
    got_one, got_tables = grp_exchange(
        (
            pack_values(pooled_one, place_one, groups),
            jnp.broadcast_to(tables[:, None, :], (groups, 8, lanes)),
        ),
        0,
    )
    rows_one = got_tables[:, 0, : sent_one.shape[1]]
    rows_two = got_tables[:, 0, sent_one.shape[1] : table_width]
    placed_one = place_rows(got_one, rows_one, balance_one)
    own_one, grad_up_one = placed_one[:, :feature], placed_one[:, feature:]
    context_one = lax.all_to_all(
        jnp.broadcast_to(own_one[None], (groups,) + own_one.shape), "grp", 0, 0, tiled=True
    ).reshape(-1, feature)
    message_one = block_apply(adjacency_one, columns_one, context_one)
    result1, pre_act1, hidden1 = layer_forward(
        own_one, message_one, weight_in[1], weight_out[1], biases[1]
    )
    pooled_two = restrict(
        pool_two, pool_two_columns, jnp.concatenate([result1, grad_up_one], axis=1), live_two
    )
    got_two = grp_exchange(pack_values(pooled_two, place_two, groups), 2)
    placed_two = place_rows(got_two, rows_two, balance_two)
    own_two, grad_out_two = placed_two[:, :feature], placed_two[:, feature:]
    context_two = grp_gather(own_two, 3)
    message_two = block_apply(adjacency_two, columns_two, context_two)
    result2, pre_act2, hidden2 = layer_forward(
        own_two, message_two, weight_in[2], weight_out[2], biases[2]
    )
    sums_two, grad_rows_two, grad_ctx_two = layer_backward(
        grad_out_two.astype(jnp.float32),
        own_two,
        message_two,
        hidden2,
        pre_act2,
        weight_in[2],
        weight_out[2],
        adjacency_two,
        columns_two,
        groups * balance_two // block_rows,
    )
    grad_own_two = grad_rows_two + grp_sum_scatter(grad_ctx_two, 4)
    returned_two = grp_exchange(
        pick_rows(jnp.concatenate([result2, grad_own_two.astype(jnp.bfloat16)], axis=1), rows_two), 5
    )
    back_two = unpack_rows(returned_two, place_two, live_two)
    lifted_one = block_transpose(pool_two, pool_two_columns, back_two, balance_one // block_rows)
    up_one = (result1.astype(jnp.float32) + lifted_one[:, :feature]).astype(jnp.bfloat16)
    grad_out_one = grad_up_one.astype(jnp.float32) + lifted_one[:, feature:]
    sums_one, grad_rows_one, grad_ctx_one = layer_backward(
        grad_out_one,
        own_one,
        message_one,
        hidden1,
        pre_act1,
        weight_in[1],
        weight_out[1],
        adjacency_one,
        columns_one,
        groups * balance_one // block_rows,
    )
    grad_own_one = grad_rows_one + grp_sum_scatter(grad_ctx_one, 6)
    returned_one = grp_exchange(
        pick_rows(jnp.concatenate([up_one, grad_own_one.astype(jnp.bfloat16)], axis=1), rows_one), 7
    )
    back_one = unpack_rows(returned_one, place_one, live_one)
    lifted_zero = block_transpose(pool_one, pool_one_columns, back_one, fine_rows // block_rows)
    node_out = (result0.astype(jnp.float32) + lifted_zero[:, :feature]).astype(jnp.bfloat16)
    grad_out_zero = cotangent.astype(jnp.float32) + lifted_zero[:, feature:]
    sums_zero, grad_rows_zero, grad_ctx_zero = layer_backward(
        grad_out_zero,
        node_feats,
        message0,
        hidden0,
        pre_act0,
        weight_in[0],
        weight_out[0],
        fine_adjacency,
        fine_columns,
        (fine_rows + 2 * HALO) // block_rows,
    )
    rim_terms = jnp.concatenate([grad_ctx_zero[:HALO], grad_ctx_zero[HALO + fine_rows :]], axis=0)
    neighbour_terms = with_halo(rim_terms.astype(jnp.bfloat16), (("grp", 0),), HALO).astype(
        rim_terms.dtype
    )
    own_terms = grad_rows_zero + grad_ctx_zero[HALO : HALO + fine_rows]
    grad_feats = jnp.concatenate(
        [
            (own_terms[:HALO] + neighbour_terms[:HALO]).astype(jnp.bfloat16),
            own_terms[HALO : fine_rows - HALO].astype(jnp.bfloat16),
            (own_terms[fine_rows - HALO :] + neighbour_terms[3 * HALO :]).astype(jnp.bfloat16),
        ],
        axis=0,
    )
    stack_in = jnp.stack([sums_zero[0], sums_one[0], sums_two[0]])
    stack_out = jnp.stack([sums_zero[1], sums_one[1], sums_two[1]])
    stack_bias = jnp.stack([sums_zero[2], sums_one[2], sums_two[2]])
    stack_in, stack_out, stack_bias = all_sum((stack_in, stack_out, stack_bias))
    inv_root = 1.0 / math.sqrt(fine_rows * groups * lax.axis_size("slab"))
    return (node_out, grad_feats, stack_in * inv_root, stack_out * inv_root, stack_bias * inv_root)


def solution(mesh):
    placed = (
        P(("slab", "grp"), None),
        P(("slab", "grp"), None),
        P(("slab", "grp"), None, None),
        P(("slab", "grp"), None),
        P(("slab", "grp"), None, None),
        P(("slab", "grp"), None),
        P(("slab", "grp")),
        P(("slab", "grp")),
        P(("slab", "grp"), None, None),
        P(("slab", "grp"), None),
        P(("slab", "grp"), None, None),
        P(("slab", "grp"), None),
        P(("slab", "grp")),
        P(("slab", "grp")),
        P(("slab", "grp"), None, None),
        P(("slab", "grp"), None),
        P(),
        P(),
        P(),
    )
    return jax.shard_map(
        body,
        mesh=mesh,
        in_specs=placed,
        out_specs=(P(("slab", "grp"), None), P(("slab", "grp"), None), P(), P(), P()),
        check_vma=False,
    )
```
